32 devices in a mesh: dp: 8 (over z, y), seq: 4 (over x, core).
Axes of the slice: x: 2, y: 2, z: 4, core: 2. Of those that a mesh axis runs over, the one named last changes fastest.
Arguments:
- pixels: bfloat16 [32, 256, 768], P('dp', 'seq'), may hold values from -6 to 6
- block_mask: int32 [32, 256], P('dp', 'seq'), may hold values from 0 to 1, as said below
- targets: bfloat16 [32, 256, 768], P('dp', 'seq'), may hold values from -6 to 6
- square_weights: float32 [3, 768, 768], P(None, 'dp'), may hold values from -0.21875 to 0.21875
- joint_weights: float32 [768, 2304], P('dp'), may hold values from -0.21875 to 0.21875
- expand_weights: float32 [768, 3072], P('dp'), may hold values from -0.21875 to 0.21875
- reduce_weights: float32 [3072, 768], P('dp'), may hold values from -0.109375 to 0.109375
- vectors: float32 [20, 768], P(None, 'dp'), may hold values from -8 to 8, as said below
- square_moment: float32 [3, 768, 768], P(None, 'dp'), may hold values from -6.1035156e-05 to 6.1035156e-05
- joint_moment: float32 [768, 2304], P('dp'), may hold values from -6.1035156e-05 to 6.1035156e-05
- expand_moment: float32 [768, 3072], P('dp'), may hold values from -6.1035156e-05 to 6.1035156e-05
- reduce_moment: float32 [3072, 768], P('dp'), may hold values from -6.1035156e-05 to 6.1035156e-05
- vector_moment: float32 [20, 768], P(None, 'dp'), may hold values from -0.00018310547 to 0.00018310547
- square_variance: float32 [3, 768, 768], P(None, 'dp'), may hold values from 1.2087666e-12 to 4.8350664e-12
- joint_variance: float32 [768, 2304], P('dp'), may hold values from 1.2087666e-12 to 4.8350664e-12
- expand_variance: float32 [768, 3072], P('dp'), may hold values from 1.2087666e-12 to 4.8350664e-12
- reduce_variance: float32 [3072, 768], P('dp'), may hold values from 1.2087666e-12 to 4.8350664e-12
- vector_variance: float32 [20, 768], P(None, 'dp'), may hold values from 1.0878899e-11 to 4.3515597e-11
Outputs:
- masked_loss: float32 [], replicated
- gradient_norm: float32 [], replicated
- moment_square: float32 [3, 768, 768], P(None, 'dp')
- variance_square: float32 [3, 768, 768], P(None, 'dp')
- master_square: float32 [3, 768, 768], P(None, 'dp')
- moment_joint: float32 [768, 2304], P('dp')
- variance_joint: float32 [768, 2304], P('dp')
- master_joint: float32 [768, 2304], P('dp')
- moment_expand: float32 [768, 3072], P('dp')
- variance_expand: float32 [768, 3072], P('dp')
- master_expand: float32 [768, 3072], P('dp')
- moment_reduce: float32 [3072, 768], P('dp')
- variance_reduce: float32 [3072, 768], P('dp')
- master_reduce: float32 [3072, 768], P('dp')
- moment_vector: float32 [20, 768], P(None, 'dp')
- variance_vector: float32 [20, 768], P(None, 'dp')
- master_vector: float32 [20, 768], P(None, 'dp')
The draws below stay inside these ranges and needn't reach their ends.
Inputs may be any that keep to these rules, and one draw needn't show every extreme that they name: `block_mask`: 1 marks a masked patch; patches are masked in whole 2 x 2 blocks of the 14 x 14 grid; the class and padding slots are 0. `vectors`: gains and layer scales are positive.
All inputs are finite; a program needn't handle non-finite values.
Results may differ from the reference program's by a relative error of at most 0.011.
Values may be sent and summed in bfloat16 or wider, within the bound.
No kernel may reach another device: no remote copies, remote signals or barrier semaphores. Data moves between devices by JAX's collectives and lax.ppermute only.
A program may use at most 128 MiB of HBM per device.

```python
import math
import jax
import jax.numpy as jnp
from jax import lax

D = 768
HEADS = 12
HEAD_DIM = 64
FF = 3072
PIX = 768
GRID = 14
SLOTS = 256
VEC = 20
MICRO = 2
IMG_MB = 2
IMAGES = 32
NPARAM = 8272896


def noise_field(key, shape):
    return jax.random.normal(key, shape, jnp.float32)


def draw_vectors(key, part):
    keys = jax.random.split(key, 2)
    base = noise_field(keys[0], (VEC, D))
    spread = jax.random.uniform(keys[1], (VEC, D), jnp.float32, -1.0, 1.0)
    row = jnp.arange(VEC)[:, None]
    result = 0.2 * base
    result = jnp.where(row < 2, base, result)
    is_gain = (row == 3) | (row == 9) | (row == 13)
    result = jnp.where(is_gain, 1.0 + 0.4 * spread, result)
    result = jnp.where(row == 8, 4.5 + 1.5 * spread, result)
    result = jnp.where(row == 12, 1.5 + 0.5 * spread, result)
    return result


def draw_block_mask(key, part):
    side = GRID // 2
    keys = jax.random.split(key, 2)
    ranks = jax.vmap(lambda one: jax.random.permutation(one, side * side))(jax.random.split(keys[0], IMAGES))
    image = jnp.arange(IMAGES)
    quota = 10 + 32 * image // IMAGES + jax.random.randint(keys[1], (IMAGES,), 0, 6)
    chosen = ranks < quota[:, None]
    slot = jnp.arange(SLOTS)
    inside = slot < GRID * GRID
    block = jnp.where(inside, slot // GRID // 2 * side + slot % GRID // 2, 0)
    picked = jnp.take(chosen, block, axis=1)
    return jnp.where(inside[None, :], picked, False).astype(jnp.int32)


def levels(own_key, shape, cuts, low, largest):
    factor_of = 1.0
    for dim, blocks in cuts:
        draws = jax.random.uniform(jax.random.fold_in(jax.random.fold_in(own_key, 6), dim), (blocks,), jnp.float32, low / len(cuts), largest / len(cuts))
        factor_of = factor_of * jnp.repeat(jnp.exp(draws), shape[dim] // blocks).reshape((-1,) + (1,) * (len(shape) - 1 - dim))
    return factor_of


def normal_values(own_key, shape, scale, reach, pieces=(), held_as=jnp.bfloat16):
    drawn = scale * jax.random.normal(own_key, shape, jnp.float32)
    if pieces:
        drawn = drawn * levels(own_key, shape, pieces, -0.22, 0.18)
    return jnp.clip(drawn, -reach, reach).astype(held_as)


def setup_inputs(seed: int = 0) -> dict:
    streams_of = jax.random.split(jax.random.key(seed), 19)
    return {
        "pixels": normal_values(streams_of[0], (IMAGES, SLOTS, PIX), 1.0, 6.0, ((0, 8), (1, 4))),
        "block_mask": draw_block_mask(jax.random.fold_in(streams_of[18], 71), 0),
        "targets": normal_values(streams_of[2], (IMAGES, SLOTS, D), 1.0, 6.0, ((0, 8), (1, 4))),
        "square_weights": normal_values(streams_of[3], (3, D, D), D ** -0.5, 0.21875, ((1, 8),), jnp.float32),
        "joint_weights": normal_values(streams_of[4], (D, 3 * D), D ** -0.5, 0.21875, ((0, 8),), jnp.float32),
        "expand_weights": normal_values(streams_of[5], (D, FF), D ** -0.5, 0.21875, ((0, 8),), jnp.float32),
        "reduce_weights": normal_values(streams_of[6], (FF, D), FF ** -0.5, 0.109375, ((0, 8),), jnp.float32),
        "vectors": draw_vectors(jax.random.fold_in(streams_of[18], 71), 0),
        "square_moment": normal_values(streams_of[8], (3, D, D), (0.011 / NPARAM ** 0.5), 6.103515625e-05, ((1, 8),), jnp.float32),
        "joint_moment": normal_values(streams_of[9], (D, 3 * D), (0.011 / NPARAM ** 0.5), 6.103515625e-05, ((0, 8),), jnp.float32),
        "expand_moment": normal_values(streams_of[10], (D, FF), (0.011 / NPARAM ** 0.5), 6.103515625e-05, ((0, 8),), jnp.float32),
        "reduce_moment": normal_values(streams_of[11], (FF, D), (0.011 / NPARAM ** 0.5), 6.103515625e-05, ((0, 8),), jnp.float32),
        "vector_moment": normal_values(streams_of[12], (VEC, D), (0.033 / NPARAM ** 0.5), 0.00018310547, ((1, 8),), jnp.float32),
        "square_variance": jnp.clip(jnp.exp(math.log(4.835066375052932e-12) - 1.3862944 * jax.random.uniform(streams_of[13], (3, D, D), jnp.float32) ** levels(streams_of[13], (3, D, D), ((1, 8),), -0.2, 0.2)), 1.208766593763233e-12, 4.835066375052932e-12),
        "joint_variance": jnp.clip(jnp.exp(math.log(4.835066375052932e-12) - 1.3862944 * jax.random.uniform(streams_of[14], (D, 3 * D), jnp.float32) ** levels(streams_of[14], (D, 3 * D), ((0, 8),), -0.2, 0.2)), 1.208766593763233e-12, 4.835066375052932e-12),
        "expand_variance": jnp.clip(jnp.exp(math.log(4.835066375052932e-12) - 1.3862944 * jax.random.uniform(streams_of[15], (D, FF), jnp.float32) ** levels(streams_of[15], (D, FF), ((0, 8),), -0.2, 0.2)), 1.208766593763233e-12, 4.835066375052932e-12),
        "reduce_variance": jnp.clip(jnp.exp(math.log(4.835066375052932e-12) - 1.3862944 * jax.random.uniform(streams_of[16], (FF, D), jnp.float32) ** levels(streams_of[16], (FF, D), ((0, 8),), -0.2, 0.2)), 1.208766593763233e-12, 4.835066375052932e-12),
        "vector_variance": jnp.clip(jnp.exp(math.log(4.351559737547639e-11) - 1.3862944 * jax.random.uniform(streams_of[17], (VEC, D), jnp.float32) ** levels(streams_of[17], (VEC, D), ((1, 8),), -0.2, 0.2)), 1.0878899343869097e-11, 4.351559737547639e-11),
    }


@jax.custom_vjp
def low(v):
    return lax.optimization_barrier(v.astype(jnp.bfloat16)).astype(jnp.float32)

@jax.custom_vjp
def low_back(v):
    return v

def low_keep(v):
    return (low(v), None)

def low_pass(kept, grad):
    return (grad,)

def back_keep(v):
    return (v, None)

def back_low(kept, grad):
    return (low(grad),)
low.defvjp(low_keep, low_pass)
low_back.defvjp(back_keep, back_low)
norm_eps = 1e-06
beta_one = 0.9
beta_two = 0.999
adam_eps = 1e-08
adam_step = 10.0
matrix_rate = 0.05
vector_rate = 0.3
weight_decay = 0.05
clip_limit = 0.1

def positions(slot_float, features):
    column = jnp.arange(features)
    frequency = jnp.exp((2 * (column // 2)).astype(jnp.float32) * (-math.log(10000.0) / features))
    angle = slot_float[:, None] * frequency[None, :]
    return jnp.where(column % 2 == 0, jnp.sin(angle), jnp.cos(angle))

def layer_norm(stream, gain, shift):
    centred = stream - lax.optimization_barrier(jnp.mean(stream, -1, keepdims=True))
    inverse = lax.rsqrt(lax.optimization_barrier(jnp.mean(centred * centred, -1, keepdims=True)) + norm_eps)
    return centred * inverse * gain + shift

def product(left, weight):
    return low_back(jnp.matmul(low(left), weight, precision=lax.Precision.HIGHEST))

def smooth_terms(residual):
    return jnp.where(jnp.abs(residual) < 2.0, 0.25 * residual * residual, jnp.abs(residual) - 1.0)

def group_loss(weights, pixels, block_mask, targets):
    square_w, joint_w, expand_w, reduce_w, vector_w = weights
    images, slots, _ = pixels.shape
    patches = GRID * GRID
    slot_index = jnp.arange(slots)
    valid = slot_index <= patches
    is_class = (slot_index == patches)[None, :, None]
    masked = block_mask.astype(jnp.float32)[:, :, None]
    embedded = product(pixels, square_w[0]) + vector_w[2]
    stream_zero = jnp.where(is_class, vector_w[0], jnp.where(masked > 0.5, vector_w[1], embedded))
    stream_zero = stream_zero + positions(slot_index.astype(jnp.float32), D)
    joint = product(layer_norm(stream_zero, vector_w[3], vector_w[4]), joint_w)
    joint = joint + jnp.concatenate([vector_w[5], jnp.zeros((D,), jnp.float32), vector_w[6]])
    query = low(joint[..., :D]).reshape(images, slots, HEADS, HEAD_DIM)
    keys = low(joint[..., D:2 * D]).reshape(images, slots, HEADS, HEAD_DIM)
    values = low(joint[..., 2 * D:]).reshape(images, slots, HEADS, HEAD_DIM)
    scores = jnp.einsum('gqhd,gkhd->ghqk', query, keys, precision=lax.Precision.HIGHEST)
    scores = low_back(scores * HEAD_DIM ** (-0.5))
    scores = jnp.where(valid[None, None, None, :], scores, -1e+30)
    shifted = jnp.exp(scores - lax.optimization_barrier(jnp.max(scores, -1, keepdims=True)))
    probs = low(shifted / lax.optimization_barrier(jnp.sum(shifted, -1, keepdims=True)))
    attended = jnp.einsum('ghqk,gkhd->gqhd', probs, values, precision=lax.Precision.HIGHEST)
    attended = low(low_back(attended)).reshape(images, slots, D)
    stream_one = stream_zero + vector_w[8] * (product(attended, square_w[1]) + vector_w[7])
    inner = product(layer_norm(stream_one, vector_w[9], vector_w[10]), expand_w) + vector_w[16:].reshape(FF)
    activated = jax.nn.gelu(inner, approximate=False)
    stream_two = stream_one + vector_w[12] * (product(activated, reduce_w) + vector_w[11])
    predicted = product(layer_norm(stream_two, vector_w[13], vector_w[14]), square_w[2]) + vector_w[15]
    return jnp.sum(masked * smooth_terms(predicted - targets))

def total_loss(weights, pixels, block_mask, targets, count):
    lowered = tuple((low(weight) for weight in weights))
    group = IMG_MB * MICRO
    shaped = (pixels.reshape(-1, group, SLOTS, PIX), block_mask.reshape(-1, group, SLOTS), targets.reshape(-1, group, SLOTS, D))
    checked = jax.checkpoint(group_loss)

    def step_group(total, inputs):
        return (total + checked(lowered, inputs[0], inputs[1], inputs[2]), None)
    total, _ = lax.scan(step_group, jnp.zeros((), jnp.float32), shaped)
    return total / count

def adam(weight, moment, variance, grad, rate, decay):
    moment_new = beta_one * moment + (1.0 - beta_one) * grad
    variance_new = beta_two * variance + (1.0 - beta_two) * grad * grad
    corrected = moment_new / (1.0 - beta_one ** adam_step) / (jnp.sqrt(variance_new / (1.0 - beta_two ** adam_step)) + adam_eps)
    return (moment_new, variance_new, weight - rate * (corrected + decay * weight))

def reference(pixels, block_mask, targets, square_weights, joint_weights, expand_weights, reduce_weights, vectors, square_moment, joint_moment, expand_moment, reduce_moment, vector_moment, square_variance, joint_variance, expand_variance, reduce_variance, vector_variance):
    weights = (square_weights, joint_weights, expand_weights, reduce_weights, vectors)
    count = jnp.sum(block_mask.astype(jnp.float32))
    pixel_values = pixels.astype(jnp.float32)
    target_values = targets.astype(jnp.float32)
    loss, pull = jax.vjp(lambda params: total_loss(params, pixel_values, block_mask, target_values, count), weights)
    grads = pull(jnp.ones_like(loss))[0]
    norm = jnp.sqrt(sum((jnp.sum(grad * grad) for grad in grads)))
    factor = clip_limit / jnp.maximum(norm, clip_limit)
    sq_m, sq_v, sq_w = adam(square_weights, square_moment, square_variance, grads[0] * factor, matrix_rate, weight_decay)
    jt_m, jt_v, jt_w = adam(joint_weights, joint_moment, joint_variance, grads[1] * factor, matrix_rate, weight_decay)
    ex_m, ex_v, ex_w = adam(expand_weights, expand_moment, expand_variance, grads[2] * factor, matrix_rate, weight_decay)
    rd_m, rd_v, rd_w = adam(reduce_weights, reduce_moment, reduce_variance, grads[3] * factor, matrix_rate, weight_decay)
    vc_m, vc_v, vc_w = adam(vectors, vector_moment, vector_variance, grads[4] * factor, vector_rate, 0.0)
    return (loss, norm, sq_m, sq_v, sq_w, jt_m, jt_v, jt_w, ex_m, ex_v, ex_w, rd_m, rd_v, rd_w, vc_m, vc_v, vc_w)
```

```python
from functools import partial
import math

import jax
import jax.numpy as jnp
from jax import lax
from jax.experimental import pallas as pl
from jax.experimental.pallas import tpu as pltpu
from jax.sharding import PartitionSpec as P

HEADS = 12
GRID = 14
LANES = 128
BLOCKS = 8
CUTS = 6

norm_eps = 1e-06
beta_one = 0.9
beta_two = 0.999
adam_eps = 1e-08
adam_step = 10.0
matrix_rate = 0.05
vector_rate = 0.3
weight_decay = 0.05
clip_limit = 0.1

f32 = jnp.float32
bf16 = jnp.bfloat16

ROW_P, ROW_QKV, ROW_O, ROW_ONE, ROW_TWO, ROW_H, ROWS = 0, 96, 384, 480, 864, 1248, 1344


def nn(left, right):
    return jnp.dot(left, right, preferred_element_type=f32)


def nt(left, right):
    return lax.dot_general(left, right, (((1,), (1,)), ((), ())), preferred_element_type=f32)


def tn(left, right):
    return lax.dot_general(left, right, (((0,), (0,)), ((), ())), preferred_element_type=f32)


def stats(stream):
    centred = stream - jnp.mean(stream, -1, keepdims=True)
    inverse = lax.rsqrt(jnp.mean(centred * centred, -1, keepdims=True) + norm_eps)
    return (centred * inverse, inverse)


def norm_back(upstream, normed, inverse, gain):
    scaled = upstream * gain
    return inverse * (
        scaled
        - jnp.mean(scaled, -1, keepdims=True)
        - normed * jnp.mean(scaled * normed, -1, keepdims=True)
    )


def column_sum(value):
    return jnp.sum(value, 0, keepdims=True)


def step_kernel(pieces, n_refs, *refs):
    info = refs[0]
    pix, target, mask, pos, vec, bias = refs[1:7]
    sources = refs[7 : 7 + n_refs]
    keep, send, vgrad, loss = refs[7 + n_refs : 11 + n_refs]
    (w, x0, x1, x2, branch, mlp, work, qkv, probs, attn, slope, act, hid, low, sem_in, sem_out) = refs[
        11 + n_refs :
    ]
    length, width = pix.shape
    pairs = width // 256
    first, second = (0, ROW_ONE), (ROW_ONE, ROWS)

    for group, (begin, end) in enumerate((first, second)):
        for source, lead, cut_slot, block_slot, row, rows in pieces:
            lo, hi = max(begin, row), min(end, row + rows)
            if lo >= hi:
                continue
            pltpu.make_async_copy(
                sources[source].at[lead, lo - row : hi - row],
                w.at[info[cut_slot], info[block_slot], lo:hi],
                sem_in.at[group],
            ).start()

    def arrived(group, begin, end):
        part = w.at[:, :, begin:end]
        pltpu.make_async_copy(part, part, sem_in.at[group]).wait()

    def block(cut, row, rows):
        return w[cut, :, row : row + rows, :].reshape(BLOCKS * rows, LANES)

    def pair(i, row, rows=96):
        return jnp.concatenate([block(2 * i, row, rows), block(2 * i + 1, row, rows)], 1)

    def cols(i, size=256):
        return pl.ds(pl.multiple_of(i * size, size), size)

    def all_cuts(row):
        return jnp.concatenate([block(cut, row, 96) for cut in range(CUTS)], 1)

    def put(cut, row, rows, value):
        w[cut, :, row : row + rows, :] = value.astype(bf16).reshape(BLOCKS, rows, LANES)

    def put_pair(i, row, value):
        put(2 * i, row, 96, value[:, :LANES])
        put(2 * i + 1, row, 96, value[:, LANES:])

    def leave(group, begin, end):
        core = info[0]
        for block_index in range(BLOCKS):
            place = info[8 + block_index]
            for number, (out, base) in enumerate(((keep, 3 * core), (send, 3 - 3 * core))):
                pltpu.make_async_copy(
                    w.at[pl.ds(base, 3), block_index, begin:end],
                    out.at[place, :, begin:end],
                    sem_out.at[number, group],
                ).start()

    row_index = lax.broadcasted_iota(jnp.int32, (length, 1), 0)
    is_class = row_index == GRID * GRID
    key_valid = lax.broadcasted_iota(jnp.int32, (1, length), 1) <= GRID * GRID
    lower_half = lax.broadcasted_iota(jnp.int32, (1, LANES), 1) < LANES // 2
    masked = mask[...] > 0.5

    arrived(0, *first)

    @pl.loop(0, pairs)
    def _(i):
        c = cols(i)
        embedded = nn(pix[...], pair(i, ROW_P)) + vec[2:3, c]
        value = jnp.where(is_class, vec[0:1, c], jnp.where(masked, vec[1:2, c], embedded))
        x0[:, c] = value + pos[:, c]

    normed, _ = stats(x0[...])
    low[...] = (normed * vec[3:4, :] + vec[4:5, :]).astype(bf16)

    @pl.loop(0, pairs)
    def _(i):
        parts = [
            w[2 * i + j // 3, :, ROW_QKV + 96 * (j % 3) : ROW_QKV + 96 * (j % 3) + 96, :].reshape(width, LANES)
            for j in range(6)
        ]
        shift = jnp.where(i == 0, vec[5:6, :], jnp.where(i == 1, 0.0, vec[6:7, :]))
        for j in range(3):
            value = nn(low[...], jnp.concatenate(parts[2 * j : 2 * j + 2], 1)) + shift[:, 256 * j : 256 * j + 256]
            qkv[i, :, 256 * j : 256 * j + 256] = value.astype(bf16)

    @pl.loop(0, HEADS // 2)
    def _(i):
        c = cols(i, LANES)
        query, key, value = qkv[0, :, c], qkv[1, :, c], qkv[2, :, c]
        outs = []
        for half in range(2):
            chosen = lower_half if half == 0 else jnp.logical_not(lower_half)
            scores = nt(jnp.where(chosen, query, jnp.zeros_like(query)), key) * 0.125
            scores = jnp.where(key_valid, scores, -1e30)
            shifted = jnp.exp(scores - jnp.max(scores, -1, keepdims=True))
            p = shifted * (1.0 / jnp.sum(shifted, -1, keepdims=True))
            probs[2 * i + half] = p
            outs.append(nn(p.astype(bf16), value))
        attn[:, c] = jnp.where(lower_half, outs[0], outs[1]).astype(bf16)

    @pl.loop(0, pairs)
    def _(i):
        c = cols(i)
        value = nn(attn[...], pair(i, ROW_O)) + vec[7:8, c]
        branch[:, c] = value
        x1[:, c] = x0[:, c] + vec[8:9, c] * value

    normed, _ = stats(x1[...])
    low[...] = (normed * vec[9:10, :] + vec[10:11, :]).astype(bf16)
    arrived(1, *second)

    @pl.loop(0, CUTS)
    def _(cut):
        for j in range(2):
            rhs = jnp.concatenate(
                [
                    w[cut, :, ROW_ONE + 96 * k : ROW_ONE + 96 * k + 96, :].reshape(width, LANES)
                    for k in (2 * j, 2 * j + 1)
                ],
                1,
            )
            c = cols(2 * cut + j)
            inner = nn(low[...], rhs) + bias[:, c]
            cdf = 0.5 + 0.5 * lax.erf(inner * math.sqrt(0.5))
            act[:, c] = (inner * cdf).astype(bf16)
            slope[:, c] = cdf + inner * (jnp.exp(-0.5 * inner * inner) * (1.0 / math.sqrt(2.0 * math.pi)))

    @pl.loop(0, pairs)
    def _(i):
        c = cols(i)
        value = nn(act[...], pair(i, ROW_TWO, 384)) + vec[11:12, c]
        mlp[:, c] = value
        x2[:, c] = x1[:, c] + vec[12:13, c] * value

    normed3, inverse3 = stats(x2[...])
    low[...] = (normed3 * vec[13:14, :] + vec[14:15, :]).astype(bf16)
    loss[...] = jnp.zeros_like(loss)

    @pl.loop(0, pairs)
    def _(i):
        c = cols(i)
        residual = nn(low[...], pair(i, ROW_H)) + vec[15:16, c] - target[:, c].astype(f32)
        size = jnp.abs(residual)
        terms = jnp.where(size < 2.0, 0.25 * residual * residual, size - 1.0)
        loss[0:1, 0:256] += column_sum(jnp.where(masked, terms, 0.0))
        grad = jnp.where(masked, jnp.clip(0.5 * residual, -1.0, 1.0), 0.0)
        vgrad[15:16, c] = column_sum(grad)
        hid[:, c] = grad.astype(bf16)

    upstream = nt(hid[...], all_cuts(ROW_H))
    vgrad[13:14, :] = column_sum(upstream * normed3)
    vgrad[14:15, :] = column_sum(upstream)
    grad2 = norm_back(upstream, normed3, inverse3, vec[13:14, :])
    x2[...] = grad2
    flipped = low[...].T

    @pl.loop(0, pairs)
    def _(i):
        put_pair(i, ROW_H, nn(flipped, hid[:, cols(i)]))

    vgrad[12:13, :] = column_sum(grad2 * mlp[...])
    grad_mlp = grad2 * vec[12:13, :]
    vgrad[11:12, :] = column_sum(grad_mlp)
    hid[...] = grad_mlp.astype(bf16)

    @pl.loop(0, BLOCKS)
    def _(q):
        c = cols(q, 384)
        rhs = jnp.concatenate([w[cut, q, ROW_TWO:ROW_H, :] for cut in range(CUTS)], 1)
        grad_inner = nt(hid[...], rhs) * slope[:, c]
        bias_grad = column_sum(grad_inner)
        slope[0:1, c] = bias_grad
        value = nn(act[:, c].T, hid[...]).astype(bf16)
        for cut in range(CUTS):
            w[cut, q, ROW_TWO:ROW_H, :] = value[:, LANES * cut : LANES * cut + LANES]
        act[:, c] = grad_inner.astype(bf16)

    for k in range(4):
        vgrad[16 + k : 17 + k, :] = slope[0:1, width * k : width * k + width]

    normed2, inverse2 = stats(x1[...])
    low[...] = (normed2 * vec[9:10, :] + vec[10:11, :]).astype(bf16)
    flipped = low[...].T
    work[...] = jnp.zeros_like(work)

    @pl.loop(0, CUTS)
    def _(cut):
        grad_inner = act[:, cols(cut, 512)]
        rhs = jnp.concatenate(
            [w[cut, :, ROW_ONE + 96 * k : ROW_ONE + 96 * k + 96, :].reshape(width, LANES) for k in range(4)], 1
        )
        work[...] += nt(grad_inner, rhs)
        for j in range(2):
            value = nn(flipped, grad_inner[:, 256 * j : 256 * j + 256])
            put(cut, ROW_ONE + 192 * j, 96, value[:, :LANES])
            put(cut, ROW_ONE + 192 * j + 96, 96, value[:, LANES:])

    leave(1, *second)

    upstream = work[...]
    vgrad[9:10, :] = column_sum(upstream * normed2)
    vgrad[10:11, :] = column_sum(upstream)
    grad1 = x2[...] + norm_back(upstream, normed2, inverse2, vec[9:10, :])
    x2[...] = grad1
    vgrad[8:9, :] = column_sum(grad1 * branch[...])
    grad_branch = grad1 * vec[8:9, :]
    vgrad[7:8, :] = column_sum(grad_branch)
    hid[...] = grad_branch.astype(bf16)
    low[...] = nt(hid[...], all_cuts(ROW_O)).astype(bf16)
    flipped = attn[...].T

    @pl.loop(0, pairs)
    def _(i):
        put_pair(i, ROW_O, nn(flipped, hid[:, cols(i)]))

    @pl.loop(0, HEADS // 2)
    def _(i):
        c = cols(i, LANES)
        query, key, value = qkv[0, :, c], qkv[1, :, c], qkv[2, :, c]
        out_grad = low[:, c]
        outs = []
        for half in range(2):
            chosen = lower_half if half == 0 else jnp.logical_not(lower_half)
            p = probs[2 * i + half]
            dp = nt(jnp.where(chosen, out_grad, jnp.zeros_like(out_grad)), value)
            ds = (p * (dp - jnp.sum(p * dp, -1, keepdims=True))).astype(bf16)
            outs.append((nn(ds, key), tn(ds, query), tn(p.astype(bf16), out_grad)))
        dq, dk, dv = (jnp.where(lower_half, one, two) for one, two in zip(*outs))
        dq, dk = (dq * 0.125, dk * 0.125)
        vgrad[5:6, c] = column_sum(dq)
        vgrad[6:7, c] = column_sum(dv)
        qkv[0, :, c], qkv[1, :, c], qkv[2, :, c] = (dq.astype(bf16), dk.astype(bf16), dv.astype(bf16))

    normed1, inverse1 = stats(x0[...])
    low[...] = (normed1 * vec[3:4, :] + vec[4:5, :]).astype(bf16)
    flipped = low[...].T
    work[...] = jnp.zeros_like(work)

    @pl.loop(0, pairs)
    def _(i):
        parts = [
            w[2 * i + j // 3, :, ROW_QKV + 96 * (j % 3) : ROW_QKV + 96 * (j % 3) + 96, :].reshape(width, LANES)
            for j in range(6)
        ]
        work[...] += nt(qkv[i], jnp.concatenate(parts, 1))
        for j in range(3):
            value = nn(flipped, qkv[i, :, 256 * j : 256 * j + 256]).astype(bf16)
            for half in range(2):
                k = 2 * j + half
                w[2 * i + k // 3, :, ROW_QKV + 96 * (k % 3) : ROW_QKV + 96 * (k % 3) + 96, :] = value[
                    :, LANES * half : LANES * half + LANES
                ].reshape(BLOCKS, 96, LANES)

    upstream = work[...]
    vgrad[3:4, :] = column_sum(upstream * normed1)
    vgrad[4:5, :] = column_sum(upstream)
    grad0 = x2[...] + norm_back(upstream, normed1, inverse1, vec[3:4, :])
    vgrad[0:1, :] = column_sum(jnp.where(is_class, grad0, 0.0))
    token = jnp.logical_and(masked, jnp.logical_not(is_class))
    vgrad[1:2, :] = column_sum(jnp.where(token, grad0, 0.0))
    grad_embed = jnp.where(jnp.logical_or(is_class, masked), 0.0, grad0)
    vgrad[2:3, :] = column_sum(grad_embed)
    hid[...] = grad_embed.astype(bf16)
    flipped = pix[...].T

    @pl.loop(0, pairs)
    def _(i):
        put_pair(i, ROW_P, nn(flipped, hid[:, cols(i)]))

    leave(0, *first)
    for number, out in enumerate((keep, send)):
        for group, (begin, end) in enumerate((first, second)):
            part = out.at[:, :, begin:end]
            pltpu.make_async_copy(part, part, sem_out.at[number, group]).wait()


def run_step(info, pix, target, mask, pos, vec, bias, pieces, sources):
    length, width = pix.shape
    hidden = bias.shape[1]
    vmem = pl.BlockSpec(memory_space=pltpu.VMEM)
    anywhere = pl.BlockSpec(memory_space=pl.ANY)
    half = jax.ShapeDtypeStruct((BLOCKS, 3, ROWS, LANES), bf16)
    big = pltpu.VMEM((length, width), f32)
    small = pltpu.VMEM((length, width), bf16)
    return pl.pallas_call(
        partial(step_kernel, pieces, len(sources)),
        out_shape=(
            half,
            half,
            jax.ShapeDtypeStruct((24, width), f32),
            jax.ShapeDtypeStruct((8, 256), f32),
        ),
        in_specs=[pl.BlockSpec(memory_space=pltpu.SMEM)] + [vmem] * 6 + [anywhere] * len(sources),
        out_specs=(anywhere, anywhere, vmem, vmem),
        scratch_shapes=[
            pltpu.VMEM((CUTS, BLOCKS, ROWS, LANES), bf16),
            big,
            big,
            big,
            big,
            big,
            big,
            pltpu.VMEM((3, length, width), bf16),
            pltpu.VMEM((HEADS, length, length), f32),
            small,
            pltpu.VMEM((length, hidden), f32),
            pltpu.VMEM((length, hidden), bf16),
            small,
            small,
            pltpu.SemaphoreType.DMA((2,)),
            pltpu.SemaphoreType.DMA((2, 2)),
        ],
        compiler_params=pltpu.CompilerParams(vmem_limit_bytes=60 * 1024 * 1024),
        name="step",
    )(info, pix, target, mask, pos, vec, bias, *sources)


def pack_kernel(square, joint, expand, reduce, out):
    for cut in range(CUTS):
        for row, n, rows, take in (
            (ROW_P, 1, 96, lambda c: square[0, :, c]),
            (ROW_QKV, 3, 96, lambda c: joint[:, c]),
            (ROW_O, 1, 96, lambda c: square[1, :, c]),
            (ROW_ONE, 4, 96, lambda c: expand[:, c]),
            (ROW_TWO, 1, 384, lambda c: reduce[:, c]),
            (ROW_H, 1, 96, lambda c: square[2, :, c]),
        ):
            for j in range(n):
                begin = LANES * (n * cut + j)
                out[cut, row + rows * j : row + rows * j + rows, :] = take(slice(begin, begin + LANES)).astype(bf16)


def pack(square, joint, expand, reduce):
    vmem = pl.BlockSpec(memory_space=pltpu.VMEM)
    return pl.pallas_call(
        pack_kernel,
        out_shape=jax.ShapeDtypeStruct((CUTS, ROWS, LANES), bf16),
        in_specs=[vmem] * 4,
        out_specs=vmem,
        name="pack",
    )(square, joint, expand, reduce)


def adam(weight, moment, variance, grad, rate, decay):
    moment_new = beta_one * moment + (1.0 - beta_one) * grad
    variance_new = beta_two * variance + (1.0 - beta_two) * grad * grad
    corrected = (
        moment_new
        / (1.0 - beta_one**adam_step)
        / (jnp.sqrt(variance_new / (1.0 - beta_two**adam_step)) + adam_eps)
    )
    return (moment_new, variance_new, weight - rate * (corrected + decay * weight))


def adam_kernel(core, factor, own, other, *refs):
    states, outs = refs[:12], refs[12:]
    cut = pl.program_id(0)
    mine = cut // 3 == core[0]
    scale = factor[0]

    def grad_of(row, rows):
        index = lax.rem(cut, 3)
        grad = jnp.where(mine, own[index, row : row + rows, :], other[index, row : row + rows, :])
        return grad.astype(f32) * scale

    def update(kind, where, row, rows):
        weight, moment, variance = (states[4 * k + kind][where] for k in range(3))
        results = adam(weight, moment, variance, grad_of(row, rows), matrix_rate, weight_decay)
        for k, result in enumerate(results):
            outs[4 * k + kind][where] = result

    for i, row in enumerate((ROW_P, ROW_O, ROW_H)):
        update(0, (i,), row, 96)
    for j in range(3):
        update(1, (slice(None), slice(LANES * j, LANES * j + LANES)), ROW_QKV + 96 * j, 96)
    for j in range(4):
        update(2, (slice(None), slice(LANES * j, LANES * j + LANES)), ROW_ONE + 96 * j, 96)
    update(3, (slice(None), slice(None)), ROW_TWO, 384)


def adam_all(core, factor, own, other, masters, moments, variances):
    smem = pl.BlockSpec(memory_space=pltpu.SMEM)
    whole = pl.BlockSpec(memory_space=pltpu.VMEM)
    blocks = [
        pl.BlockSpec((3, 96, LANES), lambda i: (0, 0, i)),
        pl.BlockSpec((96, 3 * LANES), lambda i: (0, i)),
        pl.BlockSpec((96, 4 * LANES), lambda i: (0, i)),
        pl.BlockSpec((384, LANES), lambda i: (0, i)),
    ]
    outs = [jax.ShapeDtypeStruct(master.shape, f32) for master in masters]
    results = pl.pallas_call(
        adam_kernel,
        grid=(CUTS,),
        out_shape=outs * 3,
        in_specs=[smem, smem, whole, whole] + blocks * 3,
        out_specs=blocks * 3,
        name="adam",
    )(core, factor, own, other, *masters, *moments, *variances)
    return (results[:4], results[4:8], results[8:])


def positions(slot_float, features):
    column = jnp.arange(features)
    frequency = jnp.exp((2 * (column // 2)).astype(f32) * (-math.log(10000.0) / features))
    angle = slot_float[:, None] * frequency[None, :]
    return jnp.where(column % 2 == 0, jnp.sin(angle), jnp.cos(angle))


def seq_flip(value, k, n_seq):
    return lax.ppermute(value, "seq", [(i, i ^ k) for i in range(n_seq)])


def dp_flip(value, k, n_dp):
    return lax.ppermute(value, "dp", [(i, i ^ k) for i in range(n_dp)])


def whole_image(pixels, block_mask, targets, n_seq):
    images, length, features = pixels.shape
    mask_rows = jnp.zeros((images, 16, features), bf16)
    mask_rows = lax.dynamic_update_slice(mask_rows, block_mask.astype(bf16)[:, None, :], (0, 0, 0))
    parcels = jnp.concatenate([pixels, targets, mask_rows], 1)
    me = lax.axis_index("seq")

    def parcel(k):
        return lax.dynamic_index_in_dim(parcels, me ^ k, 0, keepdims=False)

    got = jnp.stack([parcel(0)] + [seq_flip(parcel(k), k, n_seq) for k in range(1, n_seq)])
    got = jnp.take(got, me ^ jnp.arange(n_seq), axis=0)
    return (
        got[:, :length].reshape(n_seq * length, features),
        got[:, length : 2 * length].reshape(n_seq * length, features),
        got[:, 2 * length, :length].reshape(n_seq * length).astype(f32),
    )


def ring_of(n_dp):
    return list(range(0, n_dp, 2)) + list(range(n_dp - 1, 0, -2))


def tree_sum(values):
    while len(values) > 1:
        values = [left + right for left, right in zip(values[0::2], values[1::2])]
    return values[0]


def local(n_dp, n_seq, *args):
    pixels, block_mask, targets = args[:3]
    masters, moments, variances = args[3:8], args[8:13], args[13:18]
    features = pixels.shape[2]
    square, joint, expand, reduce, vectors = masters
    me, group = lax.axis_index("seq"), lax.axis_index("dp")
    ringed = n_dp == BLOCKS and n_seq == 4
    core = me % 2 if ringed else jnp.zeros((), jnp.int32)
    pix, target, mask = whole_image(pixels, block_mask, targets, n_seq)
    pos = positions(jnp.arange(pix.shape[0]).astype(f32), features)
    vectors_low = vectors.astype(bf16)
    if ringed:
        ring = ring_of(n_dp)
        forward = [(ring[i], ring[(i + 1) % n_dp]) for i in range(n_dp)]
        backward = [(b, a) for a, b in forward]
        place_of = jnp.argsort(jnp.array(ring)).astype(jnp.int32)
        ring_array = jnp.array(ring, jnp.int32)
        place = place_of[group]

        def ahead(value):
            return lax.ppermute(value, "dp", forward)

        def behind(value):
            return lax.ppermute(value, "dp", backward)

        def across(value):
            return seq_flip(value, 1, n_seq)

        stacked = jnp.stack([vectors_low] + [dp_flip(vectors_low, k, n_dp) for k in range(1, n_dp)])
        stacked = jnp.take(stacked, group ^ jnp.arange(n_dp), axis=0)
        vec = stacked.transpose(1, 0, 2).reshape(vectors.shape[0], features).astype(f32)

        slabs = pack(square, joint, expand, reduce)
        mine = lax.dynamic_slice_in_dim(slabs, 3 * core, 3, 0)
        sources, pieces = [slabs], [(0, cut, 24 + cut, 48, 0, ROWS) for cut in range(CUTS)]

        def add_piece(value, swapped, distance, row, rows):
            pieces.extend(
                (len(sources), i, 32 + 3 * swapped + i, 48 + distance, row, rows) for i in range(3)
            )
            sources.append(value)

        left, right = mine, mine
        for distance in range(1, 4):
            left, right = ahead(left), behind(right)
            for value, far in ((left, n_dp - distance), (right, distance)):
                add_piece(value, 0, far, 0, ROWS)
                add_piece(across(value), 1, far, 0, ROWS)
        half = ROWS // 2
        left, right = ahead(left[:, :half]), behind(right[:, half:])
        for value, row in ((left, 0), (right, half)):
            add_piece(value, 0, 4, row, half)
            add_piece(across(value), 1, 4, row, half)
        info = jnp.concatenate(
            [
                jnp.stack([core] + [core] * 7),
                (place_of - place) % n_dp,
                jnp.zeros(8, jnp.int32),
                jnp.arange(8, dtype=jnp.int32),
                jnp.stack([3 * core + i for i in range(3)] + [3 - 3 * core + i for i in range(3)] + [core] * 10),
                ring_array[(place + jnp.arange(8)) % n_dp],
                jnp.zeros(8, jnp.int32),
            ]
        ).astype(jnp.int32)
    else:
        gathered = [
            lax.all_gather(value.astype(bf16), "dp", axis=axis, tiled=True)
            for value, axis in zip(masters, (1, 0, 0, 0, 1))
        ]
        vec = gathered[4].astype(f32)

        def cut_up(matrix):
            rows, columns = matrix.shape
            blocks = columns // (CUTS * LANES)
            shaped = matrix.reshape(BLOCKS, rows // BLOCKS, CUTS, blocks, LANES)
            return shaped.transpose(2, 0, 3, 1, 4).reshape(CUTS, BLOCKS, -1, LANES)

        order = (gathered[0][0], gathered[1], gathered[0][1], gathered[2], gathered[3], gathered[0][2])
        slabs = jnp.concatenate([cut_up(matrix) for matrix in order], 2)
        sources = [slabs.reshape(CUTS * BLOCKS, ROWS, LANES)]
        pieces = [(0, BLOCKS * cut + q, 24 + cut, 48 + q, 0, ROWS) for cut in range(CUTS) for q in range(BLOCKS)]
        eight = jnp.arange(8, dtype=jnp.int32)
        info = jnp.concatenate([eight * 0, eight, eight * 0, eight, eight, eight, eight, eight])

    keep, send, vgrad, loss_rows = run_step(
        info, pix, target, mask[:, None], pos, vec, vec[16:].reshape(1, -1), tuple(pieces), tuple(sources)
    )
    rows = vectors.shape[0]
    loss_part, count_part = jnp.sum(loss_rows), jnp.sum(mask)

    if ringed:
        got = across(send)

        def partial_sum(r, part=slice(None)):
            return keep[r][:, part].astype(f32) + got[r][:, part].astype(f32)

        low_part, high_part = slice(0, half), slice(half, ROWS)
        left = ahead(partial_sum(4, low_part).astype(bf16))
        right = behind(partial_sum(4, high_part).astype(bf16))
        left = jnp.concatenate([partial_sum(3, low_part) + left.astype(f32), partial_sum(3, high_part)], 1)
        right = jnp.concatenate([partial_sum(5, low_part), partial_sum(5, high_part) + right.astype(f32)], 1)
        for r in (2, 1, 0):
            left, right = ahead(left.astype(bf16)).astype(f32), behind(right.astype(bf16)).astype(f32)
            if r:
                left, right = left + partial_sum(r), right + partial_sum(8 - r)
        own = (partial_sum(0) + left + right).astype(bf16)
        other_chip = seq_flip(own, 2, n_seq)
        own = (own.astype(f32) + other_chip.astype(f32)).astype(bf16)
        other = across(own)

        extra = jnp.stack([jnp.full((features,), loss_part), jnp.full((features,), count_part)])
        small = jnp.concatenate([vgrad[:rows], extra]).reshape(rows + 2, n_dp, -1).transpose(1, 0, 2)
        for k in (1, 2):
            small = small + seq_flip(small, k, n_seq)

        def row_of(k):
            return lax.dynamic_index_in_dim(small, group ^ k, 0, keepdims=False)

        small = tree_sum([row_of(0)] + [dp_flip(row_of(k), k, n_dp) for k in range(1, n_dp)])
        vector_grad, loss_sum, count = small[:rows], small[rows, 0], small[rows + 1, 0]
        squares = (
            jnp.sum(jnp.square(own.astype(f32))) + jnp.sum(jnp.square(other.astype(f32))) + jnp.sum(vector_grad**2)
        )
        squares = jnp.full((1, LANES), squares)
        squares = tree_sum([squares] + [dp_flip(squares, k, n_dp) for k in range(1, n_dp)])[0, 0]
    else:
        canonical = jnp.concatenate([keep, send], 1).transpose(1, 0, 2, 3)

        def join(row, end, blocks):
            part = canonical[:, :, row:end].astype(f32).reshape(CUTS, BLOCKS, blocks, -1, LANES)
            return part.transpose(1, 3, 0, 2, 4).reshape(-1, CUTS * blocks * LANES)

        whole = (
            jnp.stack([join(ROW_P, ROW_QKV, 1), join(ROW_O, ROW_ONE, 1), join(ROW_H, ROWS, 1)]),
            join(ROW_QKV, ROW_O, 3),
            join(ROW_ONE, ROW_TWO, 4),
            join(ROW_TWO, ROW_H, 1),
            vgrad[:rows],
        )
        grads = [
            lax.psum_scatter(grad, "dp", scatter_dimension=axis, tiled=True)
            for grad, axis in zip(whole, (1, 0, 0, 0, 1))
        ]
        grads = lax.psum(grads, "seq")
        vector_grad = grads[4]
        squares = lax.psum(sum(jnp.sum(grad * grad) for grad in grads), "dp")
        loss_sum, count = lax.psum((loss_part, count_part), ("dp", "seq"))

    norm = jnp.sqrt(squares) / count
    factor = clip_limit / jnp.maximum(norm, clip_limit) / count
    if ringed:
        new = adam_all(
            core.reshape(1), factor.reshape(1), own, other, masters[:4], moments[:4], variances[:4]
        )
    else:
        updated = [
            adam(master, moment, variance, grad * factor, matrix_rate, weight_decay)
            for master, moment, variance, grad in zip(masters[:4], moments, variances, grads)
        ]
        new = tuple(zip(*updated))
    last = adam(vectors, moments[4], variances[4], vector_grad * factor, vector_rate, 0.0)
    outs = []
    for kind in range(4):
        outs.extend((new[0][kind], new[1][kind], new[2][kind]))
    return (loss_sum / count, norm, *outs, *last)


def solution(mesh):
    matrix = P("dp", None)
    state = (P(None, "dp", None), matrix, matrix, matrix, P(None, "dp"))
    in_specs = (P("dp", "seq", None), P("dp", "seq"), P("dp", "seq", None)) + state * 3
    out_specs = (P(), P()) + tuple(spec for spec in state for _ in range(3))
    return jax.shard_map(
        partial(local, mesh.shape["dp"], mesh.shape["seq"]),
        mesh=mesh,
        in_specs=in_specs,
        out_specs=out_specs,
        check_vma=False,
    )
```

```python
from functools import partial
import math

import jax
import jax.numpy as jnp
from jax import lax
from jax.experimental import pallas as pl
from jax.experimental.pallas import tpu as pltpu
from jax.sharding import PartitionSpec as P

HEADS = 12
GRID = 14
LANES = 128
BLOCKS = 8
CUTS = 6

norm_eps = 1e-06
beta_one = 0.9
beta_two = 0.999
adam_eps = 1e-08
adam_step = 10.0
matrix_rate = 0.05
vector_rate = 0.3
weight_decay = 0.05
clip_limit = 0.1

f32 = jnp.float32
bf16 = jnp.bfloat16

ROW_P, ROW_QKV, ROW_O, ROW_ONE, ROW_TWO, ROW_H, ROWS = 0, 96, 384, 480, 864, 1248, 1344
VEC_ROWS = 32
PLACES = ((4,), (3, 5), (2, 6, 1, 7, 0))
SPLIT_PLACES = ((4, 3, 5), (2, 6, 1, 7, 0))
OUTS = 2 * len(PLACES) + 2 * len(SPLIT_PLACES)
PART, CUT, BLOCK = 8, 24, 48


def nn(left, right):
    return jnp.dot(left, right, preferred_element_type=f32)


def nt(left, right):
    return lax.dot_general(left, right, (((1,), (1,)), ((), ())), preferred_element_type=f32)


def tn(left, right):
    return lax.dot_general(left, right, (((0,), (0,)), ((), ())), preferred_element_type=f32)


def stats(stream):
    centred = stream - jnp.mean(stream, -1, keepdims=True)
    inverse = lax.rsqrt(jnp.mean(centred * centred, -1, keepdims=True) + norm_eps)
    return (centred * inverse, inverse)


def norm_back(upstream, normed, inverse, gain):
    scaled = upstream * gain
    return inverse * (
        scaled
        - jnp.mean(scaled, -1, keepdims=True)
        - normed * jnp.mean(scaled * normed, -1, keepdims=True)
    )


def column_sum(value):
    return jnp.sum(value, 0, keepdims=True)


def step_kernel(pieces, vec_pieces, n_refs, *refs):
    info, pos = refs[:2]
    n_parts = n_refs[0]
    parcels, sources = refs[2 : 2 + n_parts], refs[2 + n_parts : 2 + sum(n_refs)]
    *outs, vgrad = refs[2 + sum(n_refs) : 3 + sum(n_refs) + OUTS]
    w, vec_blocks, vec, pix, target, mask_rows, mask, bias, *refs = refs[3 + sum(n_refs) + OUTS :]
    (x0, x1, x2, branch, mlp, work, qkv, probs, attn, slope, act, hid, low, sem_in, sem_part, sem_out) = refs
    length, width = pix.shape
    part = length // n_parts
    pairs = width // 256
    first, second = (0, ROW_ONE), (ROW_ONE, ROWS)

    for k in range(n_parts):
        slot = info[PART + k]
        here = pl.ds(pl.multiple_of(slot * part, part), part)
        pltpu.make_async_copy(parcels[k].at[:part], pix.at[here], sem_part.at[0]).start()
        pltpu.make_async_copy(parcels[k].at[part : 2 * part], target.at[here], sem_part.at[1]).start()
        pltpu.make_async_copy(parcels[k].at[2 * part :, :LANES], mask_rows.at[slot], sem_part.at[2]).start()

    for source, lead, row, block_slot in vec_pieces:
        pltpu.make_async_copy(
            sources[source].at[lead, row : row + VEC_ROWS], vec_blocks.at[info[block_slot]], sem_part.at[3]
        ).start()

    for group, (begin, end) in enumerate((first, second)):
        for source, lead, cut_slot, block_slot in pieces:
            pltpu.make_async_copy(
                sources[source].at[lead, begin:end],
                w.at[info[cut_slot], info[block_slot], begin:end],
                sem_in.at[group],
            ).start()

    for number, whole in enumerate((pix, target, mask_rows, vec_blocks)):
        pltpu.make_async_copy(whole, whole, sem_part.at[number]).wait()
    diagonal = lax.broadcasted_iota(jnp.int32, (part, LANES), 0) == lax.broadcasted_iota(
        jnp.int32, (part, LANES), 1
    )
    for k in range(n_parts):
        row = mask_rows[k].astype(f32)[:1]
        mask[part * k : part * k + part, :] = jnp.sum(jnp.where(diagonal, row, 0.0), 1, keepdims=True)
    for q in range(BLOCKS):
        vec[:, 96 * q : 96 * q + 96] = vec_blocks[q].astype(f32)[:, :96]
    for k in range(4):
        bias[:, width * k : width * k + width] = vec[16 + k : 17 + k, :]

    def arrived(group, begin, end):
        part = w.at[:, :, begin:end]
        pltpu.make_async_copy(part, part, sem_in.at[group]).wait()

    def block(cut, row, rows):
        return w[cut, :, row : row + rows, :].reshape(BLOCKS * rows, LANES)

    def pair(i, row, rows=96):
        return jnp.concatenate([block(2 * i, row, rows), block(2 * i + 1, row, rows)], 1)

    def cols(i, size=256):
        return pl.ds(pl.multiple_of(i * size, size), size)

    def all_cuts(row):
        return jnp.concatenate([block(cut, row, 96) for cut in range(CUTS)], 1)

    def put(cut, row, rows, value):
        w[cut, :, row : row + rows, :] = value.astype(bf16).reshape(BLOCKS, rows, LANES)

    def put_pair(i, row, value):
        put(2 * i, row, 96, value[:, :LANES])
        put(2 * i + 1, row, 96, value[:, LANES:])

    def out_rows(number, begin, end):
        return (begin, end) if number < 2 * len(PLACES) else (begin // 2, end // 2)

    def leave(group, begin, end):
        core, side = info[0], info[1]
        half = (end - begin) // 2
        for number, out in enumerate(outs):
            split, away = number >= 2 * len(PLACES), number % 2
            first_cut = 3 * (core ^ away)
            lo, hi = out_rows(number, begin, end)
            for i, place in enumerate((PLACES + SPLIT_PLACES)[number // 2]):
                block_index = info[BLOCK + place]
                if not split:
                    pltpu.make_async_copy(
                        w.at[pl.ds(first_cut, 2), block_index, begin:end],
                        out.at[i, :, lo:hi],
                        sem_out.at[number, group],
                    ).start()
                    continue
                for part in range(2):
                    rows = pl.ds(pl.multiple_of(begin + half * (side ^ part), 16), half)
                    pltpu.make_async_copy(
                        w.at[first_cut + 2, block_index, rows], out.at[i, part, lo:hi], sem_out.at[number, group]
                    ).start()

    row_index = lax.broadcasted_iota(jnp.int32, (length, 1), 0)
    is_class = row_index == GRID * GRID
    key_valid = lax.broadcasted_iota(jnp.int32, (1, length), 1) <= GRID * GRID
    lower_half = lax.broadcasted_iota(jnp.int32, (1, LANES), 1) < LANES // 2
    masked = mask[...] > 0.5

    arrived(0, *first)

    @pl.loop(0, pairs)
    def _(i):
        c = cols(i)
        embedded = nn(pix[...], pair(i, ROW_P)) + vec[2:3, c]
        value = jnp.where(is_class, vec[0:1, c], jnp.where(masked, vec[1:2, c], embedded))
        x0[:, c] = value + pos[:, c]

    normed, _ = stats(x0[...])
    low[...] = (normed * vec[3:4, :] + vec[4:5, :]).astype(bf16)

    @pl.loop(0, pairs)
    def _(i):
        parts = [
            w[2 * i + j // 3, :, ROW_QKV + 96 * (j % 3) : ROW_QKV + 96 * (j % 3) + 96, :].reshape(width, LANES)
            for j in range(6)
        ]
        shift = jnp.where(i == 0, vec[5:6, :], jnp.where(i == 1, 0.0, vec[6:7, :]))
        for j in range(3):
            value = nn(low[...], jnp.concatenate(parts[2 * j : 2 * j + 2], 1)) + shift[:, 256 * j : 256 * j + 256]
            qkv[i, :, 256 * j : 256 * j + 256] = value.astype(bf16)

    @pl.loop(0, HEADS // 2)
    def _(i):
        c = cols(i, LANES)
        query, key, value = qkv[0, :, c], qkv[1, :, c], qkv[2, :, c]
        outs = []
        for half in range(2):
            chosen = lower_half if half == 0 else jnp.logical_not(lower_half)
            scores = nt(jnp.where(chosen, query, jnp.zeros_like(query)), key) * 0.125
            scores = jnp.where(key_valid, scores, -1e30)
            shifted = jnp.exp(scores - jnp.max(scores, -1, keepdims=True))
            p = shifted * (1.0 / jnp.sum(shifted, -1, keepdims=True))
            probs[2 * i + half] = p
            outs.append(nn(p.astype(bf16), value))
        attn[:, c] = jnp.where(lower_half, outs[0], outs[1]).astype(bf16)

    @pl.loop(0, pairs)
    def _(i):
        c = cols(i)
        value = nn(attn[...], pair(i, ROW_O)) + vec[7:8, c]
        branch[:, c] = value
        x1[:, c] = x0[:, c] + vec[8:9, c] * value

    normed, _ = stats(x1[...])
    low[...] = (normed * vec[9:10, :] + vec[10:11, :]).astype(bf16)
    arrived(1, *second)

    @pl.loop(0, CUTS)
    def _(cut):
        for j in range(2):
            rhs = jnp.concatenate(
                [
                    w[cut, :, ROW_ONE + 96 * k : ROW_ONE + 96 * k + 96, :].reshape(width, LANES)
                    for k in (2 * j, 2 * j + 1)
                ],
                1,
            )
            c = cols(2 * cut + j)
            inner = nn(low[...], rhs) + bias[:, c]
            cdf = 0.5 + 0.5 * lax.erf(inner * math.sqrt(0.5))
            act[:, c] = (inner * cdf).astype(bf16)
            slope[:, c] = cdf + inner * (jnp.exp(-0.5 * inner * inner) * (1.0 / math.sqrt(2.0 * math.pi)))

    @pl.loop(0, pairs)
    def _(i):
        c = cols(i)
        value = nn(act[...], pair(i, ROW_TWO, 384)) + vec[11:12, c]
        mlp[:, c] = value
        x2[:, c] = x1[:, c] + vec[12:13, c] * value

    normed3, inverse3 = stats(x2[...])
    low[...] = (normed3 * vec[13:14, :] + vec[14:15, :]).astype(bf16)
    loss = work
    loss[0:1, 0:256] = jnp.zeros((1, 256), f32)

    @pl.loop(0, pairs)
    def _(i):
        c = cols(i)
        residual = nn(low[...], pair(i, ROW_H)) + vec[15:16, c] - target[:, c].astype(f32)
        size = jnp.abs(residual)
        terms = jnp.where(size < 2.0, 0.25 * residual * residual, size - 1.0)
        loss[0:1, 0:256] += column_sum(jnp.where(masked, terms, 0.0))
        grad = jnp.where(masked, jnp.clip(0.5 * residual, -1.0, 1.0), 0.0)
        vgrad[15:16, c] = column_sum(grad)
        hid[:, c] = grad.astype(bf16)

    vgrad[20:21, :] = jnp.broadcast_to(jnp.sum(loss[0:1, 0:256], 1, keepdims=True), (1, width))
    vgrad[21:22, :] = jnp.broadcast_to(jnp.sum(mask[...], 0, keepdims=True), (1, width))
    vgrad[22:24, :] = jnp.zeros((2, width), f32)
    upstream = nt(hid[...], all_cuts(ROW_H))
    vgrad[13:14, :] = column_sum(upstream * normed3)
    vgrad[14:15, :] = column_sum(upstream)
    grad2 = norm_back(upstream, normed3, inverse3, vec[13:14, :])
    x2[...] = grad2
    flipped = low[...].T

    @pl.loop(0, pairs)
    def _(i):
        put_pair(i, ROW_H, nn(flipped, hid[:, cols(i)]))

    vgrad[12:13, :] = column_sum(grad2 * mlp[...])
    grad_mlp = grad2 * vec[12:13, :]
    vgrad[11:12, :] = column_sum(grad_mlp)
    hid[...] = grad_mlp.astype(bf16)

    @pl.loop(0, BLOCKS)
    def _(q):
        c = cols(q, 384)
        rhs = jnp.concatenate([w[cut, q, ROW_TWO:ROW_H, :] for cut in range(CUTS)], 1)
        grad_inner = nt(hid[...], rhs) * slope[:, c]
        bias_grad = column_sum(grad_inner)
        slope[0:1, c] = bias_grad
        value = nn(act[:, c].T, hid[...]).astype(bf16)
        for cut in range(CUTS):
            w[cut, q, ROW_TWO:ROW_H, :] = value[:, LANES * cut : LANES * cut + LANES]
        act[:, c] = grad_inner.astype(bf16)

    for k in range(4):
        vgrad[16 + k : 17 + k, :] = slope[0:1, width * k : width * k + width]

    normed2, inverse2 = stats(x1[...])
    low[...] = (normed2 * vec[9:10, :] + vec[10:11, :]).astype(bf16)
    flipped = low[...].T
    work[...] = jnp.zeros_like(work)

    @pl.loop(0, CUTS)
    def _(cut):
        grad_inner = act[:, cols(cut, 512)]
        rhs = jnp.concatenate(
            [w[cut, :, ROW_ONE + 96 * k : ROW_ONE + 96 * k + 96, :].reshape(width, LANES) for k in range(4)], 1
        )
        work[...] += nt(grad_inner, rhs)
        for j in range(2):
            value = nn(flipped, grad_inner[:, 256 * j : 256 * j + 256])
            put(cut, ROW_ONE + 192 * j, 96, value[:, :LANES])
            put(cut, ROW_ONE + 192 * j + 96, 96, value[:, LANES:])

    leave(1, *second)

    upstream = work[...]
    vgrad[9:10, :] = column_sum(upstream * normed2)
    vgrad[10:11, :] = column_sum(upstream)
    grad1 = x2[...] + norm_back(upstream, normed2, inverse2, vec[9:10, :])
    x2[...] = grad1
    vgrad[8:9, :] = column_sum(grad1 * branch[...])
    grad_branch = grad1 * vec[8:9, :]
    vgrad[7:8, :] = column_sum(grad_branch)
    hid[...] = grad_branch.astype(bf16)
    low[...] = nt(hid[...], all_cuts(ROW_O)).astype(bf16)
    flipped = attn[...].T

    @pl.loop(0, pairs)
    def _(i):
        put_pair(i, ROW_O, nn(flipped, hid[:, cols(i)]))

    @pl.loop(0, HEADS // 2)
    def _(i):
        c = cols(i, LANES)
        query, key, value = qkv[0, :, c], qkv[1, :, c], qkv[2, :, c]
        out_grad = low[:, c]
        outs = []
        for half in range(2):
            chosen = lower_half if half == 0 else jnp.logical_not(lower_half)
            p = probs[2 * i + half]
            dp = nt(jnp.where(chosen, out_grad, jnp.zeros_like(out_grad)), value)
            ds = (p * (dp - jnp.sum(p * dp, -1, keepdims=True))).astype(bf16)
            outs.append((nn(ds, key), tn(ds, query), tn(p.astype(bf16), out_grad)))
        dq, dk, dv = (jnp.where(lower_half, one, two) for one, two in zip(*outs))
        dq, dk = (dq * 0.125, dk * 0.125)
        vgrad[5:6, c] = column_sum(dq)
        vgrad[6:7, c] = column_sum(dv)
        qkv[0, :, c], qkv[1, :, c], qkv[2, :, c] = (dq.astype(bf16), dk.astype(bf16), dv.astype(bf16))

    normed1, inverse1 = stats(x0[...])
    low[...] = (normed1 * vec[3:4, :] + vec[4:5, :]).astype(bf16)
    flipped = low[...].T
    work[...] = jnp.zeros_like(work)

    @pl.loop(0, pairs)
    def _(i):
        parts = [
            w[2 * i + j // 3, :, ROW_QKV + 96 * (j % 3) : ROW_QKV + 96 * (j % 3) + 96, :].reshape(width, LANES)
            for j in range(6)
        ]
        work[...] += nt(qkv[i], jnp.concatenate(parts, 1))
        for j in range(3):
            value = nn(flipped, qkv[i, :, 256 * j : 256 * j + 256]).astype(bf16)
            for half in range(2):
                k = 2 * j + half
                w[2 * i + k // 3, :, ROW_QKV + 96 * (k % 3) : ROW_QKV + 96 * (k % 3) + 96, :] = value[
                    :, LANES * half : LANES * half + LANES
                ].reshape(BLOCKS, 96, LANES)

    upstream = work[...]
    vgrad[3:4, :] = column_sum(upstream * normed1)
    vgrad[4:5, :] = column_sum(upstream)
    grad0 = x2[...] + norm_back(upstream, normed1, inverse1, vec[3:4, :])
    vgrad[0:1, :] = column_sum(jnp.where(is_class, grad0, 0.0))
    token = jnp.logical_and(masked, jnp.logical_not(is_class))
    vgrad[1:2, :] = column_sum(jnp.where(token, grad0, 0.0))
    grad_embed = jnp.where(jnp.logical_or(is_class, masked), 0.0, grad0)
    vgrad[2:3, :] = column_sum(grad_embed)
    hid[...] = grad_embed.astype(bf16)
    flipped = pix[...].T

    @pl.loop(0, pairs)
    def _(i):
        put_pair(i, ROW_P, nn(flipped, hid[:, cols(i)]))

    leave(0, *first)
    for number, out in enumerate(outs):
        for group, (begin, end) in enumerate((first, second)):
            lo, hi = out_rows(number, begin, end)
            rows = out.at[:, :, lo:hi]
            pltpu.make_async_copy(rows, rows, sem_out.at[number, group]).wait()


def run_step(info, pos, parcels, pieces, vec_pieces, sources):
    length, width = pos.shape
    hidden = 4 * width
    vmem = pl.BlockSpec(memory_space=pltpu.VMEM)
    anywhere = pl.BlockSpec(memory_space=pl.ANY)
    big = pltpu.VMEM((length, width), f32)
    small = pltpu.VMEM((length, width), bf16)
    *outs, vgrad = pl.pallas_call(
        partial(step_kernel, pieces, vec_pieces, (len(parcels), len(sources))),
        out_shape=(
            *(jax.ShapeDtypeStruct((len(places), 2, ROWS, LANES), bf16) for places in PLACES for _ in range(2)),
            *(
                jax.ShapeDtypeStruct((len(places), 2, ROWS // 2, LANES), bf16)
                for places in SPLIT_PLACES
                for _ in range(2)
            ),
            jax.ShapeDtypeStruct((24, width), f32),
        ),
        in_specs=[pl.BlockSpec(memory_space=pltpu.SMEM)] + [vmem] + [anywhere] * (len(parcels) + len(sources)),
        out_specs=(*[anywhere] * OUTS, vmem),
        scratch_shapes=[
            pltpu.VMEM((CUTS, BLOCKS, ROWS, LANES), bf16),
            pltpu.VMEM((BLOCKS, VEC_ROWS, LANES), bf16),
            pltpu.VMEM((VEC_ROWS, width), f32),
            small,
            small,
            pltpu.VMEM((len(parcels), 16, LANES), bf16),
            pltpu.VMEM((length, 1), f32),
            pltpu.VMEM((1, hidden), f32),
            big,
            big,
            big,
            big,
            big,
            big,
            pltpu.VMEM((3, length, width), bf16),
            pltpu.VMEM((HEADS, length, length), f32),
            small,
            pltpu.VMEM((length, hidden), f32),
            pltpu.VMEM((length, hidden), bf16),
            small,
            small,
            pltpu.SemaphoreType.DMA((2,)),
            pltpu.SemaphoreType.DMA((4,)),
            pltpu.SemaphoreType.DMA((OUTS, 2)),
        ],
        compiler_params=pltpu.CompilerParams(vmem_limit_bytes=60 * 1024 * 1024),
        name="step",
    )(info, pos, *parcels, *sources)
    return outs, vgrad


def pack_kernel(chosen, square, joint, expand, reduce, vectors, out, *streams):
    for cut in range(CUTS):
        for row, n, rows, take in (
            (ROW_P, 1, 96, lambda c: square[0, :, c]),
            (ROW_QKV, 3, 96, lambda c: joint[:, c]),
            (ROW_O, 1, 96, lambda c: square[1, :, c]),
            (ROW_ONE, 4, 96, lambda c: expand[:, c]),
            (ROW_TWO, 1, 384, lambda c: reduce[:, c]),
            (ROW_H, 1, 96, lambda c: square[2, :, c]),
        ):
            for j in range(n):
                begin = LANES * (n * cut + j)
                out[cut, row + rows * j : row + rows * j + rows, :] = take(slice(begin, begin + LANES)).astype(bf16)
    for number, stream in enumerate(streams):
        for i in range(2):
            stream[i, :ROWS] = out[chosen[2 * number + i]]
            stream[i, ROWS:] = jnp.zeros((VEC_ROWS, LANES), bf16)
            stream[i, ROWS:, : vectors.shape[1]] = jnp.concatenate(
                [vectors[...], jnp.zeros((VEC_ROWS - vectors.shape[0], vectors.shape[1]), f32)]
            ).astype(bf16)


def pack(chosen, *shards):
    vmem = pl.BlockSpec(memory_space=pltpu.VMEM)
    return pl.pallas_call(
        pack_kernel,
        out_shape=[jax.ShapeDtypeStruct((CUTS, ROWS, LANES), bf16)]
        + [jax.ShapeDtypeStruct((2, ROWS + VEC_ROWS, LANES), bf16)] * 2,
        in_specs=[pl.BlockSpec(memory_space=pltpu.SMEM)] + [vmem] * 5,
        out_specs=[vmem] * 3,
        name="pack",
    )(chosen, *shards)


def parcel_kernel(slots, pixels, block_mask, targets, *outs):
    length = pixels.shape[1]
    top = lax.broadcasted_iota(jnp.int32, (16, length), 0) == 0
    for k, out in enumerate(outs):
        slot = slots[k]
        out[:length, :] = pixels[slot]
        out[length : 2 * length, :] = targets[slot]
        out[2 * length :, :] = jnp.zeros((16, out.shape[1]), bf16)
        row = block_mask[pl.ds(slot, 1), :].astype(f32)
        out[2 * length :, :length] = jnp.where(top, row, 0.0).astype(bf16)


def make_parcels(slots, pixels, block_mask, targets):
    images, length, features = pixels.shape
    vmem = pl.BlockSpec(memory_space=pltpu.VMEM)
    return pl.pallas_call(
        parcel_kernel,
        out_shape=[jax.ShapeDtypeStruct((2 * length + 16, features), bf16)] * images,
        in_specs=[pl.BlockSpec(memory_space=pltpu.SMEM)] + [vmem] * 3,
        out_specs=[vmem] * images,
        name="parcels",
    )(slots, pixels, block_mask, targets)


def adam(weight, moment, variance, grad, rate, decay):
    moment_new = beta_one * moment + (1.0 - beta_one) * grad
    variance_new = beta_two * variance + (1.0 - beta_two) * grad * grad
    corrected = (
        moment_new
        * (1.0 / (1.0 - beta_one**adam_step))
        / (jnp.sqrt(variance_new * (1.0 / (1.0 - beta_two**adam_step))) + adam_eps)
    )
    return (moment_new, variance_new, weight - rate * (corrected + decay * weight))


def adam_kernel(core, squares, table, own, split_own, other, split_other, *refs):
    masters, moments, variances = refs[:5], refs[5:10], refs[10:15]
    loss_out, norm_out, *outs = refs[15:32]
    buffers, sem_in, sem_out = refs[32:44], *refs[44:]
    order = (3, 2, 1, 0)
    for kind in order:
        for k, state in enumerate((masters, moments, variances)):
            pltpu.make_async_copy(state[kind], buffers[4 * k + kind], sem_in.at[4 * k + kind]).start()
    rows = masters[4].shape[0]
    count = table[rows + 1 : rows + 2, 0:1]
    norm = jnp.sqrt(squares[0:1, 0:1]) / count
    scale = clip_limit / jnp.maximum(norm, clip_limit) / count
    loss_out[0, 0] = (table[rows : rows + 1, 0:1] / count)[0, 0]
    norm_out[0, 0] = norm[0, 0]

    def grad_of(cut, row, rows):
        mine = cut // 3 == core[0]
        index, part = jnp.minimum(lax.rem(cut, 3), 1), slice(row, row + rows)
        grad = jnp.where(mine, own[index, part, :], other[index, part, :])
        split = jnp.where(mine, split_own[part, :], split_other[part, :])
        return jnp.where(lax.rem(cut, 3) == 2, split, grad).astype(f32) * scale

    def update(kind, where, cut, row, rows):
        states = (buffers[4 * k + kind][where] for k in range(3))
        values = adam(*states, grad_of(cut, row, rows), matrix_rate, weight_decay)
        for k, value in zip((1, 2, 0), values):
            buffers[4 * k + kind][where] = value

    def each(kind, body):
        for k, state in enumerate((masters, moments, variances)):
            pltpu.make_async_copy(state[kind], buffers[4 * k + kind], sem_in.at[4 * k + kind]).wait()
        pl.loop(0, CUTS)(body)
        for k in range(3):
            out = outs[5 * ((k + 2) % 3) + kind]
            pltpu.make_async_copy(buffers[4 * k + kind], out, sem_out.at[4 * k + kind]).start()

    def lanes(block):
        return pl.ds(pl.multiple_of(block * LANES, LANES), LANES)

    def reduce_body(cut):
        for k in range(4):
            update(3, (slice(96 * k, 96 * k + 96), lanes(cut)), cut, ROW_TWO + 96 * k, 96)

    def expand_body(cut):
        for k in range(4):
            update(2, (slice(None), lanes(4 * cut + k)), cut, ROW_ONE + 96 * k, 96)

    def joint_body(cut):
        for k in range(3):
            update(1, (slice(None), lanes(3 * cut + k)), cut, ROW_QKV + 96 * k, 96)

    def square_body(cut):
        for i, row in enumerate((ROW_P, ROW_O, ROW_H)):
            update(0, (i, slice(None), lanes(cut)), cut, row, 96)

    for kind, body in zip(order, (reduce_body, expand_body, joint_body, square_body)):
        each(kind, body)
    states = (state[4][...] for state in (masters, moments, variances))
    for k, value in enumerate(adam(*states, table[:rows, :] * scale, vector_rate, 0.0)):
        outs[5 * k + 4][...] = value
    for k in range(3):
        for kind in range(4):
            out = outs[5 * ((k + 2) % 3) + kind]
            pltpu.make_async_copy(buffers[4 * k + kind], out, sem_out.at[4 * k + kind]).wait()


def adam_all(core, squares, table, grads, masters, moments, variances):
    smem = pl.BlockSpec(memory_space=pltpu.SMEM)
    vmem = pl.BlockSpec(memory_space=pltpu.VMEM)
    anywhere = pl.BlockSpec(memory_space=pl.ANY)
    shapes = [jax.ShapeDtypeStruct(master.shape, f32) for master in masters]
    loss, norm, *results = pl.pallas_call(
        adam_kernel,
        out_shape=[jax.ShapeDtypeStruct((1, 1), f32)] * 2 + shapes * 3,
        in_specs=[smem] + [vmem] * (2 + len(grads)) + ([anywhere] * 4 + [vmem]) * 3,
        out_specs=[smem] * 2 + ([anywhere] * 4 + [vmem]) * 3,
        scratch_shapes=[pltpu.VMEM(shape.shape, f32) for shape in shapes[:4] * 3]
        + [pltpu.SemaphoreType.DMA((12,))] * 2,
        compiler_params=pltpu.CompilerParams(vmem_limit_bytes=56 * 1024 * 1024),
        name="adam",
    )(core, squares, table, *grads, *masters, *moments, *variances)
    return loss.reshape(()), norm.reshape(()), results[:5], results[5:10], results[10:]


def positions(slot_float, features):
    column = jnp.arange(features)
    frequency = jnp.exp((2 * (column // 2)).astype(f32) * (-math.log(10000.0) / features))
    angle = slot_float[:, None] * frequency[None, :]
    return jnp.where(column % 2 == 0, jnp.sin(angle), jnp.cos(angle))


def seq_flip(value, k, n_seq):
    return lax.ppermute(value, "seq", [(i, i ^ k) for i in range(n_seq)])


def hop(value, dp_k, seq_k, n_dp, n_seq):
    pairs = [(dp * n_seq + seq, (dp ^ dp_k) * n_seq + (seq ^ seq_k)) for dp in range(n_dp) for seq in range(n_seq)]
    return lax.ppermute(value, ("dp", "seq"), pairs)


def tick(*values):
    return lax.optimization_barrier(values)


def ring_of(n_dp):
    return list(range(0, n_dp, 2)) + list(range(n_dp - 1, 0, -2))


def tree_sum(values):
    while len(values) > 1:
        values = [left + right for left, right in zip(values[0::2], values[1::2])]
    return values[0]


def local(n_dp, n_seq, *args):
    pixels, block_mask, targets = args[:3]
    masters, moments, variances = args[3:8], args[8:13], args[13:18]
    length, features = pixels.shape[1:]
    square, joint, expand, reduce, vectors = masters
    me, group = lax.axis_index("seq"), lax.axis_index("dp")
    ringed = n_dp == BLOCKS and n_seq == 4
    core, side = (me % 2, me // 2) if ringed else (jnp.zeros((), jnp.int32),) * 2
    slots = me ^ jnp.arange(n_seq, dtype=jnp.int32)
    slots_info = jnp.concatenate([slots, jnp.zeros(16 - n_seq, jnp.int32)])
    eight = jnp.arange(8, dtype=jnp.int32)
    first_info = jnp.stack([core, side] + [core] * 6).astype(jnp.int32)

    if ringed:
        ring = ring_of(n_dp)
        forward = [(ring[i], ring[(i + 1) % n_dp]) for i in range(n_dp)]
        backward = [(b, a) for a, b in forward]
        place = jnp.argsort(jnp.array(ring)).astype(jnp.int32)[group]
        blocks = jnp.array(ring, jnp.int32)[(place + eight) % n_dp]
        base = jnp.stack([3 * core, 3 - 3 * core])
        cuts = jnp.stack([base, base + 1 + side, base + 2 - side], 1).astype(jnp.int32)
        info = jnp.concatenate([first_info, slots_info, eight, cuts.reshape(-1), jnp.zeros(10, jnp.int32), blocks])
        shared, on_left, on_right = CUT + 8, CUT + 9, CUT + 10
        pieces, vec_pieces, sources = [], [], []

        def ahead(value):
            return lax.ppermute(value, "dp", forward)

        def behind(value):
            return lax.ppermute(value, "dp", backward)

        def across(value):
            return seq_flip(value, 1, n_seq)

        def trade(value):
            return seq_flip(value, 2, n_seq)

        def note(swapped, number, left, right):
            for value, far, kinds in (
                (left, n_dp - number, (shared, on_left)),
                (right, number, (on_right, shared)),
            ):
                if not swapped:
                    vec_pieces.append((len(sources), kinds.index(shared), ROWS, BLOCK + far))
                pieces.extend((len(sources), i, kind + 3 * swapped, BLOCK + far) for i, kind in enumerate(kinds))
                sources.append(value)

        def note_trade(swapped, number, value):
            for i, (far, kind) in enumerate(((n_dp - number, on_right), (number, on_left))):
                pieces.append((len(sources), i, kind + 3 * swapped, BLOCK + far))
            sources.append(value)

        def in_turn(left, right, traded):
            left, traded = tick(across(left), traded)
            return left, across(right), across(traded)

        def for_trade(left, right):
            return jnp.stack([left[1], right[0]])

        order = jnp.stack([cuts[0, 0], cuts[0, 1], cuts[0, 2], cuts[0, 0]])
        slabs, left0, right0 = pack(order, square, joint, expand, reduce, vectors)
        pieces.extend((0, cut, CUT + cut, BLOCK) for cut in range(CUTS))
        vec_pieces.append((1, 0, ROWS, BLOCK))
        sources.extend((slabs, left0))
        parcels = list(make_parcels(slots, pixels, block_mask, targets))
        left1, right1, *parcels[1:] = tick(
            ahead(left0),
            behind(right0),
            *(seq_flip(parcels[k], k, n_seq) for k in range(1, n_seq)),
        )
        note(0, 1, left1, right1)
        pos = positions(jnp.arange(n_seq * length).astype(f32), features)
        left2, right2, trade1, left1, right1, pos = tick(
            ahead(left1),
            behind(right1),
            trade(for_trade(left1, right1)),
            across(left1),
            across(right1),
            pos,
        )
        note(1, 1, left1, right1)
        note(0, 2, left2, right2)
        note_trade(0, 1, trade1)
        left3, right3, trade2, left2, right2, trade1 = tick(
            ahead(left2), behind(right2), trade(for_trade(left2, right2)), *in_turn(left2, right2, trade1)
        )
        note(1, 2, left2, right2)
        note(0, 3, left3, right3)
        note_trade(1, 1, trade1)
        note_trade(0, 2, trade2)
        left4, right4, trade3, left3, right3, trade2, info = tick(
            ahead(left3),
            behind(right3[:1]),
            trade(for_trade(left3, right3)),
            *in_turn(left3, right3, trade2),
            info,
        )
        note(1, 3, left3, right3)
        note_trade(1, 2, trade2)
        note_trade(0, 3, trade3)
        far = BLOCK + n_dp // 2
        vec_pieces.append((len(sources), 0, ROWS, far))
        for swapped, values in enumerate(((left4, right4), (across(left4), across(right4)))):
            for number, (value, kinds) in enumerate(zip(values, ((shared, on_left), (on_right,)))):
                pieces.extend((len(sources) + number, i, kind + 3 * swapped, far) for i, kind in enumerate(kinds))
            sources.extend(values)
        note_trade(1, 3, across(trade3))
    else:
        parcels = make_parcels(slots, pixels, block_mask, targets)
        parcels = [parcels[0]] + [seq_flip(parcels[k], k, n_seq) for k in range(1, n_seq)]
        pos = positions(jnp.arange(n_seq * length).astype(f32), features)
        gathered = [
            lax.all_gather(value.astype(bf16), "dp", axis=axis, tiled=True)
            for value, axis in zip(masters, (1, 0, 0, 0, 1))
        ]
        def cut_up(matrix):
            rows, columns = matrix.shape
            blocks = columns // (CUTS * LANES)
            shaped = matrix.reshape(BLOCKS, rows // BLOCKS, CUTS, blocks, LANES)
            return shaped.transpose(2, 0, 3, 1, 4).reshape(CUTS, BLOCKS, -1, LANES)

        order = (gathered[0][0], gathered[1], gathered[0][1], gathered[2], gathered[3], gathered[0][2])
        slabs = jnp.concatenate([cut_up(matrix) for matrix in order], 2)
        vec_slabs = gathered[4].reshape(vectors.shape[0], BLOCKS, features // BLOCKS).transpose(1, 0, 2)
        vec_slabs = jnp.pad(vec_slabs, ((0, 0), (0, VEC_ROWS - vectors.shape[0]), (0, LANES - features // BLOCKS)))
        sources = [slabs.reshape(CUTS * BLOCKS, ROWS, LANES), vec_slabs]
        pieces = [(0, BLOCKS * cut + q, CUT + cut, BLOCK + q) for cut in range(CUTS) for q in range(BLOCKS)]
        vec_pieces = [(1, q, 0, BLOCK + q) for q in range(BLOCKS)]
        info = jnp.concatenate([first_info, slots_info, eight, jnp.zeros(16, jnp.int32), eight])

    outs, vgrad = run_step(info, pos, tuple(parcels), tuple(pieces), tuple(vec_pieces), tuple(sources))
    rows = vectors.shape[0]
    n_whole = 2 * len(PLACES)
    keeps, sends = outs[0:n_whole:2], outs[1:n_whole:2]
    split_keeps, split_sends = outs[n_whole::2], outs[n_whole + 1 :: 2]

    def join_halves(low, high):
        cut = ROW_ONE // 2
        return jnp.concatenate([low[..., :cut, :], high[..., :cut, :], low[..., cut:, :], high[..., cut:, :]], -2)

    if ringed:
        def rounded(*values):
            return sum(value.astype(f32) for value in values).astype(bf16)

        def low_half(value):
            return jnp.pad(value.astype(f32), ((0, 1), (0, 0), (0, 0)))

        def high_half(value):
            return jnp.pad(value.astype(f32), ((1, 0), (0, 0), (0, 0)))

        small = vgrad.reshape(-1, n_dp, features // n_dp).transpose(1, 0, 2)
        opposite, split_first, next_got, small, small_more, send_rest, split_send_rest = tick(
            rounded(keeps[0], across(sends[0])),
            rounded(split_keeps[0], across(split_sends[0])),
            across(sends[1]),
            small,
            across(small),
            sends[2],
            split_sends[1],
        )
        small = small + small_more
        whole, split = {}, dict(zip((4, 3, 5), split_first[:, 0]))
        left, right, pair_first, whole_next, got_rest, split_rest = tick(
            ahead(opposite[0, :1]),
            behind(opposite[0, 1:]),
            trade(split_first[:, 1]),
            rounded(keeps[1], next_got),
            across(send_rest),
            rounded(split_keeps[1], across(split_send_rest)),
        )
        whole.update(zip((3, 5), whole_next))
        split.update(zip((2, 6, 1, 7, 0), split_rest[:, 0]))
        pair = dict(zip((4, 3, 5), pair_first))
        left, right, split_left, pair_rest, whole_rest, small, small_more = tick(
            ahead(rounded(whole[3], low_half(left))),
            behind(rounded(whole[5], high_half(right))),
            ahead(rounded(split[4], pair[4])),
            trade(split_rest[:, 1]),
            rounded(keeps[2], got_rest),
            small,
            trade(small),
        )
        pair.update(zip((2, 6, 1, 7, 0), pair_rest))
        whole.update(zip((2, 6, 1, 7, 0), whole_rest))
        small = small + small_more
        left, right, split_left, split_right, small, small_more = tick(
            ahead(rounded(whole[2], left)),
            behind(rounded(whole[6], right)),
            ahead(rounded(split[3], pair[3], split_left)),
            behind(rounded(split[5], pair[5])),
            small,
            hop(small, 1, 0, n_dp, n_seq),
        )
        small = small + small_more
        left, right, split_left, split_right, small, small_more = tick(
            ahead(rounded(whole[1], left)),
            behind(rounded(whole[7], right)),
            ahead(rounded(split[2], pair[2], split_left)),
            behind(rounded(split[6], pair[6], split_right)),
            small,
            hop(small, 2, 0, n_dp, n_seq),
        )
        small = small + small_more
        own = rounded(whole[0], left, right)
        own, other_chip, split_left, split_right, small, small_more = tick(
            own,
            trade(own),
            ahead(rounded(split[1], pair[1], split_left)),
            behind(rounded(split[7], pair[7], split_right)),
            small,
            hop(small, 4, 0, n_dp, n_seq),
        )
        small = lax.dynamic_index_in_dim(small + small_more, group, 0, keepdims=False)
        split_own, own, other_chip, small = tick(
            rounded(split[0], pair[0], split_left, split_right), own, other_chip, small
        )
        own = rounded(own, other_chip)
        squares = jnp.sum(jnp.square(own.astype(f32))) + 0.5 * jnp.sum(small[:rows] ** 2)
        own, split_own, pair_own, other, squares = tick(own, split_own, trade(split_own), across(own), squares)
        split_own = join_halves(
            jnp.where(side == 0, split_own, pair_own), jnp.where(side == 0, pair_own, split_own)
        )
        split_other = across(split_own)
        squares = jnp.full((1, LANES), squares + jnp.sum(jnp.square(split_own.astype(f32))))
        for hops in (((0, 0), (0, 1), (1, 0), (1, 1)), ((0, 0), (2, 0), (4, 0), (6, 0))):
            squares = tree_sum([squares] + [hop(squares, *ks, n_dp, n_seq) for ks in hops[1:]])
    else:
        def by_place(groups, values):
            spread = dict(zip((r for places in groups for r in places), jnp.concatenate(values)))
            return jnp.stack([spread[r] for r in range(BLOCKS)])

        def three(whole, split):
            split = by_place(SPLIT_PLACES, split)
            return jnp.concatenate([by_place(PLACES, whole), join_halves(split[:, 0], split[:, 1])[:, None]], 1)

        canonical = jnp.concatenate([three(keeps, split_keeps), three(sends, split_sends)], 1).transpose(1, 0, 2, 3)

        def join(row, end, blocks):
            part = canonical[:, :, row:end].astype(f32).reshape(CUTS, BLOCKS, blocks, -1, LANES)
            return part.transpose(1, 3, 0, 2, 4).reshape(-1, CUTS * blocks * LANES)

        whole = (
            jnp.stack([join(ROW_P, ROW_QKV, 1), join(ROW_O, ROW_ONE, 1), join(ROW_H, ROWS, 1)]),
            join(ROW_QKV, ROW_O, 3),
            join(ROW_ONE, ROW_TWO, 4),
            join(ROW_TWO, ROW_H, 1),
            vgrad[:rows],
        )
        grads = [
            lax.psum_scatter(grad, "dp", scatter_dimension=axis, tiled=True)
            for grad, axis in zip(whole, (1, 0, 0, 0, 1))
        ]
        grads = lax.psum(grads, "seq")
        vector_grad = grads[4]
        squares = lax.psum(sum(jnp.sum(grad * grad) for grad in grads), "dp")
        loss_sum, count = lax.psum((vgrad[rows, 0], vgrad[rows + 1, 0]), ("dp", "seq"))

    if ringed:
        shared_grads = (own, split_own, other, split_other)
        loss, norm, *new = adam_all(core.reshape(1), squares, small, shared_grads, masters, moments, variances)
    else:
        loss, norm = loss_sum / count, jnp.sqrt(squares) / count
        factor = clip_limit / jnp.maximum(norm, clip_limit) / count
        rates = ((matrix_rate, weight_decay),) * 4 + ((vector_rate, 0.0),)
        updated = [
            adam(master, moment, variance, grad * factor, *rate)
            for master, moment, variance, grad, rate in zip(masters, moments, variances, grads, rates)
        ]
        new = tuple(zip(*updated))
    return (loss, norm, *(new[k][kind] for kind in range(5) for k in range(3)))


def solution(mesh):
    matrix = P("dp", None)
    state = (P(None, "dp", None), matrix, matrix, matrix, P(None, "dp"))
    in_specs = (P("dp", "seq", None), P("dp", "seq"), P("dp", "seq", None)) + state * 3
    out_specs = (P(), P()) + tuple(spec for spec in state for _ in range(3))
    return jax.shard_map(
        partial(local, mesh.shape["dp"], mesh.shape["seq"]),
        mesh=mesh,
        in_specs=in_specs,
        out_specs=out_specs,
        check_vma=False,
    )
```

```python
from functools import partial
import math

import jax
import jax.numpy as jnp
from jax import lax
from jax.experimental import pallas as pl
from jax.experimental.pallas import tpu as pltpu
from jax.sharding import PartitionSpec as P

HEADS = 12
GRID = 14
LANES = 128
BLOCKS = 8
CUTS = 6

norm_eps = 1e-06
beta_one = 0.9
beta_two = 0.999
adam_eps = 1e-08
adam_step = 10.0
matrix_rate = 0.05
vector_rate = 0.3
weight_decay = 0.05
clip_limit = 0.1

f32 = jnp.float32
bf16 = jnp.bfloat16

ROW_P, ROW_QKV, ROW_O, ROW_ONE, ROW_TWO, ROW_H, ROWS = 0, 96, 384, 480, 864, 1248, 1344
VEC_ROWS = 32
PLACES = ((4,), (3, 5), (2, 6, 1, 7, 0))
SPLIT_PLACES = ((4, 3, 5), (2, 6, 1, 7, 0))
OUTS = 2 * len(PLACES) + 2 * len(SPLIT_PLACES)
PART, CUT, BLOCK = 8, 24, 48


def nn(left, right):
    return jnp.dot(left, right, preferred_element_type=f32)


def nt(left, right):
    return lax.dot_general(left, right, (((1,), (1,)), ((), ())), preferred_element_type=f32)


def tn(left, right):
    return lax.dot_general(left, right, (((0,), (0,)), ((), ())), preferred_element_type=f32)


def stats(stream):
    centred = stream - jnp.mean(stream, -1, keepdims=True)
    inverse = lax.rsqrt(jnp.mean(centred * centred, -1, keepdims=True) + norm_eps)
    return (centred * inverse, inverse)


def norm_back(upstream, normed, inverse, gain):
    scaled = upstream * gain
    return inverse * (
        scaled
        - jnp.mean(scaled, -1, keepdims=True)
        - normed * jnp.mean(scaled * normed, -1, keepdims=True)
    )


def column_sum(value):
    return jnp.sum(value, 0, keepdims=True)


def step_kernel(pieces, vec_pieces, n_refs, *refs):
    info, pos = refs[:2]
    n_parts = n_refs[0]
    parcels, sources = refs[2 : 2 + n_parts], refs[2 + n_parts : 2 + sum(n_refs)]
    *outs, vgrad = refs[2 + sum(n_refs) : 3 + sum(n_refs) + OUTS]
    w, vec_blocks, vec, pix, target, mask_rows, mask, bias, *refs = refs[3 + sum(n_refs) + OUTS :]
    (x0, x1, x2, branch, mlp, work, qkv, probs, inverses, attn, slope, act, hid, low, *sems) = refs
    sem_in, sem_part, sem_out = sems
    length, width = pix.shape
    part = length // n_parts
    pairs = width // 256
    first, second = (0, ROW_ONE), (ROW_ONE, ROWS)

    for k in range(n_parts):
        slot = info[PART + k]
        here = pl.ds(pl.multiple_of(slot * part, part), part)
        pltpu.make_async_copy(parcels[k].at[:part], pix.at[here], sem_part.at[0]).start()
        pltpu.make_async_copy(parcels[k].at[part : 2 * part], target.at[here], sem_part.at[1]).start()
        pltpu.make_async_copy(parcels[k].at[2 * part :, :LANES], mask_rows.at[slot], sem_part.at[2]).start()

    for source, lead, row, block_slot in vec_pieces:
        pltpu.make_async_copy(
            sources[source].at[lead, row : row + VEC_ROWS], vec_blocks.at[info[block_slot]], sem_part.at[3]
        ).start()

    for group, (begin, end) in enumerate((first, second)):
        for source, lead, cut_slot, block_slot in pieces:
            pltpu.make_async_copy(
                sources[source].at[lead, begin:end],
                w.at[info[cut_slot], info[block_slot], begin:end],
                sem_in.at[group],
            ).start()

    for number, whole in enumerate((pix, target, mask_rows, vec_blocks)):
        pltpu.make_async_copy(whole, whole, sem_part.at[number]).wait()
    diagonal = lax.broadcasted_iota(jnp.int32, (part, LANES), 0) == lax.broadcasted_iota(
        jnp.int32, (part, LANES), 1
    )
    for k in range(n_parts):
        row = mask_rows[k].astype(f32)[:1]
        mask[part * k : part * k + part, :] = jnp.sum(jnp.where(diagonal, row, 0.0), 1, keepdims=True)
    for q in range(BLOCKS):
        vec[:, 96 * q : 96 * q + 96] = vec_blocks[q].astype(f32)[:, :96]
    for k in range(4):
        bias[:, width * k : width * k + width] = vec[16 + k : 17 + k, :]

    def arrived(group, begin, end):
        part = w.at[:, :, begin:end]
        pltpu.make_async_copy(part, part, sem_in.at[group]).wait()

    def block(cut, row, rows):
        return w[cut, :, row : row + rows, :].reshape(BLOCKS * rows, LANES)

    def pair(i, row, rows=96):
        return jnp.concatenate([block(2 * i, row, rows), block(2 * i + 1, row, rows)], 1)

    def cols(i, size=256):
        return pl.ds(pl.multiple_of(i * size, size), size)

    def all_cuts(row):
        return jnp.concatenate([block(cut, row, 96) for cut in range(CUTS)], 1)

    def put(cut, row, rows, value):
        w[cut, :, row : row + rows, :] = value.astype(bf16).reshape(BLOCKS, rows, LANES)

    def put_pair(i, row, value):
        put(2 * i, row, 96, value[:, :LANES])
        put(2 * i + 1, row, 96, value[:, LANES:])

    def out_rows(number, begin, end):
        return (begin, end) if number < 2 * len(PLACES) else (begin // 2, end // 2)

    def leave(group, begin, end):
        core, side = info[0], info[1]
        half = (end - begin) // 2
        for number, out in enumerate(outs):
            split, away = number >= 2 * len(PLACES), number % 2
            first_cut = 3 * (core ^ away)
            lo, hi = out_rows(number, begin, end)
            for i, place in enumerate((PLACES + SPLIT_PLACES)[number // 2]):
                block_index = info[BLOCK + place]
                if not split:
                    pltpu.make_async_copy(
                        w.at[pl.ds(first_cut, 2), block_index, begin:end],
                        out.at[i, :, lo:hi],
                        sem_out.at[number, group],
                    ).start()
                    continue
                for part in range(2):
                    rows = pl.ds(pl.multiple_of(begin + half * (side ^ part), 16), half)
                    pltpu.make_async_copy(
                        w.at[first_cut + 2, block_index, rows], out.at[i, part, lo:hi], sem_out.at[number, group]
                    ).start()

    row_index = lax.broadcasted_iota(jnp.int32, (length, 1), 0)
    is_class = row_index == GRID * GRID
    key_valid = lax.broadcasted_iota(jnp.int32, (1, length), 1) <= GRID * GRID
    lower_half = lax.broadcasted_iota(jnp.int32, (1, LANES), 1) < LANES // 2
    masked = mask[...] > 0.5

    arrived(0, *first)

    @pl.loop(0, pairs)
    def _(i):
        c = cols(i)
        embedded = nn(pix[...], pair(i, ROW_P)) + vec[2:3, c]
        value = jnp.where(is_class, vec[0:1, c], jnp.where(masked, vec[1:2, c], embedded))
        x0[:, c] = value + pos[:, c]

    normed, _ = stats(x0[...])
    low[...] = (normed * vec[3:4, :] + vec[4:5, :]).astype(bf16)

    @pl.loop(0, pairs)
    def _(i):
        parts = [
            w[2 * i + j // 3, :, ROW_QKV + 96 * (j % 3) : ROW_QKV + 96 * (j % 3) + 96, :].reshape(width, LANES)
            for j in range(6)
        ]
        shift = jnp.where(i == 0, vec[5:6, :], jnp.where(i == 1, 0.0, vec[6:7, :]))
        for j in range(3):
            value = nn(low[...], jnp.concatenate(parts[2 * j : 2 * j + 2], 1)) + shift[:, 256 * j : 256 * j + 256]
            qkv[i, :, 256 * j : 256 * j + 256] = value.astype(bf16)

    def half_lanes(half):
        return lower_half if half == 0 else jnp.logical_not(lower_half)

    @pl.loop(0, HEADS // 2)
    def _(i):
        c = cols(i, LANES)
        query, key, value = qkv[0, :, c] * 0.125, qkv[1, :, c], qkv[2, :, c]
        outs = []
        for half in range(2):
            chosen = half_lanes(half)
            scores = nt(jnp.where(chosen, query, jnp.zeros_like(query)), key)
            scores = jnp.where(key_valid, scores, -1e30)
            weights = jnp.exp(scores - jnp.max(scores, -1, keepdims=True)).astype(bf16)
            probs[2 * i + half] = weights
            outs.append(nn(weights, jnp.where(chosen, value, jnp.ones_like(value))))
        total = pltpu.roll(jnp.where(lower_half, outs[1], outs[0]), LANES // 2, 1)
        inverse = 1.0 / total
        inverses[:, c] = inverse
        attn[:, c] = (jnp.where(lower_half, outs[0], outs[1]) * inverse).astype(bf16)

    @pl.loop(0, pairs)
    def _(i):
        c = cols(i)
        value = nn(attn[...], pair(i, ROW_O)) + vec[7:8, c]
        branch[:, c] = value
        x1[:, c] = x0[:, c] + vec[8:9, c] * value

    normed, _ = stats(x1[...])
    low[...] = (normed * vec[9:10, :] + vec[10:11, :]).astype(bf16)
    arrived(1, *second)

    @pl.loop(0, CUTS)
    def _(cut):
        for j in range(2):
            rhs = jnp.concatenate(
                [
                    w[cut, :, ROW_ONE + 96 * k : ROW_ONE + 96 * k + 96, :].reshape(width, LANES)
                    for k in (2 * j, 2 * j + 1)
                ],
                1,
            )
            c = cols(2 * cut + j)
            inner = nn(low[...], rhs) + bias[:, c]
            cdf = 0.5 + 0.5 * lax.erf(inner * math.sqrt(0.5))
            act[:, c] = (inner * cdf).astype(bf16)
            slope[:, c] = cdf + inner * (jnp.exp(-0.5 * inner * inner) * (1.0 / math.sqrt(2.0 * math.pi)))

    @pl.loop(0, pairs)
    def _(i):
        c = cols(i)
        value = nn(act[...], pair(i, ROW_TWO, 384)) + vec[11:12, c]
        mlp[:, c] = value
        x2[:, c] = x1[:, c] + vec[12:13, c] * value

    normed3, inverse3 = stats(x2[...])
    low[...] = (normed3 * vec[13:14, :] + vec[14:15, :]).astype(bf16)
    loss = work
    loss[0:1, 0:256] = jnp.zeros((1, 256), f32)

    @pl.loop(0, pairs)
    def _(i):
        c = cols(i)
        residual = nn(low[...], pair(i, ROW_H)) + vec[15:16, c] - target[:, c].astype(f32)
        size = jnp.abs(residual)
        terms = jnp.where(size < 2.0, 0.25 * residual * residual, size - 1.0)
        loss[0:1, 0:256] += column_sum(jnp.where(masked, terms, 0.0))
        grad = jnp.where(masked, jnp.clip(0.5 * residual, -1.0, 1.0), 0.0)
        vgrad[15:16, c] = column_sum(grad)
        hid[:, c] = grad.astype(bf16)

    vgrad[20:21, :] = jnp.broadcast_to(jnp.sum(loss[0:1, 0:256], 1, keepdims=True), (1, width))
    vgrad[21:22, :] = jnp.broadcast_to(jnp.sum(mask[...], 0, keepdims=True), (1, width))
    vgrad[22:24, :] = jnp.zeros((2, width), f32)
    upstream = nt(hid[...], all_cuts(ROW_H))
    vgrad[13:14, :] = column_sum(upstream * normed3)
    vgrad[14:15, :] = column_sum(upstream)
    grad2 = norm_back(upstream, normed3, inverse3, vec[13:14, :])
    x2[...] = grad2
    flipped = low[...].T

    @pl.loop(0, pairs)
    def _(i):
        put_pair(i, ROW_H, nn(flipped, hid[:, cols(i)]))

    vgrad[12:13, :] = column_sum(grad2 * mlp[...])
    grad_mlp = grad2 * vec[12:13, :]
    vgrad[11:12, :] = column_sum(grad_mlp)
    hid[...] = grad_mlp.astype(bf16)

    @pl.loop(0, BLOCKS)
    def _(q):
        c = cols(q, 384)
        rhs = jnp.concatenate([w[cut, q, ROW_TWO:ROW_H, :] for cut in range(CUTS)], 1)
        grad_inner = nt(hid[...], rhs) * slope[:, c]
        bias_grad = column_sum(grad_inner)
        slope[0:1, c] = bias_grad
        value = nn(act[:, c].T, hid[...]).astype(bf16)
        for cut in range(CUTS):
            w[cut, q, ROW_TWO:ROW_H, :] = value[:, LANES * cut : LANES * cut + LANES]
        act[:, c] = grad_inner.astype(bf16)

    for k in range(4):
        vgrad[16 + k : 17 + k, :] = slope[0:1, width * k : width * k + width]

    normed2, inverse2 = stats(x1[...])
    low[...] = (normed2 * vec[9:10, :] + vec[10:11, :]).astype(bf16)
    flipped = low[...].T
    work[...] = jnp.zeros_like(work)

    @pl.loop(0, CUTS)
    def _(cut):
        grad_inner = act[:, cols(cut, 512)]
        rhs = jnp.concatenate(
            [w[cut, :, ROW_ONE + 96 * k : ROW_ONE + 96 * k + 96, :].reshape(width, LANES) for k in range(4)], 1
        )
        work[...] += nt(grad_inner, rhs)
        for j in range(2):
            value = nn(flipped, grad_inner[:, 256 * j : 256 * j + 256])
            put(cut, ROW_ONE + 192 * j, 96, value[:, :LANES])
            put(cut, ROW_ONE + 192 * j + 96, 96, value[:, LANES:])

    leave(1, *second)

    upstream = work[...]
    vgrad[9:10, :] = column_sum(upstream * normed2)
    vgrad[10:11, :] = column_sum(upstream)
    grad1 = x2[...] + norm_back(upstream, normed2, inverse2, vec[9:10, :])
    x2[...] = grad1
    vgrad[8:9, :] = column_sum(grad1 * branch[...])
    grad_branch = grad1 * vec[8:9, :]
    vgrad[7:8, :] = column_sum(grad_branch)
    hid[...] = grad_branch.astype(bf16)
    low[...] = nt(hid[...], all_cuts(ROW_O)).astype(bf16)
    flipped = attn[...].T

    @pl.loop(0, pairs)
    def _(i):
        put_pair(i, ROW_O, nn(flipped, hid[:, cols(i)]))

    lane = lax.broadcasted_iota(jnp.int32, (1, LANES), 1)

    @pl.loop(0, HEADS // 2)
    def _(i):
        c = cols(i, LANES)
        query, key, value = qkv[0, :, c], qkv[1, :, c], qkv[2, :, c]
        out_grad, inverse = low[:, c].astype(f32), inverses[:, c]
        product = out_grad * attn[:, c].astype(f32)
        scaled_query = (query.astype(f32) * inverse).astype(bf16)
        scaled_grad = (out_grad * inverse).astype(bf16)
        outs = []
        for half in range(2):
            chosen = half_lanes(half)
            spare = LANES // 2 * (1 - half)
            sums = jnp.sum(jnp.where(chosen, product, 0.0), -1, keepdims=True)
            rough = sums.astype(bf16).astype(f32)
            fine = jnp.where(lane == spare, rough, jnp.where(lane == spare + 1, sums - rough, 0.0))
            left = jnp.where(chosen, out_grad, fine).astype(bf16)
            minus = jnp.where(jnp.logical_or(lane == spare, lane == spare + 1), -1.0, 0.0).astype(bf16)
            weights = probs[2 * i + half]
            ds = (weights.astype(f32) * nt(left, jnp.where(chosen, value, minus))).astype(bf16)
            outs.append((nn(ds, key), tn(ds, scaled_query), tn(weights, scaled_grad)))
        dq, dk, dv = (jnp.where(lower_half, one, two) for one, two in zip(*outs))
        dq, dk = (dq * inverse * 0.125, dk * 0.125)
        vgrad[5:6, c] = column_sum(dq)
        vgrad[6:7, c] = column_sum(dv)
        qkv[0, :, c], qkv[1, :, c], qkv[2, :, c] = (dq.astype(bf16), dk.astype(bf16), dv.astype(bf16))

    normed1, inverse1 = stats(x0[...])
    low[...] = (normed1 * vec[3:4, :] + vec[4:5, :]).astype(bf16)
    flipped = low[...].T
    work[...] = jnp.zeros_like(work)

    @pl.loop(0, pairs)
    def _(i):
        parts = [
            w[2 * i + j // 3, :, ROW_QKV + 96 * (j % 3) : ROW_QKV + 96 * (j % 3) + 96, :].reshape(width, LANES)
            for j in range(6)
        ]
        work[...] += nt(qkv[i], jnp.concatenate(parts, 1))
        for j in range(3):
            value = nn(flipped, qkv[i, :, 256 * j : 256 * j + 256]).astype(bf16)
            for half in range(2):
                k = 2 * j + half
                w[2 * i + k // 3, :, ROW_QKV + 96 * (k % 3) : ROW_QKV + 96 * (k % 3) + 96, :] = value[
                    :, LANES * half : LANES * half + LANES
                ].reshape(BLOCKS, 96, LANES)

    upstream = work[...]
    vgrad[3:4, :] = column_sum(upstream * normed1)
    vgrad[4:5, :] = column_sum(upstream)
    grad0 = x2[...] + norm_back(upstream, normed1, inverse1, vec[3:4, :])
    vgrad[0:1, :] = column_sum(jnp.where(is_class, grad0, 0.0))
    token = jnp.logical_and(masked, jnp.logical_not(is_class))
    vgrad[1:2, :] = column_sum(jnp.where(token, grad0, 0.0))
    grad_embed = jnp.where(jnp.logical_or(is_class, masked), 0.0, grad0)
    vgrad[2:3, :] = column_sum(grad_embed)
    hid[...] = grad_embed.astype(bf16)
    flipped = pix[...].T

    @pl.loop(0, pairs)
    def _(i):
        put_pair(i, ROW_P, nn(flipped, hid[:, cols(i)]))

    leave(0, *first)
    for number, out in enumerate(outs):
        for group, (begin, end) in enumerate((first, second)):
            lo, hi = out_rows(number, begin, end)
            rows = out.at[:, :, lo:hi]
            pltpu.make_async_copy(rows, rows, sem_out.at[number, group]).wait()


def run_step(info, pos, parcels, pieces, vec_pieces, sources):
    length, width = pos.shape
    hidden = 4 * width
    vmem = pl.BlockSpec(memory_space=pltpu.VMEM)
    anywhere = pl.BlockSpec(memory_space=pl.ANY)
    big = pltpu.VMEM((length, width), f32)
    small = pltpu.VMEM((length, width), bf16)
    *outs, vgrad = pl.pallas_call(
        partial(step_kernel, pieces, vec_pieces, (len(parcels), len(sources))),
        out_shape=(
            *(jax.ShapeDtypeStruct((len(places), 2, ROWS, LANES), bf16) for places in PLACES for _ in range(2)),
            *(
                jax.ShapeDtypeStruct((len(places), 2, ROWS // 2, LANES), bf16)
                for places in SPLIT_PLACES
                for _ in range(2)
            ),
            jax.ShapeDtypeStruct((24, width), f32),
        ),
        in_specs=[pl.BlockSpec(memory_space=pltpu.SMEM)] + [vmem] + [anywhere] * (len(parcels) + len(sources)),
        out_specs=(*[anywhere] * OUTS, vmem),
        scratch_shapes=[
            pltpu.VMEM((CUTS, BLOCKS, ROWS, LANES), bf16),
            pltpu.VMEM((BLOCKS, VEC_ROWS, LANES), bf16),
            pltpu.VMEM((VEC_ROWS, width), f32),
            small,
            small,
            pltpu.VMEM((len(parcels), 16, LANES), bf16),
            pltpu.VMEM((length, 1), f32),
            pltpu.VMEM((1, hidden), f32),
            big,
            big,
            big,
            big,
            big,
            big,
            pltpu.VMEM((3, length, width), bf16),
            pltpu.VMEM((HEADS, length, length), bf16),
            big,
            small,
            pltpu.VMEM((length, hidden), f32),
            pltpu.VMEM((length, hidden), bf16),
            small,
            small,
            pltpu.SemaphoreType.DMA((2,)),
            pltpu.SemaphoreType.DMA((4,)),
            pltpu.SemaphoreType.DMA((OUTS, 2)),
        ],
        compiler_params=pltpu.CompilerParams(vmem_limit_bytes=60 * 1024 * 1024),
        name="step",
    )(info, pos, *parcels, *sources)
    return outs, vgrad


def pack_kernel(chosen, square, joint, expand, reduce, vectors, out, *streams):
    for cut in range(CUTS):
        for row, n, rows, take in (
            (ROW_P, 1, 96, lambda c: square[0, :, c]),
            (ROW_QKV, 3, 96, lambda c: joint[:, c]),
            (ROW_O, 1, 96, lambda c: square[1, :, c]),
            (ROW_ONE, 4, 96, lambda c: expand[:, c]),
            (ROW_TWO, 1, 384, lambda c: reduce[:, c]),
            (ROW_H, 1, 96, lambda c: square[2, :, c]),
        ):
            for j in range(n):
                begin = LANES * (n * cut + j)
                out[cut, row + rows * j : row + rows * j + rows, :] = take(slice(begin, begin + LANES)).astype(bf16)
    for number, stream in enumerate(streams):
        for i in range(2):
            stream[i, :ROWS] = out[chosen[2 * number + i]]
            stream[i, ROWS:] = jnp.zeros((VEC_ROWS, LANES), bf16)
            stream[i, ROWS:, : vectors.shape[1]] = jnp.concatenate(
                [vectors[...], jnp.zeros((VEC_ROWS - vectors.shape[0], vectors.shape[1]), f32)]
            ).astype(bf16)


def pack(chosen, *shards):
    vmem = pl.BlockSpec(memory_space=pltpu.VMEM)
    return pl.pallas_call(
        pack_kernel,
        out_shape=[jax.ShapeDtypeStruct((CUTS, ROWS, LANES), bf16)]
        + [jax.ShapeDtypeStruct((2, ROWS + VEC_ROWS, LANES), bf16)] * 2,
        in_specs=[pl.BlockSpec(memory_space=pltpu.SMEM)] + [vmem] * 5,
        out_specs=[vmem] * 3,
        name="pack",
    )(chosen, *shards)


def parcel_kernel(slots, pixels, block_mask, targets, *outs):
    length = pixels.shape[1]
    top = lax.broadcasted_iota(jnp.int32, (16, length), 0) == 0
    for k, out in enumerate(outs):
        slot = slots[k]
        out[:length, :] = pixels[slot]
        out[length : 2 * length, :] = targets[slot]
        out[2 * length :, :] = jnp.zeros((16, out.shape[1]), bf16)
        row = block_mask[pl.ds(slot, 1), :].astype(f32)
        out[2 * length :, :length] = jnp.where(top, row, 0.0).astype(bf16)


def make_parcels(slots, pixels, block_mask, targets):
    images, length, features = pixels.shape
    vmem = pl.BlockSpec(memory_space=pltpu.VMEM)
    return pl.pallas_call(
        parcel_kernel,
        out_shape=[jax.ShapeDtypeStruct((2 * length + 16, features), bf16)] * images,
        in_specs=[pl.BlockSpec(memory_space=pltpu.SMEM)] + [vmem] * 3,
        out_specs=[vmem] * images,
        name="parcels",
    )(slots, pixels, block_mask, targets)


def adam(weight, moment, variance, grad, rate, decay):
    moment_new = beta_one * moment + (1.0 - beta_one) * grad
    variance_new = beta_two * variance + (1.0 - beta_two) * grad * grad
    corrected = (
        moment_new
        * (1.0 / (1.0 - beta_one**adam_step))
        / (jnp.sqrt(variance_new * (1.0 / (1.0 - beta_two**adam_step))) + adam_eps)
    )
    return (moment_new, variance_new, weight - rate * (corrected + decay * weight))


def adam_kernel(core, squares, table, own, split_own, other, split_other, *refs):
    masters, moments, variances = refs[:5], refs[5:10], refs[10:15]
    loss_out, norm_out, *outs = refs[15:32]
    buffers, grads, sem_in, sem_out = refs[32:44], *refs[44:]
    order = (3, 2, 1, 0)
    here, there = 3 * core[0], 3 - 3 * core[0]
    for value, place in (
        (own, pl.ds(here, 2)),
        (split_own, here + 2),
        (other, pl.ds(there, 2)),
        (split_other, there + 2),
    ):
        pltpu.make_async_copy(value, grads.at[place], sem_in.at[12]).start()
    for kind in order:
        for k, state in enumerate((masters, moments, variances)):
            pltpu.make_async_copy(state[kind], buffers[4 * k + kind], sem_in.at[4 * k + kind]).start()
    rows = masters[4].shape[0]
    count = table[rows + 1 : rows + 2, 0:1]
    norm = jnp.sqrt(squares[0:1, 0:1]) / count
    scale = clip_limit / jnp.maximum(norm, clip_limit) / count
    grad_scale = (1.0 - beta_one) * scale
    square_scale = (1.0 - beta_two) / (1.0 - beta_one) ** 2
    root_scale = (1.0 - beta_two**adam_step) ** -0.5
    step_scale = matrix_rate / (1.0 - beta_one**adam_step)
    keep_scale = 1.0 - matrix_rate * weight_decay
    loss_out[0, 0] = (table[rows : rows + 1, 0:1] / count)[0, 0]
    norm_out[0, 0] = norm[0, 0]

    pltpu.make_async_copy(grads, grads, sem_in.at[12]).wait()

    def update(kind, where, cut, row, rows):
        weight, moment, variance = (buffers[4 * k + kind][where] for k in range(3))
        part = grads[cut, row : row + rows, :].astype(f32) * grad_scale
        moment = beta_one * moment + part
        variance = beta_two * variance + (square_scale * part) * part
        divisor = (root_scale * variance) * lax.rsqrt(variance) + adam_eps
        step = (step_scale * moment) * lax.rsqrt(divisor * divisor)
        for k, value in enumerate((keep_scale * weight - step, moment, variance)):
            buffers[4 * k + kind][where] = value

    def each(kind, body):
        for k, state in enumerate((masters, moments, variances)):
            pltpu.make_async_copy(state[kind], buffers[4 * k + kind], sem_in.at[4 * k + kind]).wait()
        pl.loop(0, CUTS)(body)
        for k in range(3):
            out = outs[5 * ((k + 2) % 3) + kind]
            pltpu.make_async_copy(buffers[4 * k + kind], out, sem_out.at[4 * k + kind]).start()

    def lanes(block):
        return pl.ds(pl.multiple_of(block * LANES, LANES), LANES)

    def reduce_body(cut):
        for k in range(4):
            update(3, (slice(96 * k, 96 * k + 96), lanes(cut)), cut, ROW_TWO + 96 * k, 96)

    def expand_body(cut):
        for k in range(4):
            update(2, (slice(None), lanes(4 * cut + k)), cut, ROW_ONE + 96 * k, 96)

    def joint_body(cut):
        for k in range(3):
            update(1, (slice(None), lanes(3 * cut + k)), cut, ROW_QKV + 96 * k, 96)

    def square_body(cut):
        for i, row in enumerate((ROW_P, ROW_O, ROW_H)):
            update(0, (i, slice(None), lanes(cut)), cut, row, 96)

    for kind, body in zip(order, (reduce_body, expand_body, joint_body, square_body)):
        each(kind, body)
    states = (state[4][...] for state in (masters, moments, variances))
    for k, value in enumerate(adam(*states, table[:rows, :] * scale, vector_rate, 0.0)):
        outs[5 * k + 4][...] = value
    for k in range(3):
        for kind in range(4):
            out = outs[5 * ((k + 2) % 3) + kind]
            pltpu.make_async_copy(buffers[4 * k + kind], out, sem_out.at[4 * k + kind]).wait()


def adam_all(core, squares, table, grads, masters, moments, variances):
    smem = pl.BlockSpec(memory_space=pltpu.SMEM)
    vmem = pl.BlockSpec(memory_space=pltpu.VMEM)
    anywhere = pl.BlockSpec(memory_space=pl.ANY)
    shapes = [jax.ShapeDtypeStruct(master.shape, f32) for master in masters]
    loss, norm, *results = pl.pallas_call(
        adam_kernel,
        out_shape=[jax.ShapeDtypeStruct((1, 1), f32)] * 2 + shapes * 3,
        in_specs=[smem] + [vmem] * 2 + [anywhere] * len(grads) + ([anywhere] * 4 + [vmem]) * 3,
        out_specs=[smem] * 2 + ([anywhere] * 4 + [vmem]) * 3,
        scratch_shapes=[pltpu.VMEM(shape.shape, f32) for shape in shapes[:4] * 3]
        + [
            pltpu.VMEM((CUTS, ROWS, LANES), bf16),
            pltpu.SemaphoreType.DMA((13,)),
            pltpu.SemaphoreType.DMA((12,)),
        ],
        compiler_params=pltpu.CompilerParams(vmem_limit_bytes=56 * 1024 * 1024),
        name="adam",
    )(core, squares, table, *grads, *masters, *moments, *variances)
    return loss.reshape(()), norm.reshape(()), results[:5], results[5:10], results[10:]


def positions(slot_float, features):
    column = jnp.arange(features)
    frequency = jnp.exp((2 * (column // 2)).astype(f32) * (-math.log(10000.0) / features))
    angle = slot_float[:, None] * frequency[None, :]
    return jnp.where(column % 2 == 0, jnp.sin(angle), jnp.cos(angle))


def seq_flip(value, k, n_seq):
    return lax.ppermute(value, "seq", [(i, i ^ k) for i in range(n_seq)])


def hop(value, dp_k, seq_k, n_dp, n_seq):
    pairs = [(dp * n_seq + seq, (dp ^ dp_k) * n_seq + (seq ^ seq_k)) for dp in range(n_dp) for seq in range(n_seq)]
    return lax.ppermute(value, ("dp", "seq"), pairs)


def tick(*values):
    return lax.optimization_barrier(values)


def ring_of(n_dp):
    return list(range(0, n_dp, 2)) + list(range(n_dp - 1, 0, -2))


def tree_sum(values):
    while len(values) > 1:
        values = [left + right for left, right in zip(values[0::2], values[1::2])]
    return values[0]


def local(n_dp, n_seq, *args):
    pixels, block_mask, targets = args[:3]
    masters, moments, variances = args[3:8], args[8:13], args[13:18]
    length, features = pixels.shape[1:]
    square, joint, expand, reduce, vectors = masters
    me, group = lax.axis_index("seq"), lax.axis_index("dp")
    ringed = n_dp == BLOCKS and n_seq == 4
    core, side = (me % 2, me // 2) if ringed else (jnp.zeros((), jnp.int32),) * 2
    slots = me ^ jnp.arange(n_seq, dtype=jnp.int32)
    slots_info = jnp.concatenate([slots, jnp.zeros(16 - n_seq, jnp.int32)])
    eight = jnp.arange(8, dtype=jnp.int32)
    first_info = jnp.stack([core, side] + [core] * 6).astype(jnp.int32)

    if ringed:
        ring = ring_of(n_dp)
        forward = [(ring[i], ring[(i + 1) % n_dp]) for i in range(n_dp)]
        backward = [(b, a) for a, b in forward]
        place = jnp.argsort(jnp.array(ring)).astype(jnp.int32)[group]
        blocks = jnp.array(ring, jnp.int32)[(place + eight) % n_dp]
        base = jnp.stack([3 * core, 3 - 3 * core])
        cuts = jnp.stack([base, base + 1 + side, base + 2 - side], 1).astype(jnp.int32)
        info = jnp.concatenate([first_info, slots_info, eight, cuts.reshape(-1), jnp.zeros(10, jnp.int32), blocks])
        shared, on_left, on_right = CUT + 8, CUT + 9, CUT + 10
        pieces, vec_pieces, sources = [], [], []

        def ahead(value):
            return lax.ppermute(value, "dp", forward)

        def behind(value):
            return lax.ppermute(value, "dp", backward)

        def across(value):
            return seq_flip(value, 1, n_seq)

        def trade(value):
            return seq_flip(value, 2, n_seq)

        def note(swapped, number, left, right):
            for value, far, kinds in (
                (left, n_dp - number, (shared, on_left)),
                (right, number, (on_right, shared)),
            ):
                if not swapped:
                    vec_pieces.append((len(sources), kinds.index(shared), ROWS, BLOCK + far))
                pieces.extend((len(sources), i, kind + 3 * swapped, BLOCK + far) for i, kind in enumerate(kinds))
                sources.append(value)

        def note_trade(swapped, number, value):
            for i, (far, kind) in enumerate(((n_dp - number, on_right), (number, on_left))):
                pieces.append((len(sources), i, kind + 3 * swapped, BLOCK + far))
            sources.append(value)

        def in_turn(left, right, traded):
            left, traded = tick(across(left), traded)
            return left, across(right), across(traded)

        def for_trade(left, right):
            return jnp.stack([left[1], right[0]])

        order = jnp.stack([cuts[0, 0], cuts[0, 1], cuts[0, 2], cuts[0, 0]])
        slabs, left0, right0 = pack(order, square, joint, expand, reduce, vectors)
        pieces.extend((0, cut, CUT + cut, BLOCK) for cut in range(CUTS))
        vec_pieces.append((1, 0, ROWS, BLOCK))
        sources.extend((slabs, left0))
        parcels = list(make_parcels(slots, pixels, block_mask, targets))
        left1, right1, *parcels[1:] = tick(
            ahead(left0),
            behind(right0),
            *(seq_flip(parcels[k], k, n_seq) for k in range(1, n_seq)),
        )
        note(0, 1, left1, right1)
        pos = positions(jnp.arange(n_seq * length).astype(f32), features)
        left2, right2, trade1, left1, right1, pos = tick(
            ahead(left1),
            behind(right1),
            trade(for_trade(left1, right1)),
            across(left1),
            across(right1),
            pos,
        )
        note(1, 1, left1, right1)
        note(0, 2, left2, right2)
        note_trade(0, 1, trade1)
        left3, right3, trade2, left2, right2, trade1 = tick(
            ahead(left2), behind(right2), trade(for_trade(left2, right2)), *in_turn(left2, right2, trade1)
        )
        note(1, 2, left2, right2)
        note(0, 3, left3, right3)
        note_trade(1, 1, trade1)
        note_trade(0, 2, trade2)
        left4, right4, trade3, left3, right3, trade2, info = tick(
            ahead(left3),
            behind(right3[:1]),
            trade(for_trade(left3, right3)),
            *in_turn(left3, right3, trade2),
            info,
        )
        note(1, 3, left3, right3)
        note_trade(1, 2, trade2)
        note_trade(0, 3, trade3)
        far = BLOCK + n_dp // 2
        vec_pieces.append((len(sources), 0, ROWS, far))
        for swapped, values in enumerate(((left4, right4), (across(left4), across(right4)))):
            for number, (value, kinds) in enumerate(zip(values, ((shared, on_left), (on_right,)))):
                pieces.extend((len(sources) + number, i, kind + 3 * swapped, far) for i, kind in enumerate(kinds))
            sources.extend(values)
        note_trade(1, 3, across(trade3))
    else:
        parcels = make_parcels(slots, pixels, block_mask, targets)
        parcels = [parcels[0]] + [seq_flip(parcels[k], k, n_seq) for k in range(1, n_seq)]
        pos = positions(jnp.arange(n_seq * length).astype(f32), features)
        gathered = [
            lax.all_gather(value.astype(bf16), "dp", axis=axis, tiled=True)
            for value, axis in zip(masters, (1, 0, 0, 0, 1))
        ]
        def cut_up(matrix):
            rows, columns = matrix.shape
            blocks = columns // (CUTS * LANES)
            shaped = matrix.reshape(BLOCKS, rows // BLOCKS, CUTS, blocks, LANES)
            return shaped.transpose(2, 0, 3, 1, 4).reshape(CUTS, BLOCKS, -1, LANES)

        order = (gathered[0][0], gathered[1], gathered[0][1], gathered[2], gathered[3], gathered[0][2])
        slabs = jnp.concatenate([cut_up(matrix) for matrix in order], 2)
        vec_slabs = gathered[4].reshape(vectors.shape[0], BLOCKS, features // BLOCKS).transpose(1, 0, 2)
        vec_slabs = jnp.pad(vec_slabs, ((0, 0), (0, VEC_ROWS - vectors.shape[0]), (0, LANES - features // BLOCKS)))
        sources = [slabs.reshape(CUTS * BLOCKS, ROWS, LANES), vec_slabs]
        pieces = [(0, BLOCKS * cut + q, CUT + cut, BLOCK + q) for cut in range(CUTS) for q in range(BLOCKS)]
        vec_pieces = [(1, q, 0, BLOCK + q) for q in range(BLOCKS)]
        info = jnp.concatenate([first_info, slots_info, eight, jnp.zeros(16, jnp.int32), eight])

    outs, vgrad = run_step(info, pos, tuple(parcels), tuple(pieces), tuple(vec_pieces), tuple(sources))
    rows = vectors.shape[0]
    n_whole = 2 * len(PLACES)
    keeps, sends = outs[0:n_whole:2], outs[1:n_whole:2]
    split_keeps, split_sends = outs[n_whole::2], outs[n_whole + 1 :: 2]

    def join_halves(low, high):
        cut = ROW_ONE // 2
        return jnp.concatenate([low[..., :cut, :], high[..., :cut, :], low[..., cut:, :], high[..., cut:, :]], -2)

    if ringed:
        def rounded(*values):
            return sum(value.astype(f32) for value in values).astype(bf16)

        half = ROWS // 4

        def low_half(value):
            return jnp.pad(value.astype(f32), ((0, 1), (0, 0), (0, 0)))

        def high_half(value):
            return jnp.pad(value.astype(f32), ((1, 0), (0, 0), (0, 0)))

        small = vgrad.reshape(-1, n_dp, features // n_dp).transpose(1, 0, 2)
        opposite, split_first, next_got, small, small_more, send_rest, split_send_rest = tick(
            rounded(keeps[0], across(sends[0])),
            rounded(split_keeps[0], across(split_sends[0])),
            across(sends[1]),
            small,
            across(small),
            sends[2],
            split_sends[1],
        )
        small = small + small_more
        whole, split = {}, dict(zip((4, 3, 5), split_first[:, 0]))
        left, right, pair_first, whole_next, got_rest, split_rest, small = tick(
            ahead(opposite[0, :1]),
            behind(opposite[0, 1:]),
            trade(split_first[:, 1]),
            rounded(keeps[1], next_got),
            across(send_rest),
            rounded(split_keeps[1], across(split_send_rest)),
            small,
        )
        whole.update(zip((3, 5), whole_next))
        split.update(zip((2, 6, 1, 7, 0), split_rest[:, 0]))
        pair = dict(zip((4, 3, 5), pair_first))
        pair_next, small = tick(trade(split_rest[:2, 1]), small)
        left, right, split_left, split_right, pair_next, whole_rest, split_rest, small, small_more = tick(
            ahead(rounded(whole[3], low_half(left))),
            behind(rounded(whole[5], high_half(right))),
            ahead(rounded(split[4][:half], pair[4][:half])),
            behind(rounded(split[4][half:], pair[4][half:])),
            pair_next,
            rounded(keeps[2], got_rest),
            split_rest,
            small,
            trade(small),
        )
        pair.update(zip((2, 6), pair_next))
        whole.update(zip((2, 6, 1, 7, 0), whole_rest))
        small = jnp.take(small + small_more, group ^ jnp.array([0, 4, 2, 6, 1, 5, 3, 7]), axis=0)
        pair_rest, small = tick(trade(split_rest[2:, 1]), small)
        left, right, split_left, split_right, pair_rest, small, small_more = tick(
            ahead(rounded(whole[2], left)),
            behind(rounded(whole[6], right)),
            ahead(rounded(split[3], pair[3], jnp.pad(split_left.astype(f32), ((0, half), (0, 0))))),
            behind(rounded(split[5], pair[5], jnp.pad(split_right.astype(f32), ((half, 0), (0, 0))))),
            pair_rest,
            small[:4],
            hop(small[4:], 1, 0, n_dp, n_seq),
        )
        pair.update(zip((1, 7, 0), pair_rest))
        small = small + small_more
        left, right, split_left, split_right, small, small_more = tick(
            ahead(rounded(whole[1], left)),
            behind(rounded(whole[7], right)),
            ahead(rounded(split[2], pair[2], split_left)),
            behind(rounded(split[6], pair[6], split_right)),
            small[:2],
            hop(small[2:], 2, 0, n_dp, n_seq),
        )
        small = small + small_more
        own = rounded(whole[0], left, right)
        own, other_chip, split_left, split_right, small, small_more = tick(
            own,
            trade(own),
            ahead(rounded(split[1], pair[1], split_left)),
            behind(rounded(split[7], pair[7], split_right)),
            small[0],
            hop(small[1], 4, 0, n_dp, n_seq),
        )
        small = small + small_more
        split_own, own, other_chip, small = tick(
            rounded(split[0], pair[0], split_left, split_right), own, other_chip, small
        )
        own = rounded(own, other_chip)
        squares = jnp.sum(jnp.square(own.astype(f32))) + 0.5 * jnp.sum(small[:rows] ** 2)
        own, split_own, pair_own, other, squares = tick(own, split_own, trade(split_own), across(own), squares)
        split_own = join_halves(
            jnp.where(side == 0, split_own, pair_own), jnp.where(side == 0, pair_own, split_own)
        )
        split_other = across(split_own)
        squares = jnp.full((1, LANES), squares + jnp.sum(jnp.square(split_own.astype(f32))))
        for hops in (((0, 1), (1, 0), (1, 1)), ((2, 0), (4, 0), (6, 0))):
            squares = tree_sum([squares] + [hop(squares, *ks, n_dp, n_seq) for ks in hops])
    else:
        def by_place(groups, values):
            spread = dict(zip((r for places in groups for r in places), jnp.concatenate(values)))
            return jnp.stack([spread[r] for r in range(BLOCKS)])

        def three(whole, split):
            split = by_place(SPLIT_PLACES, split)
            return jnp.concatenate([by_place(PLACES, whole), join_halves(split[:, 0], split[:, 1])[:, None]], 1)

        canonical = jnp.concatenate([three(keeps, split_keeps), three(sends, split_sends)], 1).transpose(1, 0, 2, 3)

        def join(row, end, blocks):
            part = canonical[:, :, row:end].astype(f32).reshape(CUTS, BLOCKS, blocks, -1, LANES)
            return part.transpose(1, 3, 0, 2, 4).reshape(-1, CUTS * blocks * LANES)

        whole = (
            jnp.stack([join(ROW_P, ROW_QKV, 1), join(ROW_O, ROW_ONE, 1), join(ROW_H, ROWS, 1)]),
            join(ROW_QKV, ROW_O, 3),
            join(ROW_ONE, ROW_TWO, 4),
            join(ROW_TWO, ROW_H, 1),
            vgrad[:rows],
        )
        grads = [
            lax.psum_scatter(grad, "dp", scatter_dimension=axis, tiled=True)
            for grad, axis in zip(whole, (1, 0, 0, 0, 1))
        ]
        grads = lax.psum(grads, "seq")
        vector_grad = grads[4]
        squares = lax.psum(sum(jnp.sum(grad * grad) for grad in grads), "dp")
        loss_sum, count = lax.psum((vgrad[rows, 0], vgrad[rows + 1, 0]), ("dp", "seq"))

    if ringed:
        shared_grads = (own, split_own, other, split_other)
        loss, norm, *new = adam_all(core.reshape(1), squares, small, shared_grads, masters, moments, variances)
    else:
        loss, norm = loss_sum / count, jnp.sqrt(squares) / count
        factor = clip_limit / jnp.maximum(norm, clip_limit) / count
        rates = ((matrix_rate, weight_decay),) * 4 + ((vector_rate, 0.0),)
        updated = [
            adam(master, moment, variance, grad * factor, *rate)
            for master, moment, variance, grad, rate in zip(masters, moments, variances, grads, rates)
        ]
        new = tuple(zip(*updated))
    return (loss, norm, *(new[k][kind] for kind in range(5) for k in range(3)))


def solution(mesh):
    matrix = P("dp", None)
    state = (P(None, "dp", None), matrix, matrix, matrix, P(None, "dp"))
    in_specs = (P("dp", "seq", None), P("dp", "seq"), P("dp", "seq", None)) + state * 3
    out_specs = (P(), P()) + tuple(spec for spec in state for _ in range(3))
    return jax.shard_map(
        partial(local, mesh.shape["dp"], mesh.shape["seq"]),
        mesh=mesh,
        in_specs=in_specs,
        out_specs=out_specs,
        check_vma=False,
    )
```

```python
from functools import partial
import math

import jax
import jax.numpy as jnp
from jax import lax
from jax.experimental import pallas as pl
from jax.experimental.pallas import tpu as pltpu
from jax.sharding import PartitionSpec as P

HEADS = 12
GRID = 14
LANES = 128
BLOCKS = 8
CUTS = 6

norm_eps = 1e-06
beta_one = 0.9
beta_two = 0.999
adam_eps = 1e-08
adam_step = 10.0
matrix_rate = 0.05
vector_rate = 0.3
weight_decay = 0.05
clip_limit = 0.1

f32 = jnp.float32
bf16 = jnp.bfloat16

ROW_P, ROW_QKV, ROW_O, ROW_ONE, ROW_TWO, ROW_H, ROWS = 0, 96, 384, 480, 864, 1248, 1344
VEC_ROWS = 32
PLACES = ((4,), (3, 5), (2, 6, 1, 7, 0))
SPLIT_PLACES = ((4, 3), (5, 2, 6, 1, 7, 0))
OUTS = 2 * len(PLACES) + 2 * len(SPLIT_PLACES)
PART, CUT, BLOCK = 8, 24, 48


def nn(left, right):
    return jnp.dot(left, right, preferred_element_type=f32)


def nt(left, right):
    return lax.dot_general(left, right, (((1,), (1,)), ((), ())), preferred_element_type=f32)


def tn(left, right):
    return lax.dot_general(left, right, (((0,), (0,)), ((), ())), preferred_element_type=f32)


def stats(stream):
    centred = stream - jnp.mean(stream, -1, keepdims=True)
    inverse = lax.rsqrt(jnp.mean(centred * centred, -1, keepdims=True) + norm_eps)
    return (centred * inverse, inverse)


def norm_back(upstream, normed, inverse, gain):
    scaled = upstream * gain
    return inverse * (
        scaled
        - jnp.mean(scaled, -1, keepdims=True)
        - normed * jnp.mean(scaled * normed, -1, keepdims=True)
    )


def column_sum(value):
    return jnp.sum(value, 0, keepdims=True)


def step_kernel(pieces, vec_pieces, n_refs, *refs):
    info, pos = refs[:2]
    n_parts = n_refs[0]
    parcels, sources = refs[2 : 2 + n_parts], refs[2 + n_parts : 2 + sum(n_refs)]
    *outs, vgrad = refs[2 + sum(n_refs) : 3 + sum(n_refs) + OUTS]
    w, vec_blocks, vec, pix, target, mask_rows, mask, bias, *refs = refs[3 + sum(n_refs) + OUTS :]
    (x0, x1, x2, branch, mlp, work, qkv, probs, inverses, attn, slope, act, hid, low, *sems) = refs
    sem_in, sem_part, sem_out = sems
    length, width = pix.shape
    part = length // n_parts
    pairs = width // 256
    first, second = (0, ROW_ONE), (ROW_ONE, ROWS)

    for k in range(n_parts):
        slot = info[PART + k]
        here = pl.ds(pl.multiple_of(slot * part, part), part)
        pltpu.make_async_copy(parcels[k].at[:part], pix.at[here], sem_part.at[0]).start()
        pltpu.make_async_copy(parcels[k].at[part : 2 * part], target.at[here], sem_part.at[1]).start()
        pltpu.make_async_copy(parcels[k].at[2 * part :, :LANES], mask_rows.at[slot], sem_part.at[2]).start()

    for source, lead, row, block_slot in vec_pieces:
        pltpu.make_async_copy(
            sources[source].at[lead, row : row + VEC_ROWS], vec_blocks.at[info[block_slot]], sem_part.at[3]
        ).start()

    for group, (begin, end) in enumerate((first, second)):
        for source, lead, cut_slot, block_slot in pieces:
            pltpu.make_async_copy(
                sources[source].at[lead, begin:end],
                w.at[info[cut_slot], info[block_slot], begin:end],
                sem_in.at[group],
            ).start()

    for number, whole in enumerate((pix, target, mask_rows, vec_blocks)):
        pltpu.make_async_copy(whole, whole, sem_part.at[number]).wait()
    diagonal = lax.broadcasted_iota(jnp.int32, (part, LANES), 0) == lax.broadcasted_iota(
        jnp.int32, (part, LANES), 1
    )
    for k in range(n_parts):
        row = mask_rows[k].astype(f32)[:1]
        mask[part * k : part * k + part, :] = jnp.sum(jnp.where(diagonal, row, 0.0), 1, keepdims=True)
    for q in range(BLOCKS):
        vec[:, 96 * q : 96 * q + 96] = vec_blocks[q].astype(f32)[:, :96]
    for k in range(4):
        bias[:, width * k : width * k + width] = vec[16 + k : 17 + k, :]

    def arrived(group, begin, end):
        part = w.at[:, :, begin:end]
        pltpu.make_async_copy(part, part, sem_in.at[group]).wait()

    def block(cut, row, rows):
        return w[cut, :, row : row + rows, :].reshape(BLOCKS * rows, LANES)

    def pair(i, row, rows=96):
        return jnp.concatenate([block(2 * i, row, rows), block(2 * i + 1, row, rows)], 1)

    def cols(i, size=256):
        return pl.ds(pl.multiple_of(i * size, size), size)

    def all_cuts(row):
        return jnp.concatenate([block(cut, row, 96) for cut in range(CUTS)], 1)

    def put(cut, row, rows, value):
        w[cut, :, row : row + rows, :] = value.astype(bf16).reshape(BLOCKS, rows, LANES)

    def put_pair(i, row, value):
        put(2 * i, row, 96, value[:, :LANES])
        put(2 * i + 1, row, 96, value[:, LANES:])

    def out_rows(number, begin, end):
        return (begin, end) if number < 2 * len(PLACES) else (begin // 2, end // 2)

    def leave(group, begin, end):
        core, side = info[0], info[1]
        half = (end - begin) // 2
        for number, out in enumerate(outs):
            split, away = number >= 2 * len(PLACES), number % 2
            first_cut = 3 * (core ^ away)
            lo, hi = out_rows(number, begin, end)
            for i, place in enumerate((PLACES + SPLIT_PLACES)[number // 2]):
                block_index = info[BLOCK + place]
                if not split:
                    pltpu.make_async_copy(
                        w.at[pl.ds(first_cut, 2), block_index, begin:end],
                        out.at[i, :, lo:hi],
                        sem_out.at[number, group],
                    ).start()
                    continue
                for part in range(2):
                    rows = pl.ds(pl.multiple_of(begin + half * (side ^ part), 16), half)
                    pltpu.make_async_copy(
                        w.at[first_cut + 2, block_index, rows], out.at[i, part, lo:hi], sem_out.at[number, group]
                    ).start()

    row_index = lax.broadcasted_iota(jnp.int32, (length, 1), 0)
    is_class = row_index == GRID * GRID
    key_valid = lax.broadcasted_iota(jnp.int32, (1, length), 1) <= GRID * GRID
    lower_half = lax.broadcasted_iota(jnp.int32, (1, LANES), 1) < LANES // 2
    masked = mask[...] > 0.5

    arrived(0, *first)

    @pl.loop(0, pairs)
    def _(i):
        c = cols(i)
        embedded = nn(pix[...], pair(i, ROW_P)) + vec[2:3, c]
        value = jnp.where(is_class, vec[0:1, c], jnp.where(masked, vec[1:2, c], embedded))
        x0[:, c] = value + pos[:, c]

    normed, _ = stats(x0[...])
    low[...] = (normed * vec[3:4, :] + vec[4:5, :]).astype(bf16)

    @pl.loop(0, pairs)
    def _(i):
        parts = [
            w[2 * i + j // 3, :, ROW_QKV + 96 * (j % 3) : ROW_QKV + 96 * (j % 3) + 96, :].reshape(width, LANES)
            for j in range(6)
        ]
        shift = jnp.where(i == 0, vec[5:6, :], jnp.where(i == 1, 0.0, vec[6:7, :]))
        for j in range(3):
            value = nn(low[...], jnp.concatenate(parts[2 * j : 2 * j + 2], 1)) + shift[:, 256 * j : 256 * j + 256]
            qkv[i, :, 256 * j : 256 * j + 256] = value.astype(bf16)

    def half_lanes(half):
        return lower_half if half == 0 else jnp.logical_not(lower_half)

    @pl.loop(0, HEADS // 2)
    def _(i):
        c = cols(i, LANES)
        query, key, value = qkv[0, :, c] * 0.125, qkv[1, :, c], qkv[2, :, c]
        outs = []
        for half in range(2):
            chosen = half_lanes(half)
            scores = nt(jnp.where(chosen, query, jnp.zeros_like(query)), key)
            scores = jnp.where(key_valid, scores, -1e30)
            weights = jnp.exp(scores - jnp.max(scores, -1, keepdims=True)).astype(bf16)
            probs[2 * i + half] = weights
            outs.append(nn(weights, jnp.where(chosen, value, jnp.ones_like(value))))
        total = pltpu.roll(jnp.where(lower_half, outs[1], outs[0]), LANES // 2, 1)
        inverse = 1.0 / total
        inverses[:, c] = inverse
        attn[:, c] = (jnp.where(lower_half, outs[0], outs[1]) * inverse).astype(bf16)

    @pl.loop(0, pairs)
    def _(i):
        c = cols(i)
        value = nn(attn[...], pair(i, ROW_O)) + vec[7:8, c]
        branch[:, c] = value
        x1[:, c] = x0[:, c] + vec[8:9, c] * value

    normed, _ = stats(x1[...])
    low[...] = (normed * vec[9:10, :] + vec[10:11, :]).astype(bf16)
    arrived(1, *second)

    @pl.loop(0, CUTS)
    def _(cut):
        for j in range(2):
            rhs = jnp.concatenate(
                [
                    w[cut, :, ROW_ONE + 96 * k : ROW_ONE + 96 * k + 96, :].reshape(width, LANES)
                    for k in (2 * j, 2 * j + 1)
                ],
                1,
            )
            c = cols(2 * cut + j)
            inner = nn(low[...], rhs) + bias[:, c]
            cdf = 0.5 + 0.5 * lax.erf(inner * math.sqrt(0.5))
            act[:, c] = (inner * cdf).astype(bf16)
            slope[:, c] = cdf + inner * (jnp.exp(-0.5 * inner * inner) * (1.0 / math.sqrt(2.0 * math.pi)))

    @pl.loop(0, pairs)
    def _(i):
        c = cols(i)
        value = nn(act[...], pair(i, ROW_TWO, 384)) + vec[11:12, c]
        mlp[:, c] = value
        x2[:, c] = x1[:, c] + vec[12:13, c] * value

    normed3, inverse3 = stats(x2[...])
    low[...] = (normed3 * vec[13:14, :] + vec[14:15, :]).astype(bf16)
    loss = work
    loss[0:1, 0:256] = jnp.zeros((1, 256), f32)

    @pl.loop(0, pairs)
    def _(i):
        c = cols(i)
        residual = nn(low[...], pair(i, ROW_H)) + vec[15:16, c] - target[:, c].astype(f32)
        size = jnp.abs(residual)
        terms = jnp.where(size < 2.0, 0.25 * residual * residual, size - 1.0)
        loss[0:1, 0:256] += column_sum(jnp.where(masked, terms, 0.0))
        grad = jnp.where(masked, jnp.clip(0.5 * residual, -1.0, 1.0), 0.0)
        vgrad[15:16, c] = column_sum(grad)
        hid[:, c] = grad.astype(bf16)

    vgrad[20:21, :] = jnp.broadcast_to(jnp.sum(loss[0:1, 0:256], 1, keepdims=True), (1, width))
    vgrad[21:22, :] = jnp.broadcast_to(jnp.sum(mask[...], 0, keepdims=True), (1, width))
    vgrad[22:24, :] = jnp.zeros((2, width), f32)
    upstream = nt(hid[...], all_cuts(ROW_H))
    vgrad[13:14, :] = column_sum(upstream * normed3)
    vgrad[14:15, :] = column_sum(upstream)
    grad2 = norm_back(upstream, normed3, inverse3, vec[13:14, :])
    x2[...] = grad2
    flipped = low[...].T

    @pl.loop(0, pairs)
    def _(i):
        put_pair(i, ROW_H, nn(flipped, hid[:, cols(i)]))

    vgrad[12:13, :] = column_sum(grad2 * mlp[...])
    grad_mlp = grad2 * vec[12:13, :]
    vgrad[11:12, :] = column_sum(grad_mlp)
    hid[...] = grad_mlp.astype(bf16)

    @pl.loop(0, BLOCKS)
    def _(q):
        c = cols(q, 384)
        rhs = jnp.concatenate([w[cut, q, ROW_TWO:ROW_H, :] for cut in range(CUTS)], 1)
        grad_inner = nt(hid[...], rhs) * slope[:, c]
        bias_grad = column_sum(grad_inner)
        slope[0:1, c] = bias_grad
        value = nn(act[:, c].T, hid[...]).astype(bf16)
        for cut in range(CUTS):
            w[cut, q, ROW_TWO:ROW_H, :] = value[:, LANES * cut : LANES * cut + LANES]
        act[:, c] = grad_inner.astype(bf16)

    for k in range(4):
        vgrad[16 + k : 17 + k, :] = slope[0:1, width * k : width * k + width]

    normed2, inverse2 = stats(x1[...])
    low[...] = (normed2 * vec[9:10, :] + vec[10:11, :]).astype(bf16)
    flipped = low[...].T
    work[...] = jnp.zeros_like(work)

    @pl.loop(0, CUTS)
    def _(cut):
        grad_inner = act[:, cols(cut, 512)]
        rhs = jnp.concatenate(
            [w[cut, :, ROW_ONE + 96 * k : ROW_ONE + 96 * k + 96, :].reshape(width, LANES) for k in range(4)], 1
        )
        work[...] += nt(grad_inner, rhs)
        for j in range(2):
            value = nn(flipped, grad_inner[:, 256 * j : 256 * j + 256])
            put(cut, ROW_ONE + 192 * j, 96, value[:, :LANES])
            put(cut, ROW_ONE + 192 * j + 96, 96, value[:, LANES:])

    leave(1, *second)

    upstream = work[...]
    vgrad[9:10, :] = column_sum(upstream * normed2)
    vgrad[10:11, :] = column_sum(upstream)
    grad1 = x2[...] + norm_back(upstream, normed2, inverse2, vec[9:10, :])
    x2[...] = grad1
    vgrad[8:9, :] = column_sum(grad1 * branch[...])
    grad_branch = grad1 * vec[8:9, :]
    vgrad[7:8, :] = column_sum(grad_branch)
    hid[...] = grad_branch.astype(bf16)
    low[...] = nt(hid[...], all_cuts(ROW_O)).astype(bf16)
    flipped = attn[...].T

    @pl.loop(0, pairs)
    def _(i):
        put_pair(i, ROW_O, nn(flipped, hid[:, cols(i)]))

    lane = lax.broadcasted_iota(jnp.int32, (1, LANES), 1)

    @pl.loop(0, HEADS // 2)
    def _(i):
        c = cols(i, LANES)
        query, key, value = qkv[0, :, c], qkv[1, :, c], qkv[2, :, c]
        out_grad, inverse = low[:, c].astype(f32), inverses[:, c]
        product = out_grad * attn[:, c].astype(f32)
        scaled_query = (query.astype(f32) * inverse).astype(bf16)
        scaled_grad = (out_grad * inverse).astype(bf16)
        outs = []
        for half in range(2):
            chosen = half_lanes(half)
            spare = LANES // 2 * (1 - half)
            sums = jnp.sum(jnp.where(chosen, product, 0.0), -1, keepdims=True)
            rough = sums.astype(bf16).astype(f32)
            fine = jnp.where(lane == spare, rough, jnp.where(lane == spare + 1, sums - rough, 0.0))
            left = jnp.where(chosen, out_grad, fine).astype(bf16)
            minus = jnp.where(jnp.logical_or(lane == spare, lane == spare + 1), -1.0, 0.0).astype(bf16)
            weights = probs[2 * i + half]
            ds = (weights.astype(f32) * nt(left, jnp.where(chosen, value, minus))).astype(bf16)
            outs.append((nn(ds, key), tn(ds, scaled_query), tn(weights, scaled_grad)))
        dq, dk, dv = (jnp.where(lower_half, one, two) for one, two in zip(*outs))
        dq, dk = (dq * inverse * 0.125, dk * 0.125)
        vgrad[5:6, c] = column_sum(dq)
        vgrad[6:7, c] = column_sum(dv)
        qkv[0, :, c], qkv[1, :, c], qkv[2, :, c] = (dq.astype(bf16), dk.astype(bf16), dv.astype(bf16))

    normed1, inverse1 = stats(x0[...])
    low[...] = (normed1 * vec[3:4, :] + vec[4:5, :]).astype(bf16)
    flipped = low[...].T
    work[...] = jnp.zeros_like(work)

    @pl.loop(0, pairs)
    def _(i):
        parts = [
            w[2 * i + j // 3, :, ROW_QKV + 96 * (j % 3) : ROW_QKV + 96 * (j % 3) + 96, :].reshape(width, LANES)
            for j in range(6)
        ]
        work[...] += nt(qkv[i], jnp.concatenate(parts, 1))
        for j in range(3):
            value = nn(flipped, qkv[i, :, 256 * j : 256 * j + 256]).astype(bf16)
            for half in range(2):
                k = 2 * j + half
                w[2 * i + k // 3, :, ROW_QKV + 96 * (k % 3) : ROW_QKV + 96 * (k % 3) + 96, :] = value[
                    :, LANES * half : LANES * half + LANES
                ].reshape(BLOCKS, 96, LANES)

    upstream = work[...]
    vgrad[3:4, :] = column_sum(upstream * normed1)
    vgrad[4:5, :] = column_sum(upstream)
    grad0 = x2[...] + norm_back(upstream, normed1, inverse1, vec[3:4, :])
    vgrad[0:1, :] = column_sum(jnp.where(is_class, grad0, 0.0))
    token = jnp.logical_and(masked, jnp.logical_not(is_class))
    vgrad[1:2, :] = column_sum(jnp.where(token, grad0, 0.0))
    grad_embed = jnp.where(jnp.logical_or(is_class, masked), 0.0, grad0)
    vgrad[2:3, :] = column_sum(grad_embed)
    hid[...] = grad_embed.astype(bf16)
    flipped = pix[...].T

    @pl.loop(0, pairs)
    def _(i):
        put_pair(i, ROW_P, nn(flipped, hid[:, cols(i)]))

    leave(0, *first)
    for number, out in enumerate(outs):
        for group, (begin, end) in enumerate((first, second)):
            lo, hi = out_rows(number, begin, end)
            rows = out.at[:, :, lo:hi]
            pltpu.make_async_copy(rows, rows, sem_out.at[number, group]).wait()


def run_step(info, pos, parcels, pieces, vec_pieces, sources):
    length, width = pos.shape
    hidden = 4 * width
    vmem = pl.BlockSpec(memory_space=pltpu.VMEM)
    anywhere = pl.BlockSpec(memory_space=pl.ANY)
    big = pltpu.VMEM((length, width), f32)
    small = pltpu.VMEM((length, width), bf16)
    *outs, vgrad = pl.pallas_call(
        partial(step_kernel, pieces, vec_pieces, (len(parcels), len(sources))),
        out_shape=(
            *(jax.ShapeDtypeStruct((len(places), 2, ROWS, LANES), bf16) for places in PLACES for _ in range(2)),
            *(
                jax.ShapeDtypeStruct((len(places), 2, ROWS // 2, LANES), bf16)
                for places in SPLIT_PLACES
                for _ in range(2)
            ),
            jax.ShapeDtypeStruct((24, width), f32),
        ),
        in_specs=[pl.BlockSpec(memory_space=pltpu.SMEM)] + [vmem] + [anywhere] * (len(parcels) + len(sources)),
        out_specs=(*[anywhere] * OUTS, vmem),
        scratch_shapes=[
            pltpu.VMEM((CUTS, BLOCKS, ROWS, LANES), bf16),
            pltpu.VMEM((BLOCKS, VEC_ROWS, LANES), bf16),
            pltpu.VMEM((VEC_ROWS, width), f32),
            small,
            small,
            pltpu.VMEM((len(parcels), 16, LANES), bf16),
            pltpu.VMEM((length, 1), f32),
            pltpu.VMEM((1, hidden), f32),
            big,
            big,
            big,
            big,
            big,
            big,
            pltpu.VMEM((3, length, width), bf16),
            pltpu.VMEM((HEADS, length, length), bf16),
            big,
            small,
            pltpu.VMEM((length, hidden), f32),
            pltpu.VMEM((length, hidden), bf16),
            small,
            small,
            pltpu.SemaphoreType.DMA((2,)),
            pltpu.SemaphoreType.DMA((4,)),
            pltpu.SemaphoreType.DMA((OUTS, 2)),
        ],
        compiler_params=pltpu.CompilerParams(vmem_limit_bytes=60 * 1024 * 1024),
        name="step",
    )(info, pos, *parcels, *sources)
    return outs, vgrad


def pack_kernel(chosen, square, joint, expand, reduce, vectors, out, *streams):
    for cut in range(CUTS):
        for row, n, rows, take in (
            (ROW_P, 1, 96, lambda c: square[0, :, c]),
            (ROW_QKV, 3, 96, lambda c: joint[:, c]),
            (ROW_O, 1, 96, lambda c: square[1, :, c]),
            (ROW_ONE, 4, 96, lambda c: expand[:, c]),
            (ROW_TWO, 1, 384, lambda c: reduce[:, c]),
            (ROW_H, 1, 96, lambda c: square[2, :, c]),
        ):
            for j in range(n):
                begin = LANES * (n * cut + j)
                out[cut, row + rows * j : row + rows * j + rows, :] = take(slice(begin, begin + LANES)).astype(bf16)
    for number, stream in enumerate(streams):
        for i in range(2):
            stream[i, :ROWS] = out[chosen[2 * number + i]]
            stream[i, ROWS:] = jnp.zeros((VEC_ROWS, LANES), bf16)
            stream[i, ROWS:, : vectors.shape[1]] = jnp.concatenate(
                [vectors[...], jnp.zeros((VEC_ROWS - vectors.shape[0], vectors.shape[1]), f32)]
            ).astype(bf16)


def pack(chosen, *shards):
    vmem = pl.BlockSpec(memory_space=pltpu.VMEM)
    return pl.pallas_call(
        pack_kernel,
        out_shape=[jax.ShapeDtypeStruct((CUTS, ROWS, LANES), bf16)]
        + [jax.ShapeDtypeStruct((2, ROWS + VEC_ROWS, LANES), bf16)] * 2,
        in_specs=[pl.BlockSpec(memory_space=pltpu.SMEM)] + [vmem] * 5,
        out_specs=[vmem] * 3,
        name="pack",
    )(chosen, *shards)


def parcel_kernel(slots, pixels, block_mask, targets, *outs):
    length = pixels.shape[1]
    top = lax.broadcasted_iota(jnp.int32, (16, length), 0) == 0
    for k, out in enumerate(outs):
        slot = slots[k]
        out[:length, :] = pixels[slot]
        out[length : 2 * length, :] = targets[slot]
        out[2 * length :, :] = jnp.zeros((16, out.shape[1]), bf16)
        row = block_mask[pl.ds(slot, 1), :].astype(f32)
        out[2 * length :, :length] = jnp.where(top, row, 0.0).astype(bf16)


def make_parcels(slots, pixels, block_mask, targets):
    images, length, features = pixels.shape
    vmem = pl.BlockSpec(memory_space=pltpu.VMEM)
    return pl.pallas_call(
        parcel_kernel,
        out_shape=[jax.ShapeDtypeStruct((2 * length + 16, features), bf16)] * images,
        in_specs=[pl.BlockSpec(memory_space=pltpu.SMEM)] + [vmem] * 3,
        out_specs=[vmem] * images,
        name="parcels",
    )(slots, pixels, block_mask, targets)


def adam(weight, moment, variance, grad, rate, decay):
    moment_new = beta_one * moment + (1.0 - beta_one) * grad
    variance_new = beta_two * variance + (1.0 - beta_two) * grad * grad
    corrected = (
        moment_new
        * (1.0 / (1.0 - beta_one**adam_step))
        / (jnp.sqrt(variance_new * (1.0 / (1.0 - beta_two**adam_step))) + adam_eps)
    )
    return (moment_new, variance_new, weight - rate * (corrected + decay * weight))


def adam_kernel(core, squares, table, own, split_own, other, split_other, *refs):
    masters, moments, variances = refs[:5], refs[5:10], refs[10:15]
    loss_out, norm_out, *outs = refs[15:32]
    buffers, grads, sem_in, sem_out = refs[32:44], *refs[44:]
    order = (3, 2, 1, 0)
    here, there = 3 * core[0], 3 - 3 * core[0]
    for value, place in (
        (own, pl.ds(here, 2)),
        (split_own, here + 2),
        (other, pl.ds(there, 2)),
        (split_other, there + 2),
    ):
        pltpu.make_async_copy(value, grads.at[place], sem_in.at[12]).start()
    for kind in order:
        for k, state in enumerate((masters, moments, variances)):
            pltpu.make_async_copy(state[kind], buffers[4 * k + kind], sem_in.at[4 * k + kind]).start()
    rows = masters[4].shape[0]
    count = table[rows + 1 : rows + 2, 0:1]
    norm = jnp.sqrt(squares[0:1, 0:1]) / count
    scale = clip_limit / jnp.maximum(norm, clip_limit) / count
    grad_scale = (1.0 - beta_one) * scale
    square_scale = (1.0 - beta_two) / (1.0 - beta_one) ** 2
    root_scale = (1.0 - beta_two**adam_step) ** -0.5
    step_scale = matrix_rate / (1.0 - beta_one**adam_step)
    keep_scale = 1.0 - matrix_rate * weight_decay
    loss_out[0, 0] = (table[rows : rows + 1, 0:1] / count)[0, 0]
    norm_out[0, 0] = norm[0, 0]

    pltpu.make_async_copy(grads, grads, sem_in.at[12]).wait()

    def update(kind, where, cut, row, rows):
        weight, moment, variance = (buffers[4 * k + kind][where] for k in range(3))
        part = grads[cut, row : row + rows, :].astype(f32) * grad_scale
        moment = beta_one * moment + part
        variance = beta_two * variance + (square_scale * part) * part
        divisor = (root_scale * variance) * lax.rsqrt(variance) + adam_eps
        step = (step_scale * moment) * lax.rsqrt(divisor * divisor)
        for k, value in enumerate((keep_scale * weight - step, moment, variance)):
            buffers[4 * k + kind][where] = value

    def each(kind, body):
        for k, state in enumerate((masters, moments, variances)):
            pltpu.make_async_copy(state[kind], buffers[4 * k + kind], sem_in.at[4 * k + kind]).wait()
        pl.loop(0, CUTS)(body)
        for k in range(3):
            out = outs[5 * ((k + 2) % 3) + kind]
            pltpu.make_async_copy(buffers[4 * k + kind], out, sem_out.at[4 * k + kind]).start()

    def lanes(block):
        return pl.ds(pl.multiple_of(block * LANES, LANES), LANES)

    def reduce_body(cut):
        for k in range(4):
            update(3, (slice(96 * k, 96 * k + 96), lanes(cut)), cut, ROW_TWO + 96 * k, 96)

    def expand_body(cut):
        for k in range(4):
            update(2, (slice(None), lanes(4 * cut + k)), cut, ROW_ONE + 96 * k, 96)

    def joint_body(cut):
        for k in range(3):
            update(1, (slice(None), lanes(3 * cut + k)), cut, ROW_QKV + 96 * k, 96)

    def square_body(cut):
        for i, row in enumerate((ROW_P, ROW_O, ROW_H)):
            update(0, (i, slice(None), lanes(cut)), cut, row, 96)

    for kind, body in zip(order, (reduce_body, expand_body, joint_body, square_body)):
        each(kind, body)
    states = (state[4][...] for state in (masters, moments, variances))
    for k, value in enumerate(adam(*states, table[:rows, :] * scale, vector_rate, 0.0)):
        outs[5 * k + 4][...] = value
    for k in range(3):
        for kind in range(4):
            out = outs[5 * ((k + 2) % 3) + kind]
            pltpu.make_async_copy(buffers[4 * k + kind], out, sem_out.at[4 * k + kind]).wait()


def adam_all(core, squares, table, grads, masters, moments, variances):
    smem = pl.BlockSpec(memory_space=pltpu.SMEM)
    vmem = pl.BlockSpec(memory_space=pltpu.VMEM)
    anywhere = pl.BlockSpec(memory_space=pl.ANY)
    shapes = [jax.ShapeDtypeStruct(master.shape, f32) for master in masters]
    loss, norm, *results = pl.pallas_call(
        adam_kernel,
        out_shape=[jax.ShapeDtypeStruct((1, 1), f32)] * 2 + shapes * 3,
        in_specs=[smem] + [vmem] * 2 + [anywhere] * len(grads) + ([anywhere] * 4 + [vmem]) * 3,
        out_specs=[smem] * 2 + ([anywhere] * 4 + [vmem]) * 3,
        scratch_shapes=[pltpu.VMEM(shape.shape, f32) for shape in shapes[:4] * 3]
        + [
            pltpu.VMEM((CUTS, ROWS, LANES), bf16),
            pltpu.SemaphoreType.DMA((13,)),
            pltpu.SemaphoreType.DMA((12,)),
        ],
        compiler_params=pltpu.CompilerParams(vmem_limit_bytes=56 * 1024 * 1024),
        name="adam",
    )(core, squares, table, *grads, *masters, *moments, *variances)
    return loss.reshape(()), norm.reshape(()), results[:5], results[5:10], results[10:]


def positions(slot_float, features):
    column = jnp.arange(features)
    frequency = jnp.exp((2 * (column // 2)).astype(f32) * (-math.log(10000.0) / features))
    angle = slot_float[:, None] * frequency[None, :]
    return jnp.where(column % 2 == 0, jnp.sin(angle), jnp.cos(angle))


def seq_flip(value, k, n_seq):
    return lax.ppermute(value, "seq", [(i, i ^ k) for i in range(n_seq)])


def hop(value, dp_k, seq_k, n_dp, n_seq):
    pairs = [(dp * n_seq + seq, (dp ^ dp_k) * n_seq + (seq ^ seq_k)) for dp in range(n_dp) for seq in range(n_seq)]
    return lax.ppermute(value, ("dp", "seq"), pairs)


def tick(*values):
    return lax.optimization_barrier(values)


def ring_of(n_dp):
    return list(range(0, n_dp, 2)) + list(range(n_dp - 1, 0, -2))


def tree_sum(values):
    while len(values) > 1:
        values = [left + right for left, right in zip(values[0::2], values[1::2])]
    return values[0]


def local(n_dp, n_seq, *args):
    pixels, block_mask, targets = args[:3]
    masters, moments, variances = args[3:8], args[8:13], args[13:18]
    length, features = pixels.shape[1:]
    square, joint, expand, reduce, vectors = masters
    me, group = lax.axis_index("seq"), lax.axis_index("dp")
    ringed = n_dp == BLOCKS and n_seq == 4
    core, side = (me % 2, me // 2) if ringed else (jnp.zeros((), jnp.int32),) * 2
    slots = me ^ jnp.arange(n_seq, dtype=jnp.int32)
    slots_info = jnp.concatenate([slots, jnp.zeros(16 - n_seq, jnp.int32)])
    eight = jnp.arange(8, dtype=jnp.int32)
    first_info = jnp.stack([core, side] + [core] * 6).astype(jnp.int32)

    if ringed:
        ring = ring_of(n_dp)
        forward = [(ring[i], ring[(i + 1) % n_dp]) for i in range(n_dp)]
        backward = [(b, a) for a, b in forward]
        place = jnp.argsort(jnp.array(ring)).astype(jnp.int32)[group]
        blocks = jnp.array(ring, jnp.int32)[(place + eight) % n_dp]
        base = jnp.stack([3 * core, 3 - 3 * core])
        cuts = jnp.stack([base, base + 1 + side, base + 2 - side], 1).astype(jnp.int32)
        info = jnp.concatenate([first_info, slots_info, eight, cuts.reshape(-1), jnp.zeros(10, jnp.int32), blocks])
        shared, on_left, on_right = CUT + 8, CUT + 9, CUT + 10
        pieces, vec_pieces, sources = [], [], []

        def ahead(value):
            return lax.ppermute(value, "dp", forward)

        def behind(value):
            return lax.ppermute(value, "dp", backward)

        def across(value):
            return seq_flip(value, 1, n_seq)

        def trade(value):
            return seq_flip(value, 2, n_seq)

        def note(swapped, number, left, right):
            for value, far, kinds in (
                (left, n_dp - number, (shared, on_left)),
                (right, number, (on_right, shared)),
            ):
                if not swapped:
                    vec_pieces.append((len(sources), kinds.index(shared), ROWS, BLOCK + far))
                pieces.extend((len(sources), i, kind + 3 * swapped, BLOCK + far) for i, kind in enumerate(kinds))
                sources.append(value)

        def note_trade(swapped, number, value):
            for i, (far, kind) in enumerate(((n_dp - number, on_right), (number, on_left))):
                pieces.append((len(sources), i, kind + 3 * swapped, BLOCK + far))
            sources.append(value)

        def in_turn(left, right, traded):
            left, traded = tick(across(left), traded)
            return left, across(right), across(traded)

        def for_trade(left, right):
            return jnp.stack([left[1], right[0]])

        order = jnp.stack([cuts[0, 0], cuts[0, 1], cuts[0, 2], cuts[0, 0]])
        slabs, left0, right0 = pack(order, square, joint, expand, reduce, vectors)
        pieces.extend((0, cut, CUT + cut, BLOCK) for cut in range(CUTS))
        vec_pieces.append((1, 0, ROWS, BLOCK))
        sources.extend((slabs, left0))
        parcels = list(make_parcels(slots, pixels, block_mask, targets))
        left1, right1, *parcels[1:] = tick(
            ahead(left0),
            behind(right0),
            *(seq_flip(parcels[k], k, n_seq) for k in range(1, n_seq)),
        )
        note(0, 1, left1, right1)
        pos = positions(jnp.arange(n_seq * length).astype(f32), features)
        left2, right2, trade1, left1, right1, pos = tick(
            ahead(left1),
            behind(right1),
            trade(for_trade(left1, right1)),
            across(left1),
            across(right1),
            pos,
        )
        note(1, 1, left1, right1)
        note(0, 2, left2, right2)
        note_trade(0, 1, trade1)
        left3, right3, trade2, left2, right2, trade1 = tick(
            ahead(left2), behind(right2), trade(for_trade(left2, right2)), *in_turn(left2, right2, trade1)
        )
        note(1, 2, left2, right2)
        note(0, 3, left3, right3)
        note_trade(1, 1, trade1)
        note_trade(0, 2, trade2)
        left4, right4, trade3, left3, right3, trade2, info = tick(
            ahead(left3),
            behind(right3[:1]),
            trade(for_trade(left3, right3)),
            *in_turn(left3, right3, trade2),
            info,
        )
        note(1, 3, left3, right3)
        note_trade(1, 2, trade2)
        note_trade(0, 3, trade3)
        far = BLOCK + n_dp // 2
        vec_pieces.append((len(sources), 0, ROWS, far))
        for swapped, values in enumerate(((left4, right4), (across(left4), across(right4)))):
            for number, (value, kinds) in enumerate(zip(values, ((shared, on_left), (on_right,)))):
                pieces.extend((len(sources) + number, i, kind + 3 * swapped, far) for i, kind in enumerate(kinds))
            sources.extend(values)
        note_trade(1, 3, across(trade3))
    else:
        parcels = make_parcels(slots, pixels, block_mask, targets)
        parcels = [parcels[0]] + [seq_flip(parcels[k], k, n_seq) for k in range(1, n_seq)]
        pos = positions(jnp.arange(n_seq * length).astype(f32), features)
        gathered = [
            lax.all_gather(value.astype(bf16), "dp", axis=axis, tiled=True)
            for value, axis in zip(masters, (1, 0, 0, 0, 1))
        ]
        def cut_up(matrix):
            rows, columns = matrix.shape
            blocks = columns // (CUTS * LANES)
            shaped = matrix.reshape(BLOCKS, rows // BLOCKS, CUTS, blocks, LANES)
            return shaped.transpose(2, 0, 3, 1, 4).reshape(CUTS, BLOCKS, -1, LANES)

        order = (gathered[0][0], gathered[1], gathered[0][1], gathered[2], gathered[3], gathered[0][2])
        slabs = jnp.concatenate([cut_up(matrix) for matrix in order], 2)
        vec_slabs = gathered[4].reshape(vectors.shape[0], BLOCKS, features // BLOCKS).transpose(1, 0, 2)
        vec_slabs = jnp.pad(vec_slabs, ((0, 0), (0, VEC_ROWS - vectors.shape[0]), (0, LANES - features // BLOCKS)))
        sources = [slabs.reshape(CUTS * BLOCKS, ROWS, LANES), vec_slabs]
        pieces = [(0, BLOCKS * cut + q, CUT + cut, BLOCK + q) for cut in range(CUTS) for q in range(BLOCKS)]
        vec_pieces = [(1, q, 0, BLOCK + q) for q in range(BLOCKS)]
        info = jnp.concatenate([first_info, slots_info, eight, jnp.zeros(16, jnp.int32), eight])

    outs, vgrad = run_step(info, pos, tuple(parcels), tuple(pieces), tuple(vec_pieces), tuple(sources))
    rows = vectors.shape[0]
    n_whole = 2 * len(PLACES)
    keeps, sends = outs[0:n_whole:2], outs[1:n_whole:2]
    split_keeps, split_sends = outs[n_whole::2], outs[n_whole + 1 :: 2]

    def join_halves(low, high):
        cut = ROW_ONE // 2
        return jnp.concatenate([low[..., :cut, :], high[..., :cut, :], low[..., cut:, :], high[..., cut:, :]], -2)

    if ringed:
        def rounded(*values):
            return sum(value.astype(f32) for value in values).astype(bf16)

        half = ROWS // 4

        def low_half(value):
            return jnp.pad(value.astype(f32), ((0, 1), (0, 0), (0, 0)))

        def high_half(value):
            return jnp.pad(value.astype(f32), ((1, 0), (0, 0), (0, 0)))

        small = vgrad.reshape(-1, n_dp, features // n_dp).transpose(1, 0, 2)
        opposite, split_first, next_got, small, small_more, send_rest, split_send_rest = tick(
            rounded(keeps[0], across(sends[0])),
            rounded(split_keeps[0], across(split_sends[0])),
            across(sends[1]),
            small,
            across(small),
            sends[2],
            split_sends[1],
        )
        small = small + small_more
        whole, split = {}, dict(zip((4, 3), split_first[:, 0]))
        left, right, pair_first, whole_next, got_rest, split_rest, small = tick(
            ahead(opposite[0, :1]),
            behind(opposite[0, 1:]),
            trade(split_first[:, 1]),
            rounded(keeps[1], next_got),
            across(send_rest),
            rounded(split_keeps[1], across(split_send_rest)),
            small,
        )
        whole.update(zip((3, 5), whole_next))
        split.update(zip((5, 2, 6, 1, 7, 0), split_rest[:, 0]))
        pair = dict(zip((4, 3), pair_first))
        pair_next, small = tick(trade(split_rest[:3, 1]), small)
        left, right, split_left, split_right, pair_next, whole_rest, split_rest, small, small_more = tick(
            ahead(rounded(whole[3], low_half(left))),
            behind(rounded(whole[5], high_half(right))),
            ahead(rounded(split[4][:half], pair[4][:half])),
            behind(rounded(split[4][half:], pair[4][half:])),
            pair_next,
            rounded(keeps[2], got_rest),
            split_rest,
            small,
            trade(small),
        )
        pair.update(zip((5, 2, 6), pair_next))
        whole.update(zip((2, 6, 1, 7, 0), whole_rest))
        small = jnp.take(small + small_more, group ^ jnp.array([0, 4, 2, 6, 1, 5, 3, 7]), axis=0)
        pair_rest, small = tick(trade(split_rest[3:, 1]), small)
        left, right, split_left, split_right, pair_rest, small, small_more = tick(
            ahead(rounded(whole[2], left)),
            behind(rounded(whole[6], right)),
            ahead(rounded(split[3], pair[3], jnp.pad(split_left.astype(f32), ((0, half), (0, 0))))),
            behind(rounded(split[5], pair[5], jnp.pad(split_right.astype(f32), ((half, 0), (0, 0))))),
            pair_rest,
            small[:4],
            hop(small[4:], 1, 0, n_dp, n_seq),
        )
        pair.update(zip((1, 7, 0), pair_rest))
        small = small + small_more
        left, right, split_left, split_right, small, small_more = tick(
            ahead(rounded(whole[1], left)),
            behind(rounded(whole[7], right)),
            ahead(rounded(split[2], pair[2], split_left)),
            behind(rounded(split[6], pair[6], split_right)),
            small[:2],
            hop(small[2:], 2, 0, n_dp, n_seq),
        )
        small = small + small_more
        own = rounded(whole[0], left, right)
        own, other_chip, split_left, split_right, small, small_more = tick(
            own,
            trade(own),
            ahead(rounded(split[1], pair[1], split_left)),
            behind(rounded(split[7], pair[7], split_right)),
            small[0],
            hop(small[1], 4, 0, n_dp, n_seq),
        )
        small = small + small_more
        split_own, own, other_chip, small = tick(
            rounded(split[0], pair[0], split_left, split_right), own, other_chip, small
        )
        own = rounded(own, other_chip)
        squares = jnp.sum(jnp.square(own.astype(f32))) + 0.5 * jnp.sum(small[:rows] ** 2)
        own, split_own, pair_own, other, squares = tick(own, split_own, trade(split_own), across(own), squares)
        split_own = join_halves(
            jnp.where(side == 0, split_own, pair_own), jnp.where(side == 0, pair_own, split_own)
        )
        split_other = across(split_own)
        squares = jnp.full((1, LANES), squares + jnp.sum(jnp.square(split_own.astype(f32))))
        for hops in (((0, 1), (1, 0), (1, 1)), ((2, 0), (4, 0), (6, 0))):
            squares = tree_sum([squares] + [hop(squares, *ks, n_dp, n_seq) for ks in hops])
    else:
        def by_place(groups, values):
            spread = dict(zip((r for places in groups for r in places), jnp.concatenate(values)))
            return jnp.stack([spread[r] for r in range(BLOCKS)])

        def three(whole, split):
            split = by_place(SPLIT_PLACES, split)
            return jnp.concatenate([by_place(PLACES, whole), join_halves(split[:, 0], split[:, 1])[:, None]], 1)

        canonical = jnp.concatenate([three(keeps, split_keeps), three(sends, split_sends)], 1).transpose(1, 0, 2, 3)

        def join(row, end, blocks):
            part = canonical[:, :, row:end].astype(f32).reshape(CUTS, BLOCKS, blocks, -1, LANES)
            return part.transpose(1, 3, 0, 2, 4).reshape(-1, CUTS * blocks * LANES)

        whole = (
            jnp.stack([join(ROW_P, ROW_QKV, 1), join(ROW_O, ROW_ONE, 1), join(ROW_H, ROWS, 1)]),
            join(ROW_QKV, ROW_O, 3),
            join(ROW_ONE, ROW_TWO, 4),
            join(ROW_TWO, ROW_H, 1),
            vgrad[:rows],
        )
        grads = [
            lax.psum_scatter(grad, "dp", scatter_dimension=axis, tiled=True)
            for grad, axis in zip(whole, (1, 0, 0, 0, 1))
        ]
        grads = lax.psum(grads, "seq")
        vector_grad = grads[4]
        squares = lax.psum(sum(jnp.sum(grad * grad) for grad in grads), "dp")
        loss_sum, count = lax.psum((vgrad[rows, 0], vgrad[rows + 1, 0]), ("dp", "seq"))

    if ringed:
        shared_grads = (own, split_own, other, split_other)
        loss, norm, *new = adam_all(core.reshape(1), squares, small, shared_grads, masters, moments, variances)
    else:
        loss, norm = loss_sum / count, jnp.sqrt(squares) / count
        factor = clip_limit / jnp.maximum(norm, clip_limit) / count
        rates = ((matrix_rate, weight_decay),) * 4 + ((vector_rate, 0.0),)
        updated = [
            adam(master, moment, variance, grad * factor, *rate)
            for master, moment, variance, grad, rate in zip(masters, moments, variances, grads, rates)
        ]
        new = tuple(zip(*updated))
    return (loss, norm, *(new[k][kind] for kind in range(5) for k in range(3)))


def solution(mesh):
    matrix = P("dp", None)
    state = (P(None, "dp", None), matrix, matrix, matrix, P(None, "dp"))
    in_specs = (P("dp", "seq", None), P("dp", "seq"), P("dp", "seq", None)) + state * 3
    out_specs = (P(), P()) + tuple(spec for spec in state for _ in range(3))
    return jax.shard_map(
        partial(local, mesh.shape["dp"], mesh.shape["seq"]),
        mesh=mesh,
        in_specs=in_specs,
        out_specs=out_specs,
        check_vma=False,
    )
```

```python
from functools import partial
import math

import jax
import jax.numpy as jnp
from jax import lax
from jax.experimental import pallas as pl
from jax.experimental.pallas import tpu as pltpu
from jax.sharding import PartitionSpec as P

HEADS = 12
GRID = 14
LANES = 128
BLOCKS = 8
CUTS = 6

norm_eps = 1e-06
beta_one = 0.9
beta_two = 0.999
adam_eps = 1e-08
adam_step = 10.0
matrix_rate = 0.05
vector_rate = 0.3
weight_decay = 0.05
clip_limit = 0.1

f32 = jnp.float32
bf16 = jnp.bfloat16

ROW_P, ROW_QKV, ROW_O, ROW_ONE, ROW_TWO, ROW_H, ROWS = 0, 96, 384, 480, 864, 1248, 1344
VEC_ROWS = 32
PLACES = ((4,), (3, 5), (2, 6, 1, 7, 0))
SPLIT_PLACES = ((4, 3), (5, 2, 6, 1, 7, 0))
OUTS = 2 * len(PLACES) + 2 * len(SPLIT_PLACES)
PART, CUT, BLOCK = 8, 24, 48


def nn(left, right):
    return jnp.dot(left, right, preferred_element_type=f32)


def nt(left, right):
    return lax.dot_general(left, right, (((1,), (1,)), ((), ())), preferred_element_type=f32)


def tn(left, right):
    return lax.dot_general(left, right, (((0,), (0,)), ((), ())), preferred_element_type=f32)


def stats(stream):
    centred = stream - jnp.mean(stream, -1, keepdims=True)
    inverse = lax.rsqrt(jnp.mean(centred * centred, -1, keepdims=True) + norm_eps)
    return (centred * inverse, inverse)


def norm_back(upstream, normed, inverse, gain):
    scaled = upstream * gain
    return inverse * (
        scaled
        - jnp.mean(scaled, -1, keepdims=True)
        - normed * jnp.mean(scaled * normed, -1, keepdims=True)
    )


def column_sum(value):
    return jnp.sum(value, 0, keepdims=True)


def step_kernel(pieces, vec_pieces, n_refs, *refs):
    info, pos = refs[:2]
    n_parts = n_refs[0]
    parcels, sources = refs[2 : 2 + n_parts], refs[2 + n_parts : 2 + sum(n_refs)]
    *outs, vgrad_out = refs[2 + sum(n_refs) : 3 + sum(n_refs) + OUTS]
    w, vec_blocks, vec, pix, target, mask_rows, mask, bias, *refs = refs[3 + sum(n_refs) + OUTS :]
    (x0, x1, x2, branch, mlp, work, qkv, probs, inverses, attn, slope, act, hid, low, *sems) = refs
    vgrad, sem_in, sem_part, sem_out = sems
    length, width = pix.shape
    part = length // n_parts
    pairs = width // 256
    first, second = (0, ROW_ONE), (ROW_ONE, ROWS)

    for k in range(n_parts):
        slot = info[PART + k]
        here = pl.ds(pl.multiple_of(slot * part, part), part)
        pltpu.make_async_copy(parcels[k].at[:part], pix.at[here], sem_part.at[0]).start()
        pltpu.make_async_copy(parcels[k].at[part : 2 * part], target.at[here], sem_part.at[1]).start()
        pltpu.make_async_copy(parcels[k].at[2 * part :, :LANES], mask_rows.at[slot], sem_part.at[2]).start()

    for source, lead, row, block_slot in vec_pieces:
        pltpu.make_async_copy(
            sources[source].at[lead, row : row + VEC_ROWS], vec_blocks.at[info[block_slot]], sem_part.at[3]
        ).start()

    for group, (begin, end) in enumerate((first, second)):
        for source, lead, cut_slot, block_slot in pieces:
            pltpu.make_async_copy(
                sources[source].at[lead, begin:end],
                w.at[info[cut_slot], info[block_slot], begin:end],
                sem_in.at[group],
            ).start()

    for number, whole in enumerate((pix, target, mask_rows, vec_blocks)):
        pltpu.make_async_copy(whole, whole, sem_part.at[number]).wait()
    diagonal = lax.broadcasted_iota(jnp.int32, (part, LANES), 0) == lax.broadcasted_iota(
        jnp.int32, (part, LANES), 1
    )
    for k in range(n_parts):
        row = mask_rows[k].astype(f32)[:1]
        mask[part * k : part * k + part, :] = jnp.sum(jnp.where(diagonal, row, 0.0), 1, keepdims=True)
    for q in range(BLOCKS):
        vec[:, 96 * q : 96 * q + 96] = vec_blocks[q].astype(f32)[:, :96]
    for k in range(4):
        bias[:, width * k : width * k + width] = vec[16 + k : 17 + k, :]

    def arrived(group, begin, end):
        part = w.at[:, :, begin:end]
        pltpu.make_async_copy(part, part, sem_in.at[group]).wait()

    def block(cut, row, rows):
        return w[cut, :, row : row + rows, :].reshape(BLOCKS * rows, LANES)

    def pair(i, row, rows=96):
        return jnp.concatenate([block(2 * i, row, rows), block(2 * i + 1, row, rows)], 1)

    def cols(i, size=256):
        return pl.ds(pl.multiple_of(i * size, size), size)

    def all_cuts(row):
        return jnp.concatenate([block(cut, row, 96) for cut in range(CUTS)], 1)

    def put(cut, row, rows, value):
        w[cut, :, row : row + rows, :] = value.astype(bf16).reshape(BLOCKS, rows, LANES)

    def put_pair(i, row, value):
        put(2 * i, row, 96, value[:, :LANES])
        put(2 * i + 1, row, 96, value[:, LANES:])

    def out_rows(number, begin, end):
        return (begin, end) if number < 2 * len(PLACES) else (begin // 2, end // 2)

    def leave(group, begin, end):
        core, side = info[0], info[1]
        half = (end - begin) // 2
        for number, out in enumerate(outs):
            split, away = number >= 2 * len(PLACES), number % 2
            first_cut = 3 * (core ^ away)
            lo, hi = out_rows(number, begin, end)
            for i, place in enumerate((PLACES + SPLIT_PLACES)[number // 2]):
                block_index = info[BLOCK + place]
                if not split:
                    pltpu.make_async_copy(
                        w.at[pl.ds(first_cut, 2), block_index, begin:end],
                        out.at[i, :, lo:hi],
                        sem_out.at[number, group],
                    ).start()
                    continue
                for part in range(2):
                    rows = pl.ds(pl.multiple_of(begin + half * (side ^ part), 16), half)
                    pltpu.make_async_copy(
                        w.at[first_cut + 2, block_index, rows], out.at[i, part, lo:hi], sem_out.at[number, group]
                    ).start()

    row_index = lax.broadcasted_iota(jnp.int32, (length, 1), 0)
    is_class = row_index == GRID * GRID
    key_valid = lax.broadcasted_iota(jnp.int32, (1, length), 1) <= GRID * GRID
    lower_half = lax.broadcasted_iota(jnp.int32, (1, LANES), 1) < LANES // 2
    masked = mask[...] > 0.5

    arrived(0, *first)

    @pl.loop(0, pairs)
    def _(i):
        c = cols(i)
        embedded = nn(pix[...], pair(i, ROW_P)) + vec[2:3, c]
        value = jnp.where(is_class, vec[0:1, c], jnp.where(masked, vec[1:2, c], embedded))
        x0[:, c] = value + pos[:, c]

    normed, _ = stats(x0[...])
    low[...] = (normed * vec[3:4, :] + vec[4:5, :]).astype(bf16)

    @pl.loop(0, pairs)
    def _(i):
        parts = [
            w[2 * i + j // 3, :, ROW_QKV + 96 * (j % 3) : ROW_QKV + 96 * (j % 3) + 96, :].reshape(width, LANES)
            for j in range(6)
        ]
        shift = jnp.where(i == 0, vec[5:6, :], jnp.where(i == 1, 0.0, vec[6:7, :]))
        for j in range(3):
            value = nn(low[...], jnp.concatenate(parts[2 * j : 2 * j + 2], 1)) + shift[:, 256 * j : 256 * j + 256]
            qkv[i, :, 256 * j : 256 * j + 256] = value.astype(bf16)

    def half_lanes(half):
        return lower_half if half == 0 else jnp.logical_not(lower_half)

    @pl.loop(0, HEADS // 2)
    def _(i):
        c = cols(i, LANES)
        query, key, value = qkv[0, :, c] * 0.125, qkv[1, :, c], qkv[2, :, c]
        outs = []
        for half in range(2):
            chosen = half_lanes(half)
            scores = nt(jnp.where(chosen, query, jnp.zeros_like(query)), key)
            scores = jnp.where(key_valid, scores, -1e30)
            weights = jnp.exp(scores - jnp.max(scores, -1, keepdims=True)).astype(bf16)
            probs[2 * i + half] = weights
            outs.append(nn(weights, jnp.where(chosen, value, jnp.ones_like(value))))
        total = pltpu.roll(jnp.where(lower_half, outs[1], outs[0]), LANES // 2, 1)
        inverse = 1.0 / total
        inverses[:, c] = inverse
        attn[:, c] = (jnp.where(lower_half, outs[0], outs[1]) * inverse).astype(bf16)

    @pl.loop(0, pairs)
    def _(i):
        c = cols(i)
        value = nn(attn[...], pair(i, ROW_O)) + vec[7:8, c]
        branch[:, c] = value
        x1[:, c] = x0[:, c] + vec[8:9, c] * value

    normed, _ = stats(x1[...])
    low[...] = (normed * vec[9:10, :] + vec[10:11, :]).astype(bf16)
    arrived(1, *second)

    @pl.loop(0, CUTS)
    def _(cut):
        for j in range(2):
            rhs = jnp.concatenate(
                [
                    w[cut, :, ROW_ONE + 96 * k : ROW_ONE + 96 * k + 96, :].reshape(width, LANES)
                    for k in (2 * j, 2 * j + 1)
                ],
                1,
            )
            c = cols(2 * cut + j)
            inner = nn(low[...], rhs) + bias[:, c]
            cdf = 0.5 + 0.5 * lax.erf(inner * math.sqrt(0.5))
            act[:, c] = (inner * cdf).astype(bf16)
            slope[:, c] = cdf + inner * (jnp.exp(-0.5 * inner * inner) * (1.0 / math.sqrt(2.0 * math.pi)))

    @pl.loop(0, pairs)
    def _(i):
        c = cols(i)
        value = nn(act[...], pair(i, ROW_TWO, 384)) + vec[11:12, c]
        mlp[:, c] = value
        x2[:, c] = x1[:, c] + vec[12:13, c] * value

    normed3, inverse3 = stats(x2[...])
    low[...] = (normed3 * vec[13:14, :] + vec[14:15, :]).astype(bf16)
    loss = work
    loss[0:1, 0:256] = jnp.zeros((1, 256), f32)

    @pl.loop(0, pairs)
    def _(i):
        c = cols(i)
        residual = nn(low[...], pair(i, ROW_H)) + vec[15:16, c] - target[:, c].astype(f32)
        size = jnp.abs(residual)
        terms = jnp.where(size < 2.0, 0.25 * residual * residual, size - 1.0)
        loss[0:1, 0:256] += column_sum(jnp.where(masked, terms, 0.0))
        grad = jnp.where(masked, jnp.clip(0.5 * residual, -1.0, 1.0), 0.0)
        vgrad[15:16, c] = column_sum(grad)
        hid[:, c] = grad.astype(bf16)

    vgrad[20:21, :] = jnp.broadcast_to(jnp.sum(loss[0:1, 0:256], 1, keepdims=True), (1, width))
    vgrad[21:22, :] = jnp.broadcast_to(jnp.sum(mask[...], 0, keepdims=True), (1, width))
    vgrad[22:24, :] = jnp.zeros((2, width), f32)
    upstream = nt(hid[...], all_cuts(ROW_H))
    vgrad[13:14, :] = column_sum(upstream * normed3)
    vgrad[14:15, :] = column_sum(upstream)
    grad2 = norm_back(upstream, normed3, inverse3, vec[13:14, :])
    x2[...] = grad2
    flipped = low[...].T

    @pl.loop(0, pairs)
    def _(i):
        put_pair(i, ROW_H, nn(flipped, hid[:, cols(i)]))

    vgrad[12:13, :] = column_sum(grad2 * mlp[...])
    grad_mlp = grad2 * vec[12:13, :]
    vgrad[11:12, :] = column_sum(grad_mlp)
    hid[...] = grad_mlp.astype(bf16)

    @pl.loop(0, BLOCKS)
    def _(q):
        c = cols(q, 384)
        rhs = jnp.concatenate([w[cut, q, ROW_TWO:ROW_H, :] for cut in range(CUTS)], 1)
        grad_inner = nt(hid[...], rhs) * slope[:, c]
        bias_grad = column_sum(grad_inner)
        slope[0:1, c] = bias_grad
        value = nn(act[:, c].T, hid[...]).astype(bf16)
        for cut in range(CUTS):
            w[cut, q, ROW_TWO:ROW_H, :] = value[:, LANES * cut : LANES * cut + LANES]
        act[:, c] = grad_inner.astype(bf16)

    for k in range(4):
        vgrad[16 + k : 17 + k, :] = slope[0:1, width * k : width * k + width]

    normed2, inverse2 = stats(x1[...])
    low[...] = (normed2 * vec[9:10, :] + vec[10:11, :]).astype(bf16)
    flipped = low[...].T
    work[...] = jnp.zeros_like(work)

    @pl.loop(0, CUTS)
    def _(cut):
        grad_inner = act[:, cols(cut, 512)]
        rhs = jnp.concatenate(
            [w[cut, :, ROW_ONE + 96 * k : ROW_ONE + 96 * k + 96, :].reshape(width, LANES) for k in range(4)], 1
        )
        work[...] += nt(grad_inner, rhs)
        for j in range(2):
            value = nn(flipped, grad_inner[:, 256 * j : 256 * j + 256])
            put(cut, ROW_ONE + 192 * j, 96, value[:, :LANES])
            put(cut, ROW_ONE + 192 * j + 96, 96, value[:, LANES:])

    leave(1, *second)

    upstream = work[...]
    vgrad[9:10, :] = column_sum(upstream * normed2)
    vgrad[10:11, :] = column_sum(upstream)
    grad1 = x2[...] + norm_back(upstream, normed2, inverse2, vec[9:10, :])
    x2[...] = grad1
    vgrad[8:9, :] = column_sum(grad1 * branch[...])
    grad_branch = grad1 * vec[8:9, :]
    vgrad[7:8, :] = column_sum(grad_branch)
    hid[...] = grad_branch.astype(bf16)
    low[...] = nt(hid[...], all_cuts(ROW_O)).astype(bf16)
    flipped = attn[...].T

    @pl.loop(0, pairs)
    def _(i):
        put_pair(i, ROW_O, nn(flipped, hid[:, cols(i)]))

    lane = lax.broadcasted_iota(jnp.int32, (1, LANES), 1)

    @pl.loop(0, HEADS // 2)
    def _(i):
        c = cols(i, LANES)
        query, key, value = qkv[0, :, c], qkv[1, :, c], qkv[2, :, c]
        out_grad, inverse = low[:, c].astype(f32), inverses[:, c]
        product = out_grad * attn[:, c].astype(f32)
        scaled_query = (query.astype(f32) * inverse).astype(bf16)
        scaled_grad = (out_grad * inverse).astype(bf16)
        outs = []
        for half in range(2):
            chosen = half_lanes(half)
            spare = LANES // 2 * (1 - half)
            sums = jnp.sum(jnp.where(chosen, product, 0.0), -1, keepdims=True)
            rough = sums.astype(bf16).astype(f32)
            fine = jnp.where(lane == spare, rough, jnp.where(lane == spare + 1, sums - rough, 0.0))
            left = jnp.where(chosen, out_grad, fine).astype(bf16)
            minus = jnp.where(jnp.logical_or(lane == spare, lane == spare + 1), -1.0, 0.0).astype(bf16)
            weights = probs[2 * i + half]
            ds = (weights.astype(f32) * nt(left, jnp.where(chosen, value, minus))).astype(bf16)
            outs.append((nn(ds, key), tn(ds, scaled_query), tn(weights, scaled_grad)))
        dq, dk, dv = (jnp.where(lower_half, one, two) for one, two in zip(*outs))
        dq, dk = (dq * inverse * 0.125, dk * 0.125)
        vgrad[5:6, c] = column_sum(dq)
        vgrad[6:7, c] = column_sum(dv)
        qkv[0, :, c], qkv[1, :, c], qkv[2, :, c] = (dq.astype(bf16), dk.astype(bf16), dv.astype(bf16))

    normed1, inverse1 = stats(x0[...])
    low[...] = (normed1 * vec[3:4, :] + vec[4:5, :]).astype(bf16)
    flipped = low[...].T
    work[...] = jnp.zeros_like(work)

    @pl.loop(0, pairs)
    def _(i):
        parts = [
            w[2 * i + j // 3, :, ROW_QKV + 96 * (j % 3) : ROW_QKV + 96 * (j % 3) + 96, :].reshape(width, LANES)
            for j in range(6)
        ]
        work[...] += nt(qkv[i], jnp.concatenate(parts, 1))
        for j in range(3):
            value = nn(flipped, qkv[i, :, 256 * j : 256 * j + 256]).astype(bf16)
            for half in range(2):
                k = 2 * j + half
                w[2 * i + k // 3, :, ROW_QKV + 96 * (k % 3) : ROW_QKV + 96 * (k % 3) + 96, :] = value[
                    :, LANES * half : LANES * half + LANES
                ].reshape(BLOCKS, 96, LANES)

    upstream = work[...]
    vgrad[3:4, :] = column_sum(upstream * normed1)
    vgrad[4:5, :] = column_sum(upstream)
    grad0 = x2[...] + norm_back(upstream, normed1, inverse1, vec[3:4, :])
    vgrad[0:1, :] = column_sum(jnp.where(is_class, grad0, 0.0))
    token = jnp.logical_and(masked, jnp.logical_not(is_class))
    vgrad[1:2, :] = column_sum(jnp.where(token, grad0, 0.0))
    grad_embed = jnp.where(jnp.logical_or(is_class, masked), 0.0, grad0)
    vgrad[2:3, :] = column_sum(grad_embed)
    hid[...] = grad_embed.astype(bf16)
    flipped = pix[...].T

    @pl.loop(0, pairs)
    def _(i):
        put_pair(i, ROW_P, nn(flipped, hid[:, cols(i)]))

    leave(0, *first)
    for q in range(BLOCKS):
        vgrad_out[q] = vgrad[:, 96 * q : 96 * q + 96]
    for number, out in enumerate(outs):
        for group, (begin, end) in enumerate((first, second)):
            lo, hi = out_rows(number, begin, end)
            rows = out.at[:, :, lo:hi]
            pltpu.make_async_copy(rows, rows, sem_out.at[number, group]).wait()


def run_step(info, pos, parcels, pieces, vec_pieces, sources):
    length, width = pos.shape
    hidden = 4 * width
    vmem = pl.BlockSpec(memory_space=pltpu.VMEM)
    anywhere = pl.BlockSpec(memory_space=pl.ANY)
    big = pltpu.VMEM((length, width), f32)
    small = pltpu.VMEM((length, width), bf16)
    *outs, vgrad = pl.pallas_call(
        partial(step_kernel, pieces, vec_pieces, (len(parcels), len(sources))),
        out_shape=(
            *(jax.ShapeDtypeStruct((len(places), 2, ROWS, LANES), bf16) for places in PLACES for _ in range(2)),
            *(
                jax.ShapeDtypeStruct((len(places), 2, ROWS // 2, LANES), bf16)
                for places in SPLIT_PLACES
                for _ in range(2)
            ),
            jax.ShapeDtypeStruct((BLOCKS, 24, width // BLOCKS), f32),
        ),
        in_specs=[pl.BlockSpec(memory_space=pltpu.SMEM)] + [vmem] + [anywhere] * (len(parcels) + len(sources)),
        out_specs=(*[anywhere] * OUTS, vmem),
        scratch_shapes=[
            pltpu.VMEM((CUTS, BLOCKS, ROWS, LANES), bf16),
            pltpu.VMEM((BLOCKS, VEC_ROWS, LANES), bf16),
            pltpu.VMEM((VEC_ROWS, width), f32),
            small,
            small,
            pltpu.VMEM((len(parcels), 16, LANES), bf16),
            pltpu.VMEM((length, 1), f32),
            pltpu.VMEM((1, hidden), f32),
            big,
            big,
            big,
            big,
            big,
            big,
            pltpu.VMEM((3, length, width), bf16),
            pltpu.VMEM((HEADS, length, length), bf16),
            big,
            small,
            pltpu.VMEM((length, hidden), f32),
            pltpu.VMEM((length, hidden), bf16),
            small,
            small,
            pltpu.VMEM((24, width), f32),
            pltpu.SemaphoreType.DMA((2,)),
            pltpu.SemaphoreType.DMA((4,)),
            pltpu.SemaphoreType.DMA((OUTS, 2)),
        ],
        compiler_params=pltpu.CompilerParams(vmem_limit_bytes=60 * 1024 * 1024),
        name="step",
    )(info, pos, *parcels, *sources)
    return outs, vgrad


def pack_kernel(chosen, square, joint, expand, reduce, vectors, out, *streams):
    for cut in range(CUTS):
        for row, n, rows, take in (
            (ROW_P, 1, 96, lambda c: square[0, :, c]),
            (ROW_QKV, 3, 96, lambda c: joint[:, c]),
            (ROW_O, 1, 96, lambda c: square[1, :, c]),
            (ROW_ONE, 4, 96, lambda c: expand[:, c]),
            (ROW_TWO, 1, 384, lambda c: reduce[:, c]),
            (ROW_H, 1, 96, lambda c: square[2, :, c]),
        ):
            for j in range(n):
                begin = LANES * (n * cut + j)
                out[cut, row + rows * j : row + rows * j + rows, :] = take(slice(begin, begin + LANES)).astype(bf16)
    for number, stream in enumerate(streams):
        for i in range(2):
            stream[i, :ROWS] = out[chosen[2 * number + i]]
            stream[i, ROWS:] = jnp.zeros((VEC_ROWS, LANES), bf16)
            stream[i, ROWS:, : vectors.shape[1]] = jnp.concatenate(
                [vectors[...], jnp.zeros((VEC_ROWS - vectors.shape[0], vectors.shape[1]), f32)]
            ).astype(bf16)


def pack(chosen, *shards):
    vmem = pl.BlockSpec(memory_space=pltpu.VMEM)
    return pl.pallas_call(
        pack_kernel,
        out_shape=[jax.ShapeDtypeStruct((CUTS, ROWS, LANES), bf16)]
        + [jax.ShapeDtypeStruct((2, ROWS + VEC_ROWS, LANES), bf16)] * 2,
        in_specs=[pl.BlockSpec(memory_space=pltpu.SMEM)] + [vmem] * 5,
        out_specs=[vmem] * 3,
        name="pack",
    )(chosen, *shards)


def parcel_kernel(slots, pixels, block_mask, targets, *outs):
    length = pixels.shape[1]
    top = lax.broadcasted_iota(jnp.int32, (16, length), 0) == 0
    for k, out in enumerate(outs):
        slot = slots[k]
        out[:length, :] = pixels[slot]
        out[length : 2 * length, :] = targets[slot]
        out[2 * length :, :] = jnp.zeros((16, out.shape[1]), bf16)
        row = block_mask[pl.ds(slot, 1), :].astype(f32)
        out[2 * length :, :length] = jnp.where(top, row, 0.0).astype(bf16)


def make_parcels(slots, pixels, block_mask, targets):
    images, length, features = pixels.shape
    vmem = pl.BlockSpec(memory_space=pltpu.VMEM)
    return pl.pallas_call(
        parcel_kernel,
        out_shape=[jax.ShapeDtypeStruct((2 * length + 16, features), bf16)] * images,
        in_specs=[pl.BlockSpec(memory_space=pltpu.SMEM)] + [vmem] * 3,
        out_specs=[vmem] * images,
        name="parcels",
    )(slots, pixels, block_mask, targets)


def adam(weight, moment, variance, grad, rate, decay):
    moment_new = beta_one * moment + (1.0 - beta_one) * grad
    variance_new = beta_two * variance + (1.0 - beta_two) * grad * grad
    corrected = (
        moment_new
        * (1.0 / (1.0 - beta_one**adam_step))
        / (jnp.sqrt(variance_new * (1.0 / (1.0 - beta_two**adam_step))) + adam_eps)
    )
    return (moment_new, variance_new, weight - rate * (corrected + decay * weight))


def adam_kernel(core, squares, table, own, split_own, other, split_other, *refs):
    masters, moments, variances = refs[:5], refs[5:10], refs[10:15]
    loss_out, norm_out, *outs = refs[15:32]
    buffers, grads, sem_in, sem_out = refs[32:44], *refs[44:]
    order = (3, 2, 1, 0)
    here, there = 3 * core[0], 3 - 3 * core[0]
    for value, place in (
        (own, pl.ds(here, 2)),
        (split_own, here + 2),
        (other, pl.ds(there, 2)),
        (split_other, there + 2),
    ):
        pltpu.make_async_copy(value, grads.at[place], sem_in.at[12]).start()
    for kind in order:
        for k, state in enumerate((masters, moments, variances)):
            pltpu.make_async_copy(state[kind], buffers[4 * k + kind], sem_in.at[4 * k + kind]).start()
    rows = masters[4].shape[0]
    count = table[rows + 1 : rows + 2, 0:1]
    norm = jnp.sqrt(squares[0:1, 0:1]) / count
    scale = clip_limit / jnp.maximum(norm, clip_limit) / count
    grad_scale = (1.0 - beta_one) * scale
    square_scale = (1.0 - beta_two) / (1.0 - beta_one) ** 2
    root_scale = (1.0 - beta_two**adam_step) ** -0.5
    step_scale = matrix_rate / (1.0 - beta_one**adam_step)
    keep_scale = 1.0 - matrix_rate * weight_decay
    loss_out[0, 0] = (table[rows : rows + 1, 0:1] / count)[0, 0]
    norm_out[0, 0] = norm[0, 0]

    pltpu.make_async_copy(grads, grads, sem_in.at[12]).wait()

    def update(kind, where, cut, row, rows):
        weight, moment, variance = (buffers[4 * k + kind][where] for k in range(3))
        part = grads[cut, row : row + rows, :].astype(f32) * grad_scale
        moment = beta_one * moment + part
        variance = beta_two * variance + (square_scale * part) * part
        divisor = (root_scale * variance) * lax.rsqrt(variance) + adam_eps
        step = (step_scale * moment) * lax.rsqrt(divisor * divisor)
        for k, value in enumerate((keep_scale * weight - step, moment, variance)):
            buffers[4 * k + kind][where] = value

    def each(kind, body):
        for k, state in enumerate((masters, moments, variances)):
            pltpu.make_async_copy(state[kind], buffers[4 * k + kind], sem_in.at[4 * k + kind]).wait()
        pl.loop(0, CUTS)(body)
        for k in range(3):
            out = outs[5 * ((k + 2) % 3) + kind]
            pltpu.make_async_copy(buffers[4 * k + kind], out, sem_out.at[4 * k + kind]).start()

    def lanes(block):
        return pl.ds(pl.multiple_of(block * LANES, LANES), LANES)

    def reduce_body(cut):
        for k in range(4):
            update(3, (slice(96 * k, 96 * k + 96), lanes(cut)), cut, ROW_TWO + 96 * k, 96)

    def expand_body(cut):
        for k in range(4):
            update(2, (slice(None), lanes(4 * cut + k)), cut, ROW_ONE + 96 * k, 96)

    def joint_body(cut):
        for k in range(3):
            update(1, (slice(None), lanes(3 * cut + k)), cut, ROW_QKV + 96 * k, 96)

    def square_body(cut):
        for i, row in enumerate((ROW_P, ROW_O, ROW_H)):
            update(0, (i, slice(None), lanes(cut)), cut, row, 96)

    for kind, body in zip(order, (reduce_body, expand_body, joint_body, square_body)):
        each(kind, body)
    states = (state[4][...] for state in (masters, moments, variances))
    for k, value in enumerate(adam(*states, table[:rows, :] * scale, vector_rate, 0.0)):
        outs[5 * k + 4][...] = value
    for k in range(3):
        for kind in range(4):
            out = outs[5 * ((k + 2) % 3) + kind]
            pltpu.make_async_copy(buffers[4 * k + kind], out, sem_out.at[4 * k + kind]).wait()


def adam_all(core, squares, table, grads, masters, moments, variances):
    smem = pl.BlockSpec(memory_space=pltpu.SMEM)
    vmem = pl.BlockSpec(memory_space=pltpu.VMEM)
    anywhere = pl.BlockSpec(memory_space=pl.ANY)
    shapes = [jax.ShapeDtypeStruct(master.shape, f32) for master in masters]
    loss, norm, *results = pl.pallas_call(
        adam_kernel,
        out_shape=[jax.ShapeDtypeStruct((1, 1), f32)] * 2 + shapes * 3,
        in_specs=[smem] + [vmem] * 2 + [anywhere] * len(grads) + ([anywhere] * 4 + [vmem]) * 3,
        out_specs=[smem] * 2 + ([anywhere] * 4 + [vmem]) * 3,
        scratch_shapes=[pltpu.VMEM(shape.shape, f32) for shape in shapes[:4] * 3]
        + [
            pltpu.VMEM((CUTS, ROWS, LANES), bf16),
            pltpu.SemaphoreType.DMA((13,)),
            pltpu.SemaphoreType.DMA((12,)),
        ],
        compiler_params=pltpu.CompilerParams(vmem_limit_bytes=56 * 1024 * 1024),
        name="adam",
    )(core, squares, table, *grads, *masters, *moments, *variances)
    return loss.reshape(()), norm.reshape(()), results[:5], results[5:10], results[10:]


def positions(slot_float, features):
    column = jnp.arange(features)
    frequency = jnp.exp((2 * (column // 2)).astype(f32) * (-math.log(10000.0) / features))
    angle = slot_float[:, None] * frequency[None, :]
    return jnp.where(column % 2 == 0, jnp.sin(angle), jnp.cos(angle))


def seq_flip(value, k, n_seq):
    return lax.ppermute(value, "seq", [(i, i ^ k) for i in range(n_seq)])


def hop(value, dp_k, seq_k, n_dp, n_seq):
    pairs = [(dp * n_seq + seq, (dp ^ dp_k) * n_seq + (seq ^ seq_k)) for dp in range(n_dp) for seq in range(n_seq)]
    return lax.ppermute(value, ("dp", "seq"), pairs)


def tick(*values):
    return lax.optimization_barrier(values)


def ring_of(n_dp):
    return list(range(0, n_dp, 2)) + list(range(n_dp - 1, 0, -2))


def tree_sum(values):
    while len(values) > 1:
        values = [left + right for left, right in zip(values[0::2], values[1::2])]
    return values[0]


def local(n_dp, n_seq, *args):
    pixels, block_mask, targets = args[:3]
    masters, moments, variances = args[3:8], args[8:13], args[13:18]
    length, features = pixels.shape[1:]
    square, joint, expand, reduce, vectors = masters
    me, group = lax.axis_index("seq"), lax.axis_index("dp")
    ringed = n_dp == BLOCKS and n_seq == 4
    core, side = (me % 2, me // 2) if ringed else (jnp.zeros((), jnp.int32),) * 2
    slots = me ^ jnp.arange(n_seq, dtype=jnp.int32)
    slots_info = jnp.concatenate([slots, jnp.zeros(16 - n_seq, jnp.int32)])
    eight = jnp.arange(8, dtype=jnp.int32)
    first_info = jnp.stack([core, side] + [core] * 6).astype(jnp.int32)

    if ringed:
        ring = ring_of(n_dp)
        forward = [(ring[i], ring[(i + 1) % n_dp]) for i in range(n_dp)]
        backward = [(b, a) for a, b in forward]
        place = jnp.argsort(jnp.array(ring)).astype(jnp.int32)[group]
        blocks = jnp.array(ring, jnp.int32)[(place + eight) % n_dp]
        base = jnp.stack([3 * core, 3 - 3 * core])
        cuts = jnp.stack([base, base + 1 + side, base + 2 - side], 1).astype(jnp.int32)
        info = jnp.concatenate([first_info, slots_info, eight, cuts.reshape(-1), jnp.zeros(10, jnp.int32), blocks])
        shared, on_left, on_right = CUT + 8, CUT + 9, CUT + 10
        pieces, vec_pieces, sources = [], [], []

        def ahead(value):
            return lax.ppermute(value, "dp", forward)

        def behind(value):
            return lax.ppermute(value, "dp", backward)

        def across(value):
            return seq_flip(value, 1, n_seq)

        def trade(value):
            return seq_flip(value, 2, n_seq)

        def note(swapped, number, left, right):
            for value, far, kinds in (
                (left, n_dp - number, (shared, on_left)),
                (right, number, (on_right, shared)),
            ):
                if not swapped:
                    vec_pieces.append((len(sources), kinds.index(shared), ROWS, BLOCK + far))
                pieces.extend((len(sources), i, kind + 3 * swapped, BLOCK + far) for i, kind in enumerate(kinds))
                sources.append(value)

        def note_trade(swapped, number, value):
            for i, (far, kind) in enumerate(((n_dp - number, on_right), (number, on_left))):
                pieces.append((len(sources), i, kind + 3 * swapped, BLOCK + far))
            sources.append(value)

        def in_turn(left, right, traded):
            left, traded = tick(across(left), traded)
            return left, across(right), across(traded)

        def for_trade(left, right):
            return jnp.stack([left[1], right[0]])

        order = jnp.stack([cuts[0, 0], cuts[0, 1], cuts[0, 2], cuts[0, 0]])
        slabs, left0, right0 = pack(order, square, joint, expand, reduce, vectors)
        pieces.extend((0, cut, CUT + cut, BLOCK) for cut in range(CUTS))
        vec_pieces.append((1, 0, ROWS, BLOCK))
        sources.extend((slabs, left0))
        parcels = list(make_parcels(slots, pixels, block_mask, targets))
        left1, right1, *parcels[1:] = tick(
            ahead(left0),
            behind(right0),
            *(seq_flip(parcels[k], k, n_seq) for k in range(1, n_seq)),
        )
        note(0, 1, left1, right1)
        pos = positions(jnp.arange(n_seq * length).astype(f32), features)
        left2, right2, trade1, left1, right1, pos = tick(
            ahead(left1),
            behind(right1),
            trade(for_trade(left1, right1)),
            across(left1),
            across(right1),
            pos,
        )
        note(1, 1, left1, right1)
        note(0, 2, left2, right2)
        note_trade(0, 1, trade1)
        left3, right3, trade2, left2, right2, trade1 = tick(
            ahead(left2), behind(right2), trade(for_trade(left2, right2)), *in_turn(left2, right2, trade1)
        )
        note(1, 2, left2, right2)
        note(0, 3, left3, right3)
        note_trade(1, 1, trade1)
        note_trade(0, 2, trade2)
        left4, right4, trade3, left3, right3, trade2, info = tick(
            ahead(left3),
            behind(right3[:1]),
            trade(for_trade(left3, right3)),
            *in_turn(left3, right3, trade2),
            info,
        )
        note(1, 3, left3, right3)
        note_trade(1, 2, trade2)
        note_trade(0, 3, trade3)
        far = BLOCK + n_dp // 2
        vec_pieces.append((len(sources), 0, ROWS, far))
        for swapped, values in enumerate(((left4, right4), (across(left4), across(right4)))):
            for number, (value, kinds) in enumerate(zip(values, ((shared, on_left), (on_right,)))):
                pieces.extend((len(sources) + number, i, kind + 3 * swapped, far) for i, kind in enumerate(kinds))
            sources.extend(values)
        note_trade(1, 3, across(trade3))
    else:
        parcels = make_parcels(slots, pixels, block_mask, targets)
        parcels = [parcels[0]] + [seq_flip(parcels[k], k, n_seq) for k in range(1, n_seq)]
        pos = positions(jnp.arange(n_seq * length).astype(f32), features)
        gathered = [
            lax.all_gather(value.astype(bf16), "dp", axis=axis, tiled=True)
            for value, axis in zip(masters, (1, 0, 0, 0, 1))
        ]
        def cut_up(matrix):
            rows, columns = matrix.shape
            blocks = columns // (CUTS * LANES)
            shaped = matrix.reshape(BLOCKS, rows // BLOCKS, CUTS, blocks, LANES)
            return shaped.transpose(2, 0, 3, 1, 4).reshape(CUTS, BLOCKS, -1, LANES)

        order = (gathered[0][0], gathered[1], gathered[0][1], gathered[2], gathered[3], gathered[0][2])
        slabs = jnp.concatenate([cut_up(matrix) for matrix in order], 2)
        vec_slabs = gathered[4].reshape(vectors.shape[0], BLOCKS, features // BLOCKS).transpose(1, 0, 2)
        vec_slabs = jnp.pad(vec_slabs, ((0, 0), (0, VEC_ROWS - vectors.shape[0]), (0, LANES - features // BLOCKS)))
        sources = [slabs.reshape(CUTS * BLOCKS, ROWS, LANES), vec_slabs]
        pieces = [(0, BLOCKS * cut + q, CUT + cut, BLOCK + q) for cut in range(CUTS) for q in range(BLOCKS)]
        vec_pieces = [(1, q, 0, BLOCK + q) for q in range(BLOCKS)]
        info = jnp.concatenate([first_info, slots_info, eight, jnp.zeros(16, jnp.int32), eight])

    outs, vgrad = run_step(info, pos, tuple(parcels), tuple(pieces), tuple(vec_pieces), tuple(sources))
    rows = vectors.shape[0]
    n_whole = 2 * len(PLACES)
    keeps, sends = outs[0:n_whole:2], outs[1:n_whole:2]
    split_keeps, split_sends = outs[n_whole::2], outs[n_whole + 1 :: 2]

    def join_halves(low, high):
        cut = ROW_ONE // 2
        return jnp.concatenate([low[..., :cut, :], high[..., :cut, :], low[..., cut:, :], high[..., cut:, :]], -2)

    if ringed:
        def rounded(*values):
            return sum(value.astype(f32) for value in values).astype(bf16)

        half = ROWS // 4

        def low_half(value):
            return jnp.pad(value.astype(f32), ((0, 1), (0, 0), (0, 0)))

        def high_half(value):
            return jnp.pad(value.astype(f32), ((1, 0), (0, 0), (0, 0)))

        small = vgrad
        opposite, split_first, next_got, small, small_more, send_rest, split_send_rest = tick(
            rounded(keeps[0], across(sends[0])),
            rounded(split_keeps[0], across(split_sends[0])),
            across(sends[1]),
            small,
            across(small),
            sends[2],
            split_sends[1],
        )
        small = small + small_more
        whole, split = {}, dict(zip((4, 3), split_first[:, 0]))
        left, right, pair_first, whole_next, got_rest, split_rest, small = tick(
            ahead(opposite[0, :1]),
            behind(opposite[0, 1:]),
            trade(split_first[:, 1]),
            rounded(keeps[1], next_got),
            across(send_rest),
            rounded(split_keeps[1], across(split_send_rest)),
            small,
        )
        whole.update(zip((3, 5), whole_next))
        split.update(zip((5, 2, 6, 1, 7, 0), split_rest[:, 0]))
        pair = dict(zip((4, 3), pair_first))
        pair_next, small = tick(trade(split_rest[:3, 1]), small)
        left, right, split_left, split_right, pair_next, whole_rest, split_rest, small, small_more = tick(
            ahead(rounded(whole[3], low_half(left))),
            behind(rounded(whole[5], high_half(right))),
            ahead(rounded(split[4][:half], pair[4][:half])),
            behind(rounded(split[4][half:], pair[4][half:])),
            pair_next,
            rounded(keeps[2], got_rest),
            split_rest,
            small,
            trade(small),
        )
        pair.update(zip((5, 2, 6), pair_next))
        whole.update(zip((2, 6, 1, 7, 0), whole_rest))
        small = jnp.take(small + small_more, group ^ jnp.array([0, 4, 2, 6, 1, 5, 3, 7]), axis=0)
        pair_rest, small = tick(trade(split_rest[3:, 1]), small)
        left, right, split_left, split_right, pair_rest, small, small_more = tick(
            ahead(rounded(whole[2], left)),
            behind(rounded(whole[6], right)),
            ahead(rounded(split[3], pair[3], jnp.pad(split_left.astype(f32), ((0, half), (0, 0))))),
            behind(rounded(split[5], pair[5], jnp.pad(split_right.astype(f32), ((half, 0), (0, 0))))),
            pair_rest,
            small[:4],
            hop(small[4:], 1, 0, n_dp, n_seq),
        )
        pair.update(zip((1, 7, 0), pair_rest))
        small = small + small_more
        left, right, split_left, split_right, small, small_more = tick(
            ahead(rounded(whole[1], left)),
            behind(rounded(whole[7], right)),
            ahead(rounded(split[2], pair[2], split_left)),
            behind(rounded(split[6], pair[6], split_right)),
            small[:2],
            hop(small[2:], 2, 0, n_dp, n_seq),
        )
        small = small + small_more
        own = rounded(whole[0], left, right)
        own, other_chip, split_left, split_right, small, small_more = tick(
            own,
            trade(own),
            ahead(rounded(split[1], pair[1], split_left)),
            behind(rounded(split[7], pair[7], split_right)),
            small[0],
            hop(small[1], 4, 0, n_dp, n_seq),
        )
        small = small + small_more
        split_own, own, other_chip, small = tick(
            rounded(split[0], pair[0], split_left, split_right), own, other_chip, small
        )
        own = rounded(own, other_chip)
        squares = jnp.sum(jnp.square(own.astype(f32))) + 0.5 * jnp.sum(small[:rows] ** 2)
        own, split_own, pair_own, other, squares = tick(own, split_own, trade(split_own), across(own), squares)
        split_own = join_halves(
            jnp.where(side == 0, split_own, pair_own), jnp.where(side == 0, pair_own, split_own)
        )
        split_other = across(split_own)
        squares = jnp.full((1, LANES), squares + jnp.sum(jnp.square(split_own.astype(f32))))
        for hops in (((0, 1), (1, 0), (1, 1)), ((2, 0), (4, 0), (6, 0))):
            squares = tree_sum([squares] + [hop(squares, *ks, n_dp, n_seq) for ks in hops])
    else:
        def by_place(groups, values):
            spread = dict(zip((r for places in groups for r in places), jnp.concatenate(values)))
            return jnp.stack([spread[r] for r in range(BLOCKS)])

        def three(whole, split):
            split = by_place(SPLIT_PLACES, split)
            return jnp.concatenate([by_place(PLACES, whole), join_halves(split[:, 0], split[:, 1])[:, None]], 1)

        vgrad = vgrad.transpose(1, 0, 2).reshape(-1, features)
        canonical = jnp.concatenate([three(keeps, split_keeps), three(sends, split_sends)], 1).transpose(1, 0, 2, 3)

        def join(row, end, blocks):
            part = canonical[:, :, row:end].astype(f32).reshape(CUTS, BLOCKS, blocks, -1, LANES)
            return part.transpose(1, 3, 0, 2, 4).reshape(-1, CUTS * blocks * LANES)

        whole = (
            jnp.stack([join(ROW_P, ROW_QKV, 1), join(ROW_O, ROW_ONE, 1), join(ROW_H, ROWS, 1)]),
            join(ROW_QKV, ROW_O, 3),
            join(ROW_ONE, ROW_TWO, 4),
            join(ROW_TWO, ROW_H, 1),
            vgrad[:rows],
        )
        grads = [
            lax.psum_scatter(grad, "dp", scatter_dimension=axis, tiled=True)
            for grad, axis in zip(whole, (1, 0, 0, 0, 1))
        ]
        grads = lax.psum(grads, "seq")
        vector_grad = grads[4]
        squares = lax.psum(sum(jnp.sum(grad * grad) for grad in grads), "dp")
        loss_sum, count = lax.psum((vgrad[rows, 0], vgrad[rows + 1, 0]), ("dp", "seq"))

    if ringed:
        shared_grads = (own, split_own, other, split_other)
        loss, norm, *new = adam_all(core.reshape(1), squares, small, shared_grads, masters, moments, variances)
    else:
        loss, norm = loss_sum / count, jnp.sqrt(squares) / count
        factor = clip_limit / jnp.maximum(norm, clip_limit) / count
        rates = ((matrix_rate, weight_decay),) * 4 + ((vector_rate, 0.0),)
        updated = [
            adam(master, moment, variance, grad * factor, *rate)
            for master, moment, variance, grad, rate in zip(masters, moments, variances, grads, rates)
        ]
        new = tuple(zip(*updated))
    return (loss, norm, *(new[k][kind] for kind in range(5) for k in range(3)))


def solution(mesh):
    matrix = P("dp", None)
    state = (P(None, "dp", None), matrix, matrix, matrix, P(None, "dp"))
    in_specs = (P("dp", "seq", None), P("dp", "seq"), P("dp", "seq", None)) + state * 3
    out_specs = (P(), P()) + tuple(spec for spec in state for _ in range(3))
    return jax.shard_map(
        partial(local, mesh.shape["dp"], mesh.shape["seq"]),
        mesh=mesh,
        in_specs=in_specs,
        out_specs=out_specs,
        check_vma=False,
    )
```
